32 devices in a mesh: dp: 16 (over z, y, x), head: 2 (over core).
Axes of the slice: x: 2, y: 2, z: 4, core: 2. Of those that a mesh axis runs over, the one named last changes fastest.
Arguments:
- patches: bfloat16 [16384, 768], P('dp'), may hold values from -6 to 6
- image_grids: int32 [96, 2], P('dp'), may hold values from 0 to 24, as said below
- out_grad: bfloat16 [16384, 768], P('dp'), may hold values from -6 to 6
- first_gain: float32 [768], replicated, may hold values from 0.5 to 1.5
- first_shift: float32 [768], replicated, may hold values from -1 to 1
- qkv_weight: bfloat16 [3, 768, 768], P(None, None, 'head'), may hold values from -0.21875 to 0.21875
- qkv_bias: float32 [3, 768], P(None, 'head'), may hold values from -1 to 1
- rope_freqs: float32 [2, 12, 32], P(None, 'head'), may hold values from -0.8 to 0.8
- proj_weight: bfloat16 [768, 768], P('head'), may hold values from -2.5 to 2.5
- proj_bias: float32 [768], replicated, may hold values from -1 to 1
- second_gain: float32 [768], replicated, may hold values from 0.5 to 1.5
- second_shift: float32 [768], replicated, may hold values from -1 to 1
- expand_weight: bfloat16 [768, 3072], P(None, 'head'), may hold values from -0.21875 to 0.21875
- expand_bias: float32 [3072], P('head'), may hold values from -1 to 1
- contract_weight: bfloat16 [3072, 768], P('head'), may hold values from -0.109375 to 0.109375
- contract_bias: float32 [768], replicated, may hold values from -1 to 1
Outputs:
- mixed_out: bfloat16 [16384, 768], P('dp')
- patches_grad: float32 [16384, 768], P('dp')
- qkv_weight_grad: float32 [3, 768, 768], P(None, 'dp', 'head')
- proj_weight_grad: float32 [768, 768], P('head', 'dp')
- expand_weight_grad: float32 [768, 3072], P('dp', 'head')
- contract_weight_grad: float32 [3072, 768], P('head', 'dp')
- first_gain_grad: float32 [768], replicated
- first_shift_grad: float32 [768], replicated
- qkv_bias_grad: float32 [3, 768], P(None, 'head')
- rope_freqs_grad: float32 [2, 12, 32], P(None, 'head')
- proj_bias_grad: float32 [768], replicated
- second_gain_grad: float32 [768], replicated
- second_shift_grad: float32 [768], replicated
- expand_bias_grad: float32 [3072], P('head')
- contract_bias_grad: float32 [768], replicated
The draws below stay inside these ranges and needn't reach their ends.
Inputs may be any that keep to these rules, and one draw needn't show every extreme that they name: `image_grids`: every image is square with side 14, 20 or 24, height equal to width. In each block of 6 rows (one index of dp) the images come first and the empty slots (0, 0) after them; the images' patches total at most 1024, and every block has an empty slot.
All inputs are finite; a program needn't handle non-finite values.
Results may differ from the reference program's by a relative error of at most 0.012.
Values sent between devices are 32-bit elements; how exact they have to be, the bound alone decides.
A program may use at most 192 MiB of HBM per device.

```python
import jax
import jax.numpy as jnp
from jax import lax

D = 768
HEADS = 12
HS = 64
FF = 3072
TOK_DEV = 1024
SIDE_SMALL = 14
SIDE_MID = 20
SIDE_BIG = 24
HQ = 768
SLOTS = 6
IMAGES = 96
TOKENS = 16384


def draw_image_grids(key, part):
    devices = IMAGES // SLOTS
    side_table = jnp.array([SIDE_SMALL, SIDE_MID, SIDE_BIG], dtype=jnp.int32)
    picked = jax.random.randint(key, (devices, SLOTS), 0, 3).astype(jnp.int32)
    picked = picked.at[0, 0].set(2)
    room_left = jnp.full((devices,), TOK_DEV, dtype=jnp.int32)
    columns = []
    for slot_num in range(SLOTS):
        wanted = side_table[picked[:, slot_num]]
        candidate = jnp.zeros((devices,), dtype=jnp.int32)
        for side_value in (SIDE_SMALL, SIDE_MID, SIDE_BIG):
            fits = (side_value <= wanted) & (side_value * side_value <= room_left)
            candidate = jnp.where(fits, side_value, candidate).astype(jnp.int32)
        room_left = (room_left - candidate * candidate).astype(jnp.int32)
        columns.append(candidate)
    chosen = jnp.stack(columns, axis=1).reshape(devices * SLOTS)
    return jnp.stack([chosen, chosen], axis=1).astype(jnp.int32)


def strengthened(result, key, source, target, blocks, factor):
    owner, partner = [(jnp.arange(result.shape[axis_at]) // (result.shape[axis_at] // blocks)).reshape([-1 if axis == axis_at else 1 for axis in range(result.ndim)]) for axis_at in (source, target)]
    chosen = jax.random.permutation(key, blocks)[partner]
    strong = (owner == chosen) | (owner == (partner + blocks // 2) % blocks)
    return jnp.where(strong, factor * result, result)


def shard_levels(stream_key, extent, split, low, top_value):
    def one(dim, blocks):
        steps = jax.random.uniform(jax.random.fold_in(jax.random.fold_in(stream_key, 6), dim), (blocks,), jnp.float32, low / len(split), top_value / len(split))
        return jnp.repeat(jnp.exp(steps), extent[dim] // blocks).reshape((-1,) + (1,) * (len(extent) - dim - 1))

    level = one(*split[0])
    for cut in split[1:]:
        level = level * one(*cut)
    return level


def noise(key, shape, deviation, reach, cuts=(), kind=jnp.bfloat16):
    factor_of = shard_levels(key, shape, cuts, -0.22, 0.18) if cuts else 1.0
    drawn = jax.random.normal(key, shape, jnp.float32) * deviation * factor_of
    return jnp.minimum(jnp.maximum(drawn, -reach), reach).astype(kind)


def noise_with(rng, shape, scale, reach, shards, heavy, held_as=jnp.bfloat16):
    result = scale * jax.random.normal(rng, shape, jnp.float32)
    if shards:
        result = result * shard_levels(rng, shape, shards, -0.22, 0.18)
    return jnp.clip(strengthened(result, jax.random.fold_in(rng, 3), *heavy), -reach, reach).astype(held_as)


def setup_inputs(seed: int = 0) -> dict:
    seeds = jax.random.split(jax.random.key(seed), 17)
    patches = noise_with(seeds[0], (TOKENS, D), 1.0, 6.0, ((0, 16),), (0, 1, 16, 2.0))
    image_grids = draw_image_grids(jax.random.fold_in(seeds[16], 71), 0)
    out_grad = noise_with(seeds[2], (TOKENS, D), 1.0, 6.0, ((0, 16),), (0, 1, 16, 2.0))
    first_gain = jnp.clip(1.0 + 0.1 * jax.random.normal(seeds[3], (D,), jnp.float32), 0.5, 1.5)
    first_shift = noise(seeds[4], (D,), 0.2, 1.0, (), jnp.float32)
    qkv_weight = noise(seeds[5], (3, D, HQ), D ** -0.5, 0.21875, ((2, 2),))
    qkv_bias = noise(seeds[6], (3, HQ), 0.2, 1.0, ((1, 2),), jnp.float32)
    rope_freqs = jnp.clip(jax.random.uniform(seeds[7], (2, HEADS, HS // 2), jnp.float32, -0.8, 0.8) * shard_levels(seeds[7], (2, HEADS, HS // 2), ((1, 2),), -0.4, 0.0), -0.8, 0.8)
    proj_weight = noise(seeds[8], (HQ, D), (max(1, HQ * 8 // TOK_DEV)) ** -0.5, 2.5, ((0, 2),))
    proj_bias = noise(seeds[9], (D,), 0.2, 1.0, (), jnp.float32)
    second_gain = jnp.clip(1.0 + 0.1 * jax.random.normal(seeds[10], (D,), jnp.float32), 0.5, 1.5)
    second_shift = noise(seeds[11], (D,), 0.2, 1.0, (), jnp.float32)
    expand_weight = noise(seeds[12], (D, FF), D ** -0.5, 0.21875, ((1, 2),))
    expand_bias = noise(seeds[13], (FF,), 0.2, 1.0, ((0, 2),), jnp.float32)
    contract_weight = noise(seeds[14], (FF, D), FF ** -0.5, 0.109375, ((0, 2),))
    contract_bias = noise(seeds[15], (D,), 0.2, 1.0, (), jnp.float32)
    return {"patches": patches, "image_grids": image_grids, "out_grad": out_grad, "first_gain": first_gain, "first_shift": first_shift, "qkv_weight": qkv_weight, "qkv_bias": qkv_bias, "rope_freqs": rope_freqs, "proj_weight": proj_weight, "proj_bias": proj_bias, "second_gain": second_gain, "second_shift": second_shift, "expand_weight": expand_weight, "expand_bias": expand_bias, "contract_weight": contract_weight, "contract_bias": contract_bias}


@jax.custom_vjp
def low(v):
    return lax.optimization_barrier(v.astype(jnp.bfloat16)).astype(jnp.float32)

@jax.custom_vjp
def low_back(v):
    return v

def low_keep(v):
    return (low(v), None)

def low_pass(kept, grad):
    return (grad,)

def back_keep(v):
    return (v, None)

def back_low(kept, grad):
    return (low(grad),)
low.defvjp(low_keep, low_pass)
low_back.defvjp(back_keep, back_low)
eps = 1e-06
masked_score = -1e+30

def positions(image_grids, row_count):
    slot_count = image_grids.shape[0]
    image_len = (image_grids[:, 0] * image_grids[:, 1]).astype(jnp.int32)
    image_end = jnp.cumsum(image_len).astype(jnp.int32)
    image_start = (image_end - image_len).astype(jnp.int32)
    token_pos = jnp.arange(row_count, dtype=jnp.int32)
    segment = lax.optimization_barrier(jnp.sum((token_pos[:, None] >= image_end[None, :]).astype(jnp.int32), axis=1)).astype(jnp.int32)
    member = segment[:, None] == jnp.arange(slot_count, dtype=jnp.int32)[None, :]
    start_tok = lax.optimization_barrier(jnp.sum(jnp.where(member, image_start[None, :], 0), axis=1)).astype(jnp.int32)
    width_tok = lax.optimization_barrier(jnp.sum(jnp.where(member, image_grids[None, :, 1], 0), axis=1)).astype(jnp.int32)
    offset = (token_pos - start_tok).astype(jnp.int32)
    safe_width = jnp.maximum(width_tok, 1).astype(jnp.int32)
    real_row = segment < slot_count
    grid_row = jnp.where(real_row, offset // safe_width, 0).astype(jnp.float32)
    grid_col = jnp.where(real_row, offset % safe_width, 0).astype(jnp.float32)
    return (segment, grid_row, grid_col, real_row.astype(jnp.float32))

def layer_norm(source, gain, shift):
    mean_val = lax.optimization_barrier(jnp.mean(source, axis=-1, keepdims=True))
    centred = source - mean_val
    inv_dev = lax.rsqrt(lax.optimization_barrier(jnp.mean(centred * centred, axis=-1, keepdims=True)) + eps)
    return centred * inv_dev * gain + shift

def rotate_pairs(source, cosine, sine_val):
    row_count = source.shape[0]
    head_count = cosine.shape[1]
    half_size = cosine.shape[2]
    shaped = source.reshape(row_count, head_count, 2, half_size)
    first_half = shaped[:, :, 0]
    second_half = shaped[:, :, 1]
    turned = jnp.stack([first_half * cosine - second_half * sine_val, first_half * sine_val + second_half * cosine], axis=2)
    return turned.reshape(row_count, head_count * 2 * half_size)

def attend(query_low, key_low, value_low, segment):
    row_count = query_low.shape[0]
    block = min(512, row_count)
    count = row_count // block
    score_scale = HS ** (-0.5)
    key_heads = key_low.reshape(row_count, HEADS, HS)
    value_heads = value_low.reshape(row_count, HEADS, HS)
    query_blocks = query_low.reshape(count, block, HEADS, HS)
    segment_blocks = segment.reshape(count, block)

    def one_block(block_item):
        query_block, segment_query = block_item
        scores = jnp.einsum('qhd,khd->hqk', query_block, key_heads, precision=lax.Precision.HIGHEST) * score_scale
        scores = low_back(scores)
        same_image = (segment_query[:, None] == segment[None, :])[None]
        scores = jnp.where(same_image, scores, masked_score)
        probabilities = low(jax.nn.softmax(scores, axis=-1))
        return jnp.einsum('hqk,khd->qhd', probabilities, value_heads, precision=lax.Precision.HIGHEST)
    block_out = lax.map(jax.checkpoint(one_block), (query_blocks, segment_blocks))
    return block_out.reshape(row_count, HEADS * HS)

def forward(source, params, segment, grid_row, grid_col):
    gain_one, shift_one, weight_qkv, bias_qkv, rope_table, weight_proj, bias_proj, gain_two, shift_two, weight_expand, bias_expand, weight_contract, bias_contract = params
    normed_first = low(layer_norm(source, gain_one, shift_one))
    projected = jnp.einsum('td,kdh->kth', normed_first, weight_qkv, precision=lax.Precision.HIGHEST) + bias_qkv[:, None, :]
    projected = low_back(projected)
    turn_angle = grid_row[:, None, None] * rope_table[0][None] + grid_col[:, None, None] * rope_table[1][None]
    cosine = jnp.cos(turn_angle)
    sine_val = jnp.sin(turn_angle)
    query_low = low(rotate_pairs(projected[0], cosine, sine_val))
    key_low = low(rotate_pairs(projected[1], cosine, sine_val))
    value_low = low(projected[2])
    attended = low(low_back(attend(query_low, key_low, value_low, segment)))
    branch = low_back(jnp.dot(attended, weight_proj, precision=lax.Precision.HIGHEST) + bias_proj)
    middle = source + branch
    normed_second = low(layer_norm(middle, gain_two, shift_two))
    hidden = low_back(jnp.dot(normed_second, weight_expand, precision=lax.Precision.HIGHEST) + bias_expand)
    active = low(jax.nn.gelu(hidden, approximate=False))
    branch_two = low_back(jnp.dot(active, weight_contract, precision=lax.Precision.HIGHEST) + bias_contract)
    return middle + branch_two

def add_up(first_term, second_term):
    return first_term + second_term

def reference(patches, image_grids, out_grad, first_gain, first_shift, qkv_weight, qkv_bias, rope_freqs, proj_weight, proj_bias, second_gain, second_shift, expand_weight, expand_bias, contract_weight, contract_bias):
    params = (first_gain.astype(jnp.float32), first_shift.astype(jnp.float32), qkv_weight.astype(jnp.float32), qkv_bias.astype(jnp.float32), rope_freqs.astype(jnp.float32), proj_weight.astype(jnp.float32), proj_bias.astype(jnp.float32), second_gain.astype(jnp.float32), second_shift.astype(jnp.float32), expand_weight.astype(jnp.float32), expand_bias.astype(jnp.float32), contract_weight.astype(jnp.float32), contract_bias.astype(jnp.float32))
    row_count = TOK_DEV
    blocks = patches.shape[0] // row_count
    patch_blocks = patches.astype(jnp.float32).reshape(blocks, row_count, D)
    grad_blocks = out_grad.astype(jnp.float32).reshape(blocks, row_count, D)
    grid_blocks = image_grids.reshape(blocks, SLOTS, 2)

    def one_device(totals, entries):
        patch_block, grad_block, grid_block = entries
        segment, grid_row, grid_col, real_row = positions(grid_block, row_count)

        def local_pass(source, weights):
            return forward(source, weights, segment, grid_row, grid_col)
        outcome, pullback = jax.vjp(local_pass, patch_block, params)
        source_grad, weight_grads = pullback(grad_block * real_row[:, None])
        return (jax.tree.map(add_up, totals, weight_grads), (outcome.astype(jnp.bfloat16), source_grad))
    start_sums = jax.tree.map(jnp.zeros_like, params)
    totals, (outcomes, source_grads) = lax.scan(one_device, start_sums, (patch_blocks, grad_blocks, grid_blocks))
    first_gain_grad, first_shift_grad, qkv_weight_grad, qkv_bias_grad, rope_freqs_grad, proj_weight_grad, proj_bias_grad, second_gain_grad, second_shift_grad, expand_weight_grad, expand_bias_grad, contract_weight_grad, contract_bias_grad = totals
    return (outcomes.reshape(blocks * row_count, D), source_grads.reshape(blocks * row_count, D), qkv_weight_grad, proj_weight_grad, expand_weight_grad, contract_weight_grad, first_gain_grad, first_shift_grad, qkv_bias_grad, rope_freqs_grad, proj_bias_grad, second_gain_grad, second_shift_grad, expand_bias_grad, contract_bias_grad)
```

```python
from functools import partial

import jax
import jax.numpy as jnp
from jax import lax
from jax.experimental import pallas as pl
from jax.experimental.pallas import tpu as pltpu
from jax.sharding import PartitionSpec as P

F32 = jnp.float32
BF16 = jnp.bfloat16
EPS = 1e-06
FAR = 2.0**100
R = 256
SUB = 64
PAIR = 128
HALF = 64
CHUNK = 256
MESH = pl.DeviceIdType.MESH
ANY = pl.ANY


def dot_nn(a, b):
    return lax.dot_general(a, b, (((1,), (0,)), ((), ())), preferred_element_type=F32)


def dot_nt(a, b):
    return lax.dot_general(a, b, (((1,), (1,)), ((), ())), preferred_element_type=F32)


def aligned(i, size):
    return pl.ds(pl.multiple_of(i * size, size), size)


def loop(count, fn):
    def step(i, carry):
        fn(i)
        return carry

    lax.fori_loop(0, count, step, 0)


def unit_of(rows):
    centred = rows - jnp.mean(rows, axis=-1, keepdims=True)
    inv = lax.rsqrt(jnp.mean(centred * centred, axis=-1, keepdims=True) + EPS)
    return centred * inv, inv


def norm_back(upstream, unit, inv, gain):
    scaled = upstream * gain
    return inv * (
        scaled
        - jnp.mean(scaled, axis=-1, keepdims=True)
        - unit * jnp.mean(scaled * unit, axis=-1, keepdims=True)
    )


def swap_halves(v, lane_first):
    return jnp.where(lane_first, pltpu.roll(v, PAIR - HALF // 2, 1), pltpu.roll(v, HALF // 2, 1))


def lane_ids(rows):
    return lax.broadcasted_iota(jnp.int32, (rows, PAIR), 1)


def head_mask(h):
    lane = lax.broadcasted_iota(jnp.int32, (1, PAIR), 1)
    return (lane // HALF == h).astype(F32)


def front_kernel(
    grids, x, gain, shift, w, b, freqs,
    q8, key, val, nf, att, lse, ohq, ohk, cos, sin, pos,
    kx, lcol,
):
    rows_all = x.shape[0]
    slots = grids.shape[0]
    pairs = q8.shape[1] // PAIR
    side = lax.broadcasted_iota(jnp.int32, (32, 1), 0).astype(F32)
    ang_r = side * freqs[0:1, :]
    ang_c = side * freqs[1:2, :]
    table_r = jnp.concatenate([jnp.cos(ang_r), jnp.sin(ang_r)], axis=1)
    table_c = jnp.concatenate([jnp.cos(ang_c), jnp.sin(ang_c)], axis=1)
    width_all = q8.shape[1]

    def first(r):
        rows = aligned(r, R)
        t = lax.broadcasted_iota(jnp.int32, (R, 1), 0) + r * R
        seg = jnp.zeros((R, 1), jnp.int32)
        start = jnp.zeros((R, 1), jnp.int32)
        width = jnp.ones((R, 1), jnp.int32)
        end = jnp.int32(0)
        for s in range(slots):
            begin = end
            end = end + grids[s, 0] * grids[s, 1]
            inside = (t >= begin) & (t < end)
            start = jnp.where(inside, begin, start)
            width = jnp.where(inside, grids[s, 1], width)
            seg = seg + (t >= end).astype(jnp.int32)
        real = (seg < slots).astype(F32)
        off = (t - start).astype(F32)
        wide = width.astype(F32)
        grow = jnp.floor((off + 0.5) / wide) * real
        gcol = (off - grow * wide) * real
        lane = lane_ids(R)
        pos[rows, :] = (
            jnp.where(lane == 0, real, 0.0)
            + jnp.where(lane == 1, grow, 0.0)
            + jnp.where(lane == 2, gcol, 0.0)
        )
        hot = (lane % HALF == seg).astype(F32)
        ohq[rows, :] = hot.astype(BF16)
        ohk[rows, :] = ((1.0 - hot) * (-FAR)).astype(BF16)
        spot = lax.broadcasted_iota(jnp.int32, (R, 32), 1)
        hot_r = (spot == grow.astype(jnp.int32)).astype(F32)
        hot_c = (spot == gcol.astype(jnp.int32)).astype(F32)
        got_r = jnp.dot(hot_r, table_r, precision=lax.Precision.HIGHEST, preferred_element_type=F32)
        got_c = jnp.dot(hot_c, table_c, precision=lax.Precision.HIGHEST, preferred_element_type=F32)
        cr, sr = got_r[:, :width_all], got_r[:, width_all:]
        cc, sc = got_c[:, :width_all], got_c[:, width_all:]
        cos[rows, :] = cr * cc - sr * sc
        sin[rows, :] = sr * cc + cr * sc
        unit, _ = unit_of(x[rows, :].astype(F32))
        normed = (unit * gain[...] + shift[...]).astype(BF16)
        nf[rows, :] = normed
        lane_first = lane % HALF < HALF // 2
        sign = jnp.where(lane_first, -1.0, 1.0)
        for k, out in ((0, q8), (1, key)):
            got = dot_nn(normed, w[k]) + b[k : k + 1, :]
            for p in range(pairs):
                cols = slice(p * PAIR, (p + 1) * PAIR)
                part = got[:, cols]
                turned = part * cos[rows, cols] + swap_halves(part, lane_first) * (
                    sin[rows, cols] * sign
                )
                turned = turned.astype(BF16)
                if k == 0:
                    turned = turned * jnp.asarray(HALF**-0.5, BF16)
                out[rows, cols] = turned
        val[rows, :] = (dot_nn(normed, w[2]) + b[2:3, :]).astype(BF16)

    loop(rows_all // R, first)

    def heads(p):
        cols = aligned(p, PAIR)
        for h in range(2):
            mine = head_mask(h).astype(BF16)
            other = head_mask(1 - h).astype(BF16)
            kx[...] = key[:, cols] * mine + ohk[...] * other

            def queries(r, h=h, mine=mine, other=other):
                rows = aligned(r, R)
                qx = q8[rows, cols] * mine + ohq[rows, :] * other
                score = dot_nt(qx, kx[...])
                top = jnp.max(score, axis=-1, keepdims=True)
                grown = jnp.exp(score - top)
                total = jnp.sum(grown, axis=-1, keepdims=True)
                got = dot_nn(grown.astype(BF16), val[:, cols]) * (1.0 / total)
                lane = lane_ids(R)
                log_sum = top + jnp.log(total)
                if h == 0:
                    att[rows, cols] = got
                else:
                    att[rows, cols] = jnp.where(lane < HALF, att[rows, cols], got)
                lcol[rows, :] = jnp.where(lane == p * 2 + h, log_sum, lcol[rows, :])

            loop(rows_all // R, queries)

    loop(pairs, heads)

    def turn(r):
        rows = aligned(r, PAIR)
        lse[:, rows] = jnp.transpose(lcol[rows, :])[: lse.shape[0], :]

    loop(rows_all // PAIR, turn)


def front(grids, x, gain, shift, w, b, freqs):
    rows, width = x.shape
    cols = w.shape[2]
    shape = jax.ShapeDtypeStruct
    vm = pl.BlockSpec(memory_space=pltpu.VMEM)
    outs = [
        shape((rows, cols), BF16), shape((rows, cols), BF16), shape((rows, cols), BF16),
        shape((rows, width), BF16), shape((rows, cols), F32), shape((8, rows), F32),
        shape((rows, PAIR), BF16), shape((rows, PAIR), BF16),
        shape((rows, cols), F32), shape((rows, cols), F32), shape((rows, PAIR), F32),
    ]
    return pl.pallas_call(
        front_kernel,
        name="front",
        out_shape=outs,
        in_specs=[pl.BlockSpec(memory_space=pltpu.SMEM)] + [vm] * 6,
        out_specs=[vm] * len(outs),
        scratch_shapes=[pltpu.VMEM((rows, PAIR), BF16), pltpu.VMEM((rows, PAIR), F32)],
        compiler_params=pltpu.CompilerParams(vmem_limit_bytes=48 << 20),
    )(grids, x, gain, shift, w, b, freqs)


PARTS = 16


def main_kernel(
    fuse, pairs, chunks,
    att_h, q8_h, key_h, val_h, nf_h, ohq_h, ohk_h, cos_h, sin_h, lse_h, pos_h,
    x_h, og_h, wp_h, we_h, wc_h, wq_h,
    bias_p, gain_two, shift_two, bias_e, bias_c, gain_one,
    mixed_h, pgrad_h, ff_h, pq_h, small_h,
    att, q8, key, val, ohq, ohk, lse, pos, x, cot, wp, we, wc,
    acc_a, acc_b, xbuf, mid, cott, ns, nst, act, hgb, dgrad, delta,
    km, vm, kt, kmt, dk, dv, dqt, qkvg, cos, sin, sums,
    gf, gq, r1, r2, r3, small, small_r,
    lsem, xs, xr, credit, s1, e1, s2, e2, s3, e3, c1, c2, c3, ms, mr, osem,
):
    me = lax.axis_index("dp")
    core = lax.axis_index("head")
    blocks = x.shape[0] // R
    subs = x.shape[0] // SUB
    mate = (me, 1 - core)
    if fuse:
        xx, yy, zz = me % 2, (me // 2) % 2, me // 4
        fst = xx * (1 - core) + yy * core
        snd = yy * (1 - core) + xx * core
        peer1 = (me + (1 - 2 * fst) * (1 + core), core)
        peer2 = (me + (1 - 2 * snd) * (2 - core), core)
        peers_z = [(((zz + j) % 4) * 4 + me % 4, core) for j in (1, 2, 3)]

        def where(z, f, s):
            return z * 4 + s * (2 - core) + f * (1 + core)

    def load(src, dst, i):
        copy = pltpu.make_async_copy(src, dst, lsem.at[i])
        copy.start()
        return copy

    get_att = load(att_h, att, 0)
    get_wp = load(wp_h, wp, 1)
    get_og = load(og_h, cot, 2)
    get_pos = load(pos_h, pos, 3)
    get_x = load(x_h, x, 4)
    get_we = load(we_h, we, 5)
    get_wc = load(wc_h, wc, 6)
    get_late = [
        load(q8_h, q8, 7), load(key_h, key, 8), load(val_h, val, 9),
        load(ohq_h, ohq, 10), load(ohk_h, ohk, 11), load(lse_h, lse, 12),
    ]

    barrier = pltpu.get_barrier_semaphore()
    friends = [mate] + ([peer1, peer2] + peers_z if fuse else [])
    for friend in friends:
        pl.semaphore_signal(barrier, inc=1, device_id=friend, device_id_type=MESH)
    pl.semaphore_wait(barrier, len(friends))

    def exchange(src, r):
        return pltpu.make_async_remote_copy(
            src.at[aligned(r, R), :], xbuf.at[aligned(r, R), :], xs.at[r], xr.at[r],
            device_id=mate, device_id_type=MESH,
        )

    def send(src, r):
        exchange(src, r).start()

    def give_credit(r):
        pl.semaphore_signal(credit.at[r], inc=1, device_id=mate, device_id_type=MESH)

    def take_credit(r):
        pl.semaphore_wait(credit.at[r], 1)

    def remote(src, dst, ss, rs, peer):
        return pltpu.make_async_remote_copy(
            src, dst, ss, rs, device_id=peer, device_id_type=MESH
        )

    class Line:
        def __init__(self, grads, base, width, out, guard):
            self.g, self.base, self.n, self.out, self.guard = grads, base, width, out, guard

        def buf(self, buf, j, b):
            return buf.at[j, b, :, pl.ds(0, self.n)]

        def whole(self, buf, j):
            return buf.at[j, :, :, pl.ds(0, self.n)]

        def start1(self, j):
            if self.guard == "take":
                pl.semaphore_wait(c1.at[j], 1)

            def one(i):
                remote(
                    self.g.at[j, where(i // 2, 1 - fst, i % 2)], self.buf(r1, j, i),
                    s1.at[self.base + j], e1.at[self.base + j], peer1,
                ).start()

            loop(8, one)

        def give(self, sem, j, peers):
            if self.guard == "give":
                def go():
                    for peer in peers:
                        pl.semaphore_signal(sem.at[j], inc=1, device_id=peer, device_id_type=MESH)
                if isinstance(j, int):
                    if j < 4:
                        go()
                else:
                    pl.when(j < 4)(go)

        def finish1(self, j):
            remote(
                self.g.at[j, pl.ds(0, 8)], self.whole(r1, j),
                s1.at[self.base + j], e1.at[self.base + j], peer1,
            ).wait_recv()

            def one(i):
                b = where(i // 2, fst, i % 2)
                self.g[j, b] = self.g[j, b] + self.buf(r1, j, i)[...]

            loop(8, one)
            self.give(c1, j, [peer1])
            if self.guard == "take":
                pl.semaphore_wait(c2.at[j], 1)

            def two(i):
                remote(
                    self.g.at[j, where(i, fst, 1 - snd)], self.buf(r2, j, i),
                    s2.at[self.base + j], e2.at[self.base + j], peer2,
                ).start()

            loop(4, two)

        def finish2(self, j):
            remote(
                self.g.at[j, pl.ds(0, 4)], self.whole(r2, j),
                s2.at[self.base + j], e2.at[self.base + j], peer2,
            ).wait_recv()

            def one(i):
                b = where(i, fst, snd)
                self.g[j, b] = self.g[j, b] + self.buf(r2, j, i)[...]

            loop(4, one)
            self.give(c2, j, [peer2])
            if self.guard == "take":
                pl.semaphore_wait(c3.at[j], 3)
            for k in range(3):
                remote(
                    self.g.at[j, where((zz + k + 1) % 4, fst, snd)], self.buf(r3, j, k),
                    s3.at[self.base + j], e3.at[self.base + j], peers_z[k],
                ).start()

        def finish3(self, j):
            remote(
                self.g.at[j, pl.ds(0, 3)], self.whole(r3, j),
                s3.at[self.base + j], e3.at[self.base + j], peers_z[0],
            ).wait_recv()
            self.g[j, me] = (
                self.g[j, me]
                + self.buf(r3, j, 0)[...] + self.buf(r3, j, 1)[...] + self.buf(r3, j, 2)[...]
            )
            self.give(c3, j, peers_z)
            pltpu.make_async_copy(self.g.at[j, me], self.out.at[j], osem.at[self.base + j]).start()

        def drain(self, j):
            for src, dst, ss, rs, peer in (
                (self.g.at[j, pl.ds(0, 8)], self.whole(r1, j), s1, e1, peer1),
                (self.g.at[j, pl.ds(0, 4)], self.whole(r2, j), s2, e2, peer2),
                (self.g.at[j, pl.ds(0, 3)], self.whole(r3, j), s3, e3, peers_z[0]),
            ):
                remote(src, dst, ss.at[self.base + j], rs.at[self.base + j], peer).wait_send()
            pltpu.make_async_copy(self.g.at[j, me], self.out.at[j], osem.at[self.base + j]).wait()

    class Plain:
        def __init__(self, grads, base, width, out, guard):
            self.g, self.base, self.out = grads, base, out

        def copy(self, j):
            return pltpu.make_async_copy(self.g.at[j], self.out.at[j], osem.at[self.base + j])

        def start1(self, j):
            self.copy(j).start()

        def finish1(self, j):
            pass

        finish2 = finish3 = finish1

        def drain(self, j):
            self.copy(j).wait()

    kind = Line if fuse else Plain
    ff = kind(gf, 0, 2 * CHUNK, ff_h, "give")
    pq = kind(gq, chunks, 3 * PAIR, pq_h, "take")

    small[...] = jnp.zeros_like(small)
    sums[...] = jnp.zeros_like(sums)

    get_att.wait()
    get_wp.wait()

    def project(r):
        acc_a[aligned(r, R), :] = dot_nn(att[aligned(r, R), :].astype(BF16), wp[...])
        send(acc_a, r)

    loop(blocks, project)

    get_og.wait()
    get_pos.wait()

    def mask_cot(r):
        rows = aligned(r, R)
        block = (cot[rows, :].astype(F32) * pos[rows, 0:1])
        small[0, 0:1, :] = small[0, 0:1, :] + jnp.sum(block, axis=0, keepdims=True)
        low = block.astype(BF16)
        cot[rows, :] = low
        cott[:, rows] = jnp.transpose(low)

    loop(blocks, mask_cot)
    get_x.wait()

    def second_norm(r):
        exchange(acc_a, r).wait()

        def sub(i):
            rows = pl.ds(pl.multiple_of(r * R + i * SUB, SUB), SUB)
            middle = x[rows, :].astype(F32) + ((acc_a[rows, :] + xbuf[rows, :]) + bias_p[...])
            unit, _ = unit_of(middle)
            mid[rows, :] = middle
            ns[rows, :] = (unit * gain_two[...] + shift_two[...]).astype(BF16)
            acc_b[rows, :] = 0.5 * (middle + bias_c[...])
            acc_a[rows, :] = jnp.zeros_like(middle)

        loop(R // SUB, sub)
        give_credit(r)
        nst[:, aligned(r, R)] = jnp.transpose(ns[aligned(r, R), :])

    loop(blocks, second_norm)
    get_we.wait()
    get_wc.wait()

    def feed(j):
        cols = aligned(j, CHUNK)

        def rows_of(r):
            rows = aligned(r, R)
            hidden = dot_nn(ns[rows, :], we[:, cols]) + bias_e[:, cols]
            upstream = dot_nt(cot[rows, :], wc[cols, :])
            phi = 0.5 * (1.0 + lax.erf(hidden * (0.5**0.5)))
            slope = phi + hidden * (jnp.exp(-0.5 * hidden * hidden) * (0.3989422804014327))
            active = (hidden * phi).astype(BF16)
            hgrad = (upstream * slope).astype(BF16)
            act[rows, :] = active
            hgb[rows, :] = hgrad
            sums[0:1, cols] = sums[0:1, cols] + jnp.sum(hgrad.astype(F32), axis=0, keepdims=True)
            acc_b[rows, :] = acc_b[rows, :] + dot_nn(active, wc[cols, :])
            acc_a[rows, :] = acc_a[rows, :] + dot_nt(hgrad, we[:, cols])

        loop(blocks, rows_of)
        got = dot_nn(cott[...], act[...])
        gf[j, :, :, pl.ds(0, CHUNK)] = got.reshape(gf.shape[1], gf.shape[2], CHUNK)
        got = dot_nn(nst[...], hgb[...])
        gf[j, :, :, pl.ds(CHUNK, CHUNK)] = got.reshape(gf.shape[1], gf.shape[2], CHUNK)
        ff.start1(j)

    loop(chunks, feed)

    def send_second(r):
        take_credit(r)
        send(acc_a, r)

    loop(blocks, send_second)
    get_nf = load(nf_h, ns, 0)
    ff.finish1(0)
    ff.finish1(1)

    def second_back(r):
        exchange(acc_a, r).wait()

        def sub(i):
            rows = pl.ds(pl.multiple_of(r * R + i * SUB, SUB), SUB)
            up = acc_a[rows, :] + xbuf[rows, :]
            unit, inv = unit_of(mid[rows, :])
            small[0, 1:2, :] = small[0, 1:2, :] + jnp.sum(up * unit, axis=0, keepdims=True)
            small[0, 2:3, :] = small[0, 2:3, :] + jnp.sum(up, axis=0, keepdims=True)
            grad = cot[rows, :].astype(F32) + norm_back(up, unit, inv, gain_two[...])
            mid[rows, :] = grad
            low = grad.astype(BF16)
            cot[rows, :] = low
            small[0, 3:4, :] = small[0, 3:4, :] + jnp.sum(
                low.astype(F32), axis=0, keepdims=True
            )
            acc_a[rows, :] = jnp.zeros_like(up)

        loop(R // SUB, sub)
        give_credit(r)
        rows = aligned(r, R)
        cott[:, rows] = jnp.transpose(cot[rows, :])
        low = dot_nt(cot[rows, :], wp[...]).astype(BF16)
        dgrad[rows, :] = low
        prod = low.astype(F32) * att[rows, :]
        head = lax.broadcasted_iota(jnp.int32, (8, prod.shape[1]), 0)
        lane = lax.broadcasted_iota(jnp.int32, (8, prod.shape[1]), 1)
        pick = (lane // HALF == head).astype(F32)
        delta[:, rows] = lax.dot_general(
            pick, prod, (((1,), (1,)), ((), ())), precision=lax.Precision.HIGHEST,
            preferred_element_type=F32,
        )

    loop(blocks, second_back)
    gq[0] = dot_nn(cott[...], att[...].astype(BF16)).reshape(gq.shape[1:])
    pq.start1(0)

    def send_mixed(r):
        take_credit(r)
        send(acc_b, r)

    loop(blocks, send_mixed)

    get_nf.wait()

    def turn_first(r):
        nst[:, aligned(r, R)] = jnp.transpose(ns[aligned(r, R), :])

    loop(blocks, turn_first)
    get_wq = [
        load(wq_h.at[k], we.at[:, pl.ds(k * pairs * PAIR, pairs * PAIR)], 4 + k) for k in range(3)
    ]
    for copy in get_late:
        copy.wait()
    kt[...] = jnp.transpose(key[...])

    def mixed_block(r):
        exchange(acc_b, r).wait()
        rows = aligned(r, R)
        ns[rows, :] = (acc_b[rows, :] + xbuf[rows, :]).astype(BF16)
        give_credit(r)
        pltpu.make_async_copy(ns.at[rows, :], mixed_h.at[rows, :], ms.at[r]).start()

    loop(blocks, mixed_block)
    for copy in get_wq:
        copy.wait()

    def pair_back(p):
        cols = aligned(p, PAIR)
        get_cos = load(cos_h.at[:, cols], cos, 0)
        get_sin = load(sin_h.at[:, cols], sin, 1)
        dk[...] = jnp.zeros_like(dk)
        dv[...] = jnp.zeros_like(dv)
        dqt[...] = jnp.zeros_like(dqt)

        def head_back(h):
            mine = head_mask(h).astype(BF16)
            other = head_mask(1 - h).astype(BF16)
            km[...] = key[:, cols] * mine + ohk[...] * other
            vm[...] = val[:, cols] * mine
            spot = lax.broadcasted_iota(jnp.int32, (PAIR, 1), 0)
            kmt[...] = kt[cols, :] * (spot // HALF == h).astype(F32).astype(BF16)
            n = p * 2 + h

            def query_back(r):
                rows = aligned(r, R)
                qm = q8[rows, cols] * mine
                qx = qm + ohq[rows, :] * other
                do = dgrad[rows, cols]
                score = dot_nt(km[...], qx)
                prob = jnp.exp(score - lse[pl.ds(n, 1), rows])
                pgrad = dot_nt(vm[...], do)
                sgrad = (prob * (pgrad - delta[pl.ds(n, 1), rows])).astype(BF16)
                dv[...] = dv[...] + dot_nn(prob.astype(BF16), do * mine)
                dk[...] = dk[...] + dot_nn(sgrad, qm)
                dqt[:, rows] = dqt[:, rows] + dot_nn(kmt[...], sgrad)

            loop(blocks, query_back)
            if fuse:
                pl.when(n < 4)(lambda: ff.finish1(n + 2))
                ff.finish2(n)

        loop(2, head_back)
        get_cos.wait()
        get_sin.wait()

        def turn_back(r):
            rows = aligned(r, R)
            lane_first = lane_ids(R) % HALF < HALF // 2
            sign = jnp.where(lane_first, 1.0, -1.0)
            c, s = cos[rows, :], sin[rows, :]
            total = jnp.zeros((R, PAIR), F32)
            grads = []
            scale = HALF**-0.5
            for k, (grad, turned) in enumerate(
                (
                    (jnp.transpose(dqt[:, rows]) * scale, q8[rows, cols].astype(F32) * (1.0 / scale)),
                    (dk[rows, :], key[rows, cols].astype(F32)),
                )
            ):
                swapped = swap_halves(grad, lane_first) * sign
                total = total + swapped * turned
                grads.append((grad * c + swapped * s).astype(BF16))
            grads.append(dv[rows, :].astype(BF16))
            for k, low in enumerate(grads):
                qkvg[rows, k * PAIR : (k + 1) * PAIR] = low
                sums[k + 1 : k + 2, cols] = sums[k + 1 : k + 2, cols] + jnp.sum(
                    low.astype(F32), axis=0, keepdims=True
                )
            for k in range(2):
                sums[k + 4 : k + 5, cols] = sums[k + 4 : k + 5, cols] + jnp.sum(
                    total * pos[rows, k + 1 : k + 2], axis=0, keepdims=True
                )
            weight = jnp.concatenate(
                [we[:, aligned(k * pairs + p, PAIR)] for k in range(3)], axis=1
            )
            acc_a[rows, :] = acc_a[rows, :] + dot_nt(qkvg[rows, :], weight)

        loop(blocks, turn_back)
        gq[p + 1] = dot_nn(nst[...], qkvg[...]).reshape(gq.shape[1:])
        pq.start1(p + 1)
        if fuse:
            pl.when(p == 0)(lambda: pq.finish1(0))
            pl.when(p == 1)(lambda: pq.finish1(1))
            ff.finish3(p * 2)
            ff.finish3(p * 2 + 1)

    loop(pairs, pair_back)

    def first_send(r):
        def sub(i):
            rows = pl.ds(pl.multiple_of(r * R + i * SUB, SUB), SUB)
            unit, _ = unit_of(x[rows, :].astype(F32))
            up = acc_a[rows, :]
            small[0, 6:7, :] = small[0, 6:7, :] + jnp.sum(up * unit, axis=0, keepdims=True)
            small[0, 7:8, :] = small[0, 7:8, :] + jnp.sum(up, axis=0, keepdims=True)

        take_credit(r)
        send(acc_a, r)
        loop(R // SUB, sub)

    loop(blocks, first_send)

    n = chunks * CHUNK // 2
    small[0, 4:5, :] = sums[0:1, 0:n]
    small[0, 5:6, :] = sums[0:1, n : 2 * n]
    m = pairs * PAIR
    for k in range(5):
        small[0, 8 + k : 9 + k, 0:m] = sums[1 + k : 2 + k, 0:m]

    def small_copy(i, k, peer):
        return remote(small.at[k], small_r.at[i], ms.at[4 + i], mr.at[i], peer)

    copy = small_copy(0, 0, mate)
    copy.start()
    if fuse:
        pq.finish2(0)
    copy.wait()
    line = lax.broadcasted_iota(jnp.int32, small.shape[1:], 0)
    small[1] = small[0] + jnp.where((line == 6) | (line == 7), small_r[0], 0.0)
    if fuse:
        copy = small_copy(1, 1, peer1)
        copy.start()
        pq.finish1(2)
        copy.wait()
        small[2] = small[1] + small_r[1]
        copy = small_copy(2, 2, peer2)
        copy.start()
        pq.finish2(1)
        copy.wait()
        small[3] = small[2] + small_r[2]
        copies = [small_copy(3 + k, 3, peers_z[k]) for k in range(3)]
        for copy in copies:
            copy.start()
    last = 4 if fuse else 1

    def first_back(r):
        exchange(acc_a, r).wait()

        def sub(i):
            rows = pl.ds(pl.multiple_of(r * R + i * SUB, SUB), SUB)
            unit, inv = unit_of(x[rows, :].astype(F32))
            up = acc_a[rows, :] + xbuf[rows, :]
            mid[rows, :] = mid[rows, :] + norm_back(up, unit, inv, gain_one[...])

        loop(R // SUB, sub)
        rows = aligned(r, R)
        pltpu.make_async_copy(mid.at[rows, :], pgrad_h.at[rows, :], xs.at[r]).start()

    loop(blocks, first_back)
    if fuse:
        for copy in copies:
            copy.wait()
        small[4] = small[3] + (small_r[3] + small_r[4] + small_r[5])
    out_small = pltpu.make_async_copy(small.at[last], small_h, lsem.at[0])
    out_small.start()
    if fuse:
        pq.finish3(0)
        pq.finish1(3)
        pq.finish2(2)
        pq.finish3(1)
        pq.finish2(3)
        pq.finish3(2)
        pq.finish3(3)
    loop(chunks, ff.drain)
    loop(pairs + 1, pq.drain)
    out_small.wait()

    def finish_out(r):
        rows = aligned(r, R)
        pltpu.make_async_copy(ns.at[rows, :], mixed_h.at[rows, :], ms.at[r]).wait()
        pltpu.make_async_copy(mid.at[rows, :], pgrad_h.at[rows, :], xs.at[r]).wait()

    loop(blocks, finish_out)


def main_call(fuse, parts, big, small_in):
    (att, q8, key, val, nf, ohq, ohk, cos, sin, lse, pos, x, og, wp, we, wc, wq) = big
    rows, width = x.shape
    heads = q8.shape[1]
    hidden = we.shape[1]
    pairs, chunks = heads // PAIR, hidden // CHUNK
    shape = jax.ShapeDtypeStruct
    part_rows = width // parts
    sent = parts if fuse else 0
    if fuse:
        ff_shape, pq_shape = (chunks, part_rows, 2 * CHUNK), (pairs + 1, part_rows, 3 * PAIR)
        grain = (parts, part_rows)
        slots = chunks
    else:
        ff_shape, pq_shape = (chunks, 1, width, 2 * CHUNK), (pairs + 1, 1, width, 3 * PAIR)
        grain = (1, width)
        slots = 1
    outs = [
        shape((rows, width), BF16), shape((rows, width), F32), shape(ff_shape, F32),
        shape(pq_shape, F32), shape((16, width), F32),
    ]
    any_spec = pl.BlockSpec(memory_space=ANY)
    vm_spec = pl.BlockSpec(memory_space=pltpu.VMEM)
    V = pltpu.VMEM
    DMA = pltpu.SemaphoreType.DMA
    REG = pltpu.SemaphoreType.REGULAR
    blocks = rows // R
    lines = chunks + pairs + 1
    recv = (lambda n: V((slots, n, part_rows, 2 * CHUNK), F32)) if fuse else (lambda n: V((1, 1, 8, PAIR), F32))
    scratch = [
        V((rows, heads), F32), V((rows, heads), BF16), V((rows, heads), BF16), V((rows, heads), BF16),
        V((rows, PAIR), BF16), V((rows, PAIR), BF16), V((8, rows), F32), V((rows, PAIR), F32),
        V((rows, width), BF16), V((rows, width), BF16), V((heads, width), BF16),
        V((width, hidden), BF16), V((hidden, width), BF16),
        V((rows, width), F32), V((rows, width), F32), V((rows, width), F32), V((rows, width), F32),
        V((width, rows), BF16), V((rows, width), BF16), V((width, rows), BF16),
        V((rows, CHUNK), BF16), V((rows, CHUNK), BF16), V((rows, heads), BF16), V((8, rows), F32),
        V((rows, PAIR), BF16), V((rows, PAIR), BF16), V((heads, rows), BF16), V((PAIR, rows), BF16),
        V((rows, PAIR), F32), V((rows, PAIR), F32), V((PAIR, rows), F32), V((rows, 3 * PAIR), BF16),
        V((rows, PAIR), F32), V((rows, PAIR), F32), V((8, hidden), F32),
        V((chunks, *grain, 2 * CHUNK), F32), V((pairs + 1, *grain, 3 * PAIR), F32),
        recv(8), recv(4), recv(3), V((5, 16, width), F32), V((6, 16, width), F32),
        DMA((16,)), DMA((blocks,)), DMA((blocks,)), REG((blocks,)),
        DMA((lines,)), DMA((lines,)), DMA((lines,)), DMA((lines,)), DMA((lines,)), DMA((lines,)),
        REG((4,)), REG((4,)), REG((4,)), DMA((10,)), DMA((6,)), DMA((lines,)),
    ]
    return pl.pallas_call(
        partial(main_kernel, fuse, pairs, chunks),
        name="main",
        out_shape=outs,
        in_specs=[any_spec] * len(big) + [vm_spec] * len(small_in),
        out_specs=[any_spec] * len(outs),
        scratch_shapes=scratch,
        compiler_params=pltpu.CompilerParams(
            collective_id=0, has_side_effects=True, vmem_limit_bytes=67043328
        ),
    )(*big, *small_in)


def body(
    fuse, parts,
    patches, image_grids, out_grad, first_gain, first_shift, qkv_weight, qkv_bias, rope_freqs,
    proj_weight, proj_bias, second_gain, second_shift, expand_weight, expand_bias,
    contract_weight, contract_bias,
):
    width = patches.shape[1]
    heads = qkv_weight.shape[2]
    freqs = jnp.concatenate([rope_freqs, rope_freqs], axis=2).reshape(2, heads)
    row = lambda v: v.reshape(1, -1)
    q8, key, val, nf, att, lse, ohq, ohk, cos, sin, pos = front(
        image_grids, patches, row(first_gain), row(first_shift), qkv_weight, qkv_bias, freqs
    )
    mixed, pgrad, ff, pq, small = main_call(
        fuse,
        parts,
        (att, q8, key, val, nf, ohq, ohk, cos, sin, lse, pos, patches, out_grad,
         proj_weight, expand_weight, contract_weight, qkv_weight),
        (row(proj_bias), row(second_gain), row(second_shift), row(expand_bias),
         row(contract_bias), row(first_gain)),
    )
    pairs = heads // PAIR
    if not fuse:
        scatter = partial(lax.psum_scatter, axis_name="dp", scatter_dimension=1, tiled=True)
        ff = scatter(ff.reshape(ff.shape[0], width, ff.shape[-1]))
        pq = scatter(pq.reshape(pq.shape[0], width, pq.shape[-1]))
        small = lax.psum(small, "dp")
    mine = ff.shape[1]
    contract = ff[:, :, :CHUNK].transpose(0, 2, 1).reshape(-1, mine)
    expand = ff[:, :, CHUNK:].transpose(1, 0, 2).reshape(mine, -1)
    proj = pq[0].T
    qkv = pq[1:].reshape(pairs, mine, 3, PAIR).transpose(2, 1, 0, 3).reshape(3, mine, heads)
    rope = small[11:13, :heads].reshape(2, heads // HALF, 2, HALF // 2).sum(2)
    return (
        mixed, pgrad, qkv, proj, expand, contract,
        small[6], small[7], small[8:11, :heads], rope, small[3], small[1], small[2],
        small[4:6].reshape(-1), small[0],
    )


def solution(mesh):
    in_specs = (
        P("dp", None), P("dp", None), P("dp", None), P(), P(), P(None, None, "head"),
        P(None, "head"), P(None, "head", None), P("head", None), P(), P(), P(),
        P(None, "head"), P("head"), P("head", None), P(),
    )
    out_specs = (
        P("dp", None), P("dp", None), P(None, "dp", "head"), P("head", "dp"), P("dp", "head"),
        P("head", "dp"), P(), P(), P(None, "head"), P(None, "head", None), P(), P(), P(),
        P("head"), P(),
    )
    parts = mesh.shape["dp"]
    run = partial(body, parts == PARTS, parts)
    return jax.shard_map(run, mesh=mesh, in_specs=in_specs, out_specs=out_specs, check_vma=False)
```

```python
from functools import partial

import jax
import jax.numpy as jnp
from jax import lax
from jax.experimental import pallas as pl
from jax.experimental.pallas import tpu as pltpu
from jax.sharding import PartitionSpec as P

F32 = jnp.float32
BF16 = jnp.bfloat16
EPS = 1e-06
FAR = 2.0**100
R = 256
SUB = 64
PAIR = 128
HALF = 64
CHUNK = 256
MESH = pl.DeviceIdType.MESH
ANY = pl.ANY


def dot_nn(a, b):
    return lax.dot_general(a, b, (((1,), (0,)), ((), ())), preferred_element_type=F32)


def dot_nt(a, b):
    return lax.dot_general(a, b, (((1,), (1,)), ((), ())), preferred_element_type=F32)


def aligned(i, size):
    return pl.ds(pl.multiple_of(i * size, size), size)


def loop(count, fn):
    def step(i, carry):
        fn(i)
        return carry

    lax.fori_loop(0, count, step, 0)


def unit_of(rows):
    centred = rows - jnp.mean(rows, axis=-1, keepdims=True)
    inv = lax.rsqrt(jnp.mean(centred * centred, axis=-1, keepdims=True) + EPS)
    return centred * inv, inv


def norm_back(upstream, unit, inv, gain):
    scaled = upstream * gain
    return inv * (
        scaled
        - jnp.mean(scaled, axis=-1, keepdims=True)
        - unit * jnp.mean(scaled * unit, axis=-1, keepdims=True)
    )


def swap_halves(v, lane_first):
    return jnp.where(lane_first, pltpu.roll(v, PAIR - HALF // 2, 1), pltpu.roll(v, HALF // 2, 1))


def lane_ids(rows):
    return lax.broadcasted_iota(jnp.int32, (rows, PAIR), 1)


def head_mask(h):
    lane = lax.broadcasted_iota(jnp.int32, (1, PAIR), 1)
    return (lane // HALF == h).astype(F32)


def front_rows(grids, slots, x, gain, shift, w, b, freqs, q8, key, val, nf, ohq, ohk, cossin, pos):
    rows_all, width_all = q8.shape
    pairs = width_all // PAIR
    side = lax.broadcasted_iota(jnp.int32, (32, 1), 0).astype(F32)
    ang_r = side * freqs[0]
    ang_c = side * freqs[1]
    table_r = jnp.concatenate([jnp.cos(ang_r), jnp.sin(ang_r)], axis=1)
    table_c = jnp.concatenate([jnp.cos(ang_c), jnp.sin(ang_c)], axis=1)

    def first(r):
        rows = aligned(r, R)
        t = lax.broadcasted_iota(jnp.int32, (R, 1), 0) + r * R
        seg = jnp.zeros((R, 1), jnp.int32)
        start = jnp.zeros((R, 1), jnp.int32)
        width = jnp.ones((R, 1), jnp.int32)
        end = jnp.int32(0)
        for s in range(slots):
            begin = end
            end = end + grids[0, s] * grids[1, s]
            inside = (t >= begin) & (t < end)
            start = jnp.where(inside, begin, start)
            width = jnp.where(inside, grids[1, s], width)
            seg = seg + (t >= end).astype(jnp.int32)
        real = (seg < slots).astype(F32)
        off = (t - start).astype(F32)
        wide = width.astype(F32)
        grow = jnp.floor((off + 0.5) / wide) * real
        gcol = (off - grow * wide) * real
        lane = lane_ids(R)
        pos[rows, :] = (
            jnp.where(lane == 0, real, 0.0)
            + jnp.where(lane == 1, grow, 0.0)
            + jnp.where(lane == 2, gcol, 0.0)
        )
        hot = (lane % HALF == seg).astype(F32)
        ohq[rows, :] = hot.astype(BF16)
        ohk[rows, :] = ((1.0 - hot) * (-FAR)).astype(BF16)
        spot = lax.broadcasted_iota(jnp.int32, (R, 32), 1)
        hot_r = (spot == grow.astype(jnp.int32)).astype(F32)
        hot_c = (spot == gcol.astype(jnp.int32)).astype(F32)
        got_r = jnp.dot(hot_r, table_r, precision=lax.Precision.HIGHEST, preferred_element_type=F32)
        got_c = jnp.dot(hot_c, table_c, precision=lax.Precision.HIGHEST, preferred_element_type=F32)
        cr, sr = got_r[:, :width_all], got_r[:, width_all:]
        cc, sc = got_c[:, :width_all], got_c[:, width_all:]
        cossin[rows, :width_all] = cr * cc - sr * sc
        cossin[rows, width_all:] = sr * cc + cr * sc
        unit, _ = unit_of(x[rows, :].astype(F32))
        normed = (unit * gain + shift).astype(BF16)
        nf[rows, :] = normed
        lane_first = lane % HALF < HALF // 2
        sign = jnp.where(lane_first, -1.0, 1.0)
        for k, out in ((0, q8), (1, key)):
            got = dot_nn(normed, w[:, k * width_all : (k + 1) * width_all]) + b[k : k + 1, :]
            for p in range(pairs):
                cols = slice(p * PAIR, (p + 1) * PAIR)
                part = got[:, cols]
                turned = part * cossin[rows, cols] + swap_halves(part, lane_first) * (
                    cossin[rows, width_all + p * PAIR : width_all + (p + 1) * PAIR] * sign
                )
                turned = turned.astype(BF16)
                if k == 0:
                    turned = turned * jnp.asarray(HALF**-0.5, BF16)
                out[rows, cols] = turned
        got = dot_nn(normed, w[:, 2 * width_all : 3 * width_all])
        val[rows, :] = (got + b[2:3, :]).astype(BF16)

    loop(rows_all // R, first)


def front_heads(q8, key, val, ohq, ohk, att, lse, kx, lcol):
    rows_all, width_all = q8.shape

    def heads(p):
        cols = aligned(p, PAIR)
        for h in range(2):
            mine = head_mask(h).astype(BF16)
            other = head_mask(1 - h).astype(BF16)
            kx[...] = key[:, cols] * mine + ohk[...] * other

            def queries(r, h=h, mine=mine, other=other):
                rows = aligned(r, R)
                qx = q8[rows, cols] * mine + ohq[rows, :] * other
                score = dot_nt(qx, kx[...])
                top = jnp.max(score, axis=-1, keepdims=True)
                grown = jnp.exp(score - top)
                total = jnp.sum(grown, axis=-1, keepdims=True)
                got = dot_nn(grown.astype(BF16), val[:, cols]) * (1.0 / total)
                lane = lane_ids(R)
                log_sum = top + jnp.log(total)
                if h == 0:
                    att[rows, cols] = got
                else:
                    att[rows, cols] = jnp.where(lane < HALF, att[rows, cols], got)
                lcol[rows, :] = jnp.where(lane == p * 2 + h, log_sum, lcol[rows, :])

            loop(rows_all // R, queries)

    loop(width_all // PAIR, heads)

    def turn(r):
        rows = aligned(r, PAIR)
        lse[:, rows] = jnp.transpose(lcol[rows, :])[: lse.shape[0], :]

    loop(rows_all // PAIR, turn)


PARTS = 16


def main_kernel(
    fuse, pairs, chunks,
    x_h, og_h, wp_h, we_h, wc_h, wq_h,
    grids, freqs, bias_q, *rest,
):
    (
    gain_one, shift_one, bias_p, gain_two, shift_two, bias_e, bias_c,
    mixed_h, pgrad_h, ff_h, pq_h, small_h, nf_h, cossin_h,
    att, q8, key, val, ohq, ohk, lse, pos, x, cot, wp, we, wc,
    acc_a, acc_b, xbuf, mid, cott, ns, nst, act, hgb, dgrad, delta,
    km, vm, kt, kmt, dk, dv, dqt, qkvg, cos, sin, sums,
    gf, gq, r1, r2, r3, small, small_r,
    lsem, xs, xr, credit, s1, e1, s2, e2, s3, e3, c1, c2, c3, ms, mr, osem,
    ) = rest
    gain_one, shift_one, bias_p, gain_two, shift_two, bias_e, bias_c = (
        v[...].reshape(1, -1)
        for v in (gain_one, shift_one, bias_p, gain_two, shift_two, bias_e, bias_c)
    )
    me = lax.axis_index("dp")
    core = lax.axis_index("head")
    blocks = x.shape[0] // R
    subs = x.shape[0] // SUB
    mate = (me, 1 - core)
    if fuse:
        xx, yy, zz = me % 2, (me // 2) % 2, me // 4
        fst = xx * (1 - core) + yy * core
        snd = yy * (1 - core) + xx * core
        peer1 = (me + (1 - 2 * fst) * (1 + core), core)
        peer2 = (me + (1 - 2 * snd) * (2 - core), core)
        peers_z = [(((zz + j) % 4) * 4 + me % 4, core) for j in (1, 2, 3)]

        def where(z, f, s):
            return z * 4 + s * (2 - core) + f * (1 + core)

    def load(src, dst, i):
        copy = pltpu.make_async_copy(src, dst, lsem.at[i])
        copy.start()
        return copy

    heads = q8.shape[1]
    slots = grids.shape[1]
    get_x = load(x_h, x, 4)
    get_wq = [load(wq_h.at[k], we.at[:, pl.ds(k * heads, heads)], 7 + k) for k in range(3)]
    get_wp = load(wp_h, wp, 1)
    get_og = load(og_h, cot, 2)
    get_wc = load(wc_h, wc, 6)

    barrier = pltpu.get_barrier_semaphore()
    friends = [mate] + ([peer1, peer2] + peers_z if fuse else [])
    for friend in friends:
        pl.semaphore_signal(barrier, inc=1, device_id=friend, device_id_type=MESH)

    def exchange(src, r):
        return pltpu.make_async_remote_copy(
            src.at[aligned(r, R), :], xbuf.at[aligned(r, R), :], xs.at[r], xr.at[r],
            device_id=mate, device_id_type=MESH,
        )

    def send(src, r):
        exchange(src, r).start()

    def give_credit(r):
        pl.semaphore_signal(credit.at[r], inc=1, device_id=mate, device_id_type=MESH)

    def take_credit(r):
        pl.semaphore_wait(credit.at[r], 1)

    def remote(src, dst, ss, rs, peer):
        return pltpu.make_async_remote_copy(
            src, dst, ss, rs, device_id=peer, device_id_type=MESH
        )

    class Line:
        def __init__(self, grads, base, width, out, guard):
            self.g, self.base, self.n, self.out, self.guard = grads, base, width, out, guard

        def buf(self, buf, j, b):
            return buf.at[j, b, :, pl.ds(0, self.n)]

        def whole(self, buf, j):
            return buf.at[j, :, :, pl.ds(0, self.n)]

        def start1(self, j):
            if self.guard == "take":
                pl.semaphore_wait(c1.at[j], 1)

            def one(i):
                remote(
                    self.g.at[j, where(i // 2, 1 - fst, i % 2)], self.buf(r1, j, i),
                    s1.at[self.base + j], e1.at[self.base + j], peer1,
                ).start()

            loop(8, one)

        def give(self, sem, j, peers):
            if self.guard == "give":
                def go():
                    for peer in peers:
                        pl.semaphore_signal(sem.at[j], inc=1, device_id=peer, device_id_type=MESH)
                if isinstance(j, int):
                    if j < 4:
                        go()
                else:
                    pl.when(j < 4)(go)

        def finish1(self, j):
            remote(
                self.g.at[j, pl.ds(0, 8)], self.whole(r1, j),
                s1.at[self.base + j], e1.at[self.base + j], peer1,
            ).wait_recv()

            def one(i):
                b = where(i // 2, fst, i % 2)
                self.g[j, b] = self.g[j, b] + self.buf(r1, j, i)[...]

            loop(8, one)
            self.give(c1, j, [peer1])
            if self.guard == "take":
                pl.semaphore_wait(c2.at[j], 1)

            def two(i):
                remote(
                    self.g.at[j, where(i, fst, 1 - snd)], self.buf(r2, j, i),
                    s2.at[self.base + j], e2.at[self.base + j], peer2,
                ).start()

            loop(4, two)

        def finish2(self, j):
            remote(
                self.g.at[j, pl.ds(0, 4)], self.whole(r2, j),
                s2.at[self.base + j], e2.at[self.base + j], peer2,
            ).wait_recv()

            def one(i):
                b = where(i, fst, snd)
                self.g[j, b] = self.g[j, b] + self.buf(r2, j, i)[...]

            loop(4, one)
            self.give(c2, j, [peer2])
            if self.guard == "take":
                pl.semaphore_wait(c3.at[j], 3)
            for k in range(3):
                remote(
                    self.g.at[j, where((zz + k + 1) % 4, fst, snd)], self.buf(r3, j, k),
                    s3.at[self.base + j], e3.at[self.base + j], peers_z[k],
                ).start()

        def finish3(self, j):
            remote(
                self.g.at[j, pl.ds(0, 3)], self.whole(r3, j),
                s3.at[self.base + j], e3.at[self.base + j], peers_z[0],
            ).wait_recv()
            self.g[j, me] = (
                self.g[j, me]
                + self.buf(r3, j, 0)[...] + self.buf(r3, j, 1)[...] + self.buf(r3, j, 2)[...]
            )
            self.give(c3, j, peers_z)
            pltpu.make_async_copy(self.g.at[j, me], self.out.at[j], osem.at[self.base + j]).start()

        def drain(self, j):
            for src, dst, ss, rs, peer in (
                (self.g.at[j, pl.ds(0, 8)], self.whole(r1, j), s1, e1, peer1),
                (self.g.at[j, pl.ds(0, 4)], self.whole(r2, j), s2, e2, peer2),
                (self.g.at[j, pl.ds(0, 3)], self.whole(r3, j), s3, e3, peers_z[0]),
            ):
                remote(src, dst, ss.at[self.base + j], rs.at[self.base + j], peer).wait_send()
            pltpu.make_async_copy(self.g.at[j, me], self.out.at[j], osem.at[self.base + j]).wait()

    class Plain:
        def __init__(self, grads, base, width, out, guard):
            self.g, self.base, self.out = grads, base, out

        def copy(self, j):
            return pltpu.make_async_copy(self.g.at[j], self.out.at[j], osem.at[self.base + j])

        def start1(self, j):
            self.copy(j).start()

        def finish1(self, j):
            pass

        finish2 = finish3 = finish1

        def drain(self, j):
            self.copy(j).wait()

    kind = Line if fuse else Plain
    ff = kind(gf, 0, 2 * CHUNK, ff_h, "give")
    pq = kind(gq, chunks, 3 * PAIR, pq_h, "take")

    small[...] = jnp.zeros_like(small)
    sums[...] = jnp.zeros_like(sums)
    sums[7:8, :] = bias_e

    get_x.wait()
    for copy in get_wq:
        copy.wait()
    turns = []
    for axis in range(2):
        lines = [freqs[n, axis : axis + 1, :] for n in range(heads // HALF) for _ in range(2)]
        turns.append(jnp.concatenate(lines, axis=1))
    front_rows(
        grids, slots, x, gain_one, shift_one, we, bias_q, turns,
        q8, key, val, ns, ohq, ohk, acc_b, pos,
    )
    get_we = load(we_h, we, 5)
    put_nf = load(ns, nf_h, 10)
    put_cossin = load(acc_b.at[:, pl.ds(0, 2 * heads)], cossin_h, 11)
    front_heads(q8, key, val, ohq, ohk, att, lse, km, dk)
    pl.semaphore_wait(barrier, len(friends))
    get_wp.wait()

    def project(r):
        acc_a[aligned(r, R), :] = dot_nn(att[aligned(r, R), :].astype(BF16), wp[...])
        send(acc_a, r)

    loop(blocks, project)

    get_og.wait()

    def mask_cot(r):
        rows = aligned(r, R)
        block = (cot[rows, :].astype(F32) * pos[rows, 0:1])
        small[0, 0:1, :] = small[0, 0:1, :] + jnp.sum(block, axis=0, keepdims=True)
        low = block.astype(BF16)
        cot[rows, :] = low
        cott[:, rows] = jnp.transpose(low)

    loop(blocks, mask_cot)
    put_nf.wait()
    put_cossin.wait()

    def second_norm(r):
        exchange(acc_a, r).wait()

        def sub(i):
            rows = pl.ds(pl.multiple_of(r * R + i * SUB, SUB), SUB)
            middle = x[rows, :].astype(F32) + ((acc_a[rows, :] + xbuf[rows, :]) + bias_p)
            unit, _ = unit_of(middle)
            mid[rows, :] = middle
            ns[rows, :] = (unit * gain_two + shift_two).astype(BF16)
            acc_b[rows, :] = 0.5 * (middle + bias_c)
            acc_a[rows, :] = jnp.zeros_like(middle)

        loop(R // SUB, sub)
        give_credit(r)
        nst[:, aligned(r, R)] = jnp.transpose(ns[aligned(r, R), :])

    loop(blocks, second_norm)
    get_we.wait()
    get_wc.wait()

    def feed(j):
        cols = aligned(j, CHUNK)

        def rows_of(r):
            rows = aligned(r, R)
            hidden = dot_nn(ns[rows, :], we[:, cols]) + sums[7:8, cols]
            upstream = dot_nt(cot[rows, :], wc[cols, :])
            phi = 0.5 * (1.0 + lax.erf(hidden * (0.5**0.5)))
            slope = phi + hidden * (jnp.exp(-0.5 * hidden * hidden) * (0.3989422804014327))
            active = (hidden * phi).astype(BF16)
            hgrad = (upstream * slope).astype(BF16)
            act[rows, :] = active
            hgb[rows, :] = hgrad
            sums[0:1, cols] = sums[0:1, cols] + jnp.sum(hgrad.astype(F32), axis=0, keepdims=True)
            acc_b[rows, :] = acc_b[rows, :] + dot_nn(active, wc[cols, :])
            acc_a[rows, :] = acc_a[rows, :] + dot_nt(hgrad, we[:, cols])

        loop(blocks, rows_of)
        got = dot_nn(cott[...], act[...])
        gf[j, :, :, pl.ds(0, CHUNK)] = got.reshape(gf.shape[1], gf.shape[2], CHUNK)
        got = dot_nn(nst[...], hgb[...])
        gf[j, :, :, pl.ds(CHUNK, CHUNK)] = got.reshape(gf.shape[1], gf.shape[2], CHUNK)
        ff.start1(j)
        if fuse:
            pl.when(j == 3)(lambda: ff.finish1(0))

    loop(chunks, feed)

    def send_second(r):
        take_credit(r)
        send(acc_a, r)

    loop(blocks, send_second)
    get_nf = load(nf_h, ns, 0)
    ff.finish1(1)

    def second_back(r):
        exchange(acc_a, r).wait()

        def sub(i):
            rows = pl.ds(pl.multiple_of(r * R + i * SUB, SUB), SUB)
            up = acc_a[rows, :] + xbuf[rows, :]
            unit, inv = unit_of(mid[rows, :])
            small[0, 1:2, :] = small[0, 1:2, :] + jnp.sum(up * unit, axis=0, keepdims=True)
            small[0, 2:3, :] = small[0, 2:3, :] + jnp.sum(up, axis=0, keepdims=True)
            grad = cot[rows, :].astype(F32) + norm_back(up, unit, inv, gain_two)
            mid[rows, :] = grad
            low = grad.astype(BF16)
            cot[rows, :] = low
            small[0, 3:4, :] = small[0, 3:4, :] + jnp.sum(
                low.astype(F32), axis=0, keepdims=True
            )
            acc_a[rows, :] = jnp.zeros_like(up)

        loop(R // SUB, sub)
        give_credit(r)
        rows = aligned(r, R)
        cott[:, rows] = jnp.transpose(cot[rows, :])
        low = dot_nt(cot[rows, :], wp[...]).astype(BF16)
        dgrad[rows, :] = low
        prod = low.astype(F32) * att[rows, :]
        head = lax.broadcasted_iota(jnp.int32, (8, prod.shape[1]), 0)
        lane = lax.broadcasted_iota(jnp.int32, (8, prod.shape[1]), 1)
        pick = (lane // HALF == head).astype(F32)
        delta[:, rows] = lax.dot_general(
            pick, prod, (((1,), (1,)), ((), ())), precision=lax.Precision.HIGHEST,
            preferred_element_type=F32,
        )

    loop(blocks, second_back)
    ff.finish2(0)
    gq[0] = dot_nn(cott[...], att[...].astype(BF16)).reshape(gq.shape[1:])
    pq.start1(0)
    ff.finish1(2)

    def send_mixed(r):
        take_credit(r)
        send(acc_b, r)

    loop(blocks, send_mixed)

    get_nf.wait()

    def turn_first(r):
        nst[:, aligned(r, R)] = jnp.transpose(ns[aligned(r, R), :])

    loop(blocks, turn_first)
    get_wq = [
        load(wq_h.at[k], we.at[:, pl.ds(k * pairs * PAIR, pairs * PAIR)], 4 + k) for k in range(3)
    ]
    kt[...] = jnp.transpose(key[...])

    def mixed_block(r):
        exchange(acc_b, r).wait()
        rows = aligned(r, R)
        ns[rows, :] = (acc_b[rows, :] + xbuf[rows, :]).astype(BF16)
        give_credit(r)
        pltpu.make_async_copy(ns.at[rows, :], mixed_h.at[rows, :], ms.at[r]).start()

    loop(blocks, mixed_block)
    for copy in get_wq:
        copy.wait()

    def pair_back(p):
        cols = aligned(p, PAIR)
        get_cos = load(cossin_h.at[:, cols], cos, 0)
        get_sin = load(cossin_h.at[:, aligned(pairs + p, PAIR)], sin, 1)
        dk[...] = jnp.zeros_like(dk)
        dv[...] = jnp.zeros_like(dv)
        dqt[...] = jnp.zeros_like(dqt)

        def head_back(h):
            mine = head_mask(h).astype(BF16)
            other = head_mask(1 - h).astype(BF16)
            km[...] = key[:, cols] * mine + ohk[...] * other
            vm[...] = val[:, cols] * mine
            spot = lax.broadcasted_iota(jnp.int32, (PAIR, 1), 0)
            kmt[...] = kt[cols, :] * (spot // HALF == h).astype(F32).astype(BF16)
            n = p * 2 + h

            def query_back(r):
                rows = aligned(r, R)
                qm = q8[rows, cols] * mine
                qx = qm + ohq[rows, :] * other
                do = dgrad[rows, cols]
                score = dot_nt(km[...], qx)
                prob = jnp.exp(score - lse[pl.ds(n, 1), rows])
                pgrad = dot_nt(vm[...], do)
                sgrad = (prob * (pgrad - delta[pl.ds(n, 1), rows])).astype(BF16)
                dv[...] = dv[...] + dot_nn(prob.astype(BF16), do * mine)
                dk[...] = dk[...] + dot_nn(sgrad, qm)
                dqt[:, rows] = dqt[:, rows] + dot_nn(kmt[...], sgrad)

            loop(blocks, query_back)
            if fuse:
                if h == 0:
                    ff.finish2(p + 1)
                else:
                    ff.finish1(p + 3)

        head_back(0)
        head_back(1)
        get_cos.wait()
        get_sin.wait()

        def turn_back(r):
            rows = aligned(r, R)
            lane_first = lane_ids(R) % HALF < HALF // 2
            sign = jnp.where(lane_first, 1.0, -1.0)
            c, s = cos[rows, :], sin[rows, :]
            total = jnp.zeros((R, PAIR), F32)
            grads = []
            scale = HALF**-0.5
            for k, (grad, turned) in enumerate(
                (
                    (jnp.transpose(dqt[:, rows]) * scale, q8[rows, cols].astype(F32) * (1.0 / scale)),
                    (dk[rows, :], key[rows, cols].astype(F32)),
                )
            ):
                swapped = swap_halves(grad, lane_first) * sign
                total = total + swapped * turned
                grads.append((grad * c + swapped * s).astype(BF16))
            grads.append(dv[rows, :].astype(BF16))
            for k, low in enumerate(grads):
                qkvg[rows, k * PAIR : (k + 1) * PAIR] = low
                sums[k + 1 : k + 2, cols] = sums[k + 1 : k + 2, cols] + jnp.sum(
                    low.astype(F32), axis=0, keepdims=True
                )
            for k in range(2):
                sums[k + 4 : k + 5, cols] = sums[k + 4 : k + 5, cols] + jnp.sum(
                    total * pos[rows, k + 1 : k + 2], axis=0, keepdims=True
                )
            weight = jnp.concatenate(
                [we[:, aligned(k * pairs + p, PAIR)] for k in range(3)], axis=1
            )
            acc_a[rows, :] = acc_a[rows, :] + dot_nt(qkvg[rows, :], weight)

        loop(blocks, turn_back)
        gq[p + 1] = dot_nn(nst[...], qkvg[...]).reshape(gq.shape[1:])
        pq.start1(p + 1)
        if fuse:
            ff.finish3(p)

    loop(pairs, pair_back)

    def first_send(r):
        def sub(i):
            rows = pl.ds(pl.multiple_of(r * R + i * SUB, SUB), SUB)
            unit, _ = unit_of(x[rows, :].astype(F32))
            up = acc_a[rows, :]
            small[0, 6:7, :] = small[0, 6:7, :] + jnp.sum(up * unit, axis=0, keepdims=True)
            small[0, 7:8, :] = small[0, 7:8, :] + jnp.sum(up, axis=0, keepdims=True)

        take_credit(r)
        send(acc_a, r)
        loop(R // SUB, sub)

    loop(blocks, first_send)

    n = chunks * CHUNK // 2
    small[0, 4:5, :] = sums[0:1, 0:n]
    small[0, 5:6, :] = sums[0:1, n : 2 * n]
    m = pairs * PAIR
    for k in range(5):
        small[0, 8 + k : 9 + k, 0:m] = sums[1 + k : 2 + k, 0:m]

    def small_copy(i, k, peer):
        return remote(small.at[k], small_r.at[i], ms.at[4 + i], mr.at[i], peer)

    copy = small_copy(0, 0, mate)
    copy.start()
    if fuse:
        ff.finish2(4)
        pq.finish1(0)
        ff.finish3(3)
    copy.wait()
    line = lax.broadcasted_iota(jnp.int32, small.shape[1:], 0)
    small[1] = small[0] + jnp.where((line == 6) | (line == 7), small_r[0], 0.0)
    if fuse:
        copy = small_copy(1, 1, peer1)
        copy.start()
        ff.finish2(5)
        copy.wait()
        small[2] = small[1] + small_r[1]
        copy = small_copy(2, 2, peer2)
        copy.start()
        pq.finish1(1)
        pq.finish2(0)
        ff.finish3(4)
        copy.wait()
        small[3] = small[2] + small_r[2]
        copies = [small_copy(3 + k, 3, peers_z[k]) for k in range(3)]
        for copy in copies:
            copy.start()
    last = 4 if fuse else 1

    def first_back(r):
        exchange(acc_a, r).wait()

        def sub(i):
            rows = pl.ds(pl.multiple_of(r * R + i * SUB, SUB), SUB)
            unit, inv = unit_of(x[rows, :].astype(F32))
            up = acc_a[rows, :] + xbuf[rows, :]
            mid[rows, :] = mid[rows, :] + norm_back(up, unit, inv, gain_one)

        loop(R // SUB, sub)
        rows = aligned(r, R)
        pltpu.make_async_copy(mid.at[rows, :], pgrad_h.at[rows, :], xs.at[r]).start()

    loop(blocks, first_back)
    if fuse:
        for copy in copies:
            copy.wait()
        small[4] = small[3] + (small_r[3] + small_r[4] + small_r[5])
    out_small = pltpu.make_async_copy(small.at[last], small_h, lsem.at[0])
    out_small.start()
    if fuse:
        pq.finish1(2)
        pq.finish2(1)
        ff.finish3(5)
        pq.finish3(0)
        pq.finish1(3)
        pq.finish2(2)
        pq.finish3(1)
        pq.finish2(3)
        pq.finish3(2)
        pq.finish3(3)
    loop(chunks, ff.drain)
    loop(pairs + 1, pq.drain)
    out_small.wait()

    def finish_out(r):
        rows = aligned(r, R)
        pltpu.make_async_copy(ns.at[rows, :], mixed_h.at[rows, :], ms.at[r]).wait()
        pltpu.make_async_copy(mid.at[rows, :], pgrad_h.at[rows, :], xs.at[r]).wait()

    loop(blocks, finish_out)


def main_call(fuse, parts, big, grids, freqs, bias_q, vectors):
    x, og, wp, we, wc, wq = big
    rows, width = x.shape
    heads = wq.shape[2]
    hidden = we.shape[1]
    pairs, chunks = heads // PAIR, hidden // CHUNK
    shape = jax.ShapeDtypeStruct
    part_rows = width // parts
    sent = parts if fuse else 0
    if fuse:
        ff_shape, pq_shape = (chunks, part_rows, 2 * CHUNK), (pairs + 1, part_rows, 3 * PAIR)
        grain = (parts, part_rows)
        slots = chunks
    else:
        ff_shape, pq_shape = (chunks, 1, width, 2 * CHUNK), (pairs + 1, 1, width, 3 * PAIR)
        grain = (1, width)
        slots = 1
    outs = [
        shape((rows, width), BF16), shape((rows, width), F32), shape(ff_shape, F32),
        shape(pq_shape, F32), shape((16, width), F32), shape((rows, width), BF16),
        shape((rows, 2 * heads), F32),
    ]
    any_spec = pl.BlockSpec(memory_space=ANY)
    vm_spec = pl.BlockSpec(memory_space=pltpu.VMEM)
    V = pltpu.VMEM
    DMA = pltpu.SemaphoreType.DMA
    REG = pltpu.SemaphoreType.REGULAR
    blocks = rows // R
    lines = chunks + pairs + 1
    recv = (lambda n: V((slots, n, part_rows, 2 * CHUNK), F32)) if fuse else (lambda n: V((1, 1, 8, PAIR), F32))
    scratch = [
        V((rows, heads), F32), V((rows, heads), BF16), V((rows, heads), BF16), V((rows, heads), BF16),
        V((rows, PAIR), BF16), V((rows, PAIR), BF16), V((8, rows), F32), V((rows, PAIR), F32),
        V((rows, width), BF16), V((rows, width), BF16), V((heads, width), BF16),
        V((width, hidden), BF16), V((hidden, width), BF16),
        V((rows, width), F32), V((rows, width), F32), V((rows, width), F32), V((rows, width), F32),
        V((width, rows), BF16), V((rows, width), BF16), V((width, rows), BF16),
        V((rows, CHUNK), BF16), V((rows, CHUNK), BF16), V((rows, heads), BF16), V((8, rows), F32),
        V((rows, PAIR), BF16), V((rows, PAIR), BF16), V((heads, rows), BF16), V((PAIR, rows), BF16),
        V((rows, PAIR), F32), V((rows, PAIR), F32), V((PAIR, rows), F32), V((rows, 3 * PAIR), BF16),
        V((rows, PAIR), F32), V((rows, PAIR), F32), V((8, hidden), F32),
        V((chunks, *grain, 2 * CHUNK), F32), V((pairs + 1, *grain, 3 * PAIR), F32),
        recv(8), recv(4), recv(3), V((5, 16, width), F32), V((6, 16, width), F32),
        DMA((16,)), DMA((blocks,)), DMA((blocks,)), REG((blocks,)),
        DMA((lines,)), DMA((lines,)), DMA((lines,)), DMA((lines,)), DMA((lines,)), DMA((lines,)),
        REG((4,)), REG((4,)), REG((4,)), DMA((10,)), DMA((6,)), DMA((lines,)),
    ]
    return pl.pallas_call(
        partial(main_kernel, fuse, pairs, chunks),
        name="main",
        out_shape=outs,
        in_specs=[any_spec] * len(big)
        + [pl.BlockSpec(memory_space=pltpu.SMEM)]
        + [vm_spec] * (2 + len(vectors)),
        out_specs=[any_spec] * len(outs),
        scratch_shapes=scratch,
        compiler_params=pltpu.CompilerParams(
            collective_id=0, has_side_effects=True, vmem_limit_bytes=67043328
        ),
    )(*big, grids, freqs, bias_q, *vectors)


def finish_kernel(
    mixed_h, pgrad_h, ff_h, pq_h, small_h,
    mixed_o, pgrad_o, qkv_o, proj_o, expand_o, contract_o,
    gain_one, shift_one, bias_q, rope, bias_p, gain_two, shift_two, bias_e, bias_c,
    mixed, pgrad, ff, pq, small, isem, osem,
):
    blocks = mixed.shape[0] // R
    chunks, pairs = ff.shape[0], pq.shape[0] - 1
    jobs = [(small_h, small, [])]
    for src, buf, dst in ((pgrad_h, pgrad, pgrad_o), (mixed_h, mixed, mixed_o)):
        for r in range(blocks):
            part = (pl.ds(r * R, R), slice(None))
            jobs.append((src.at[part], buf.at[part], [(buf.at[part], dst.at[part])]))
    for j in range(chunks):
        cols = pl.ds(j * CHUNK, CHUNK)
        jobs.append((ff_h.at[j], ff.at[j], [
            (ff.at[j, :, pl.ds(0, CHUNK)], contract_o.at[:, cols]),
            (ff.at[j, :, pl.ds(CHUNK, CHUNK)], expand_o.at[:, cols]),
        ]))
    jobs.append((pq_h.at[0], pq.at[0], [(pq.at[0], proj_o)]))
    for p in range(pairs):
        jobs.append((pq_h.at[p + 1], pq.at[p + 1], [
            (pq.at[p + 1, :, pl.ds(k * PAIR, PAIR)], qkv_o.at[k, :, pl.ds(p * PAIR, PAIR)])
            for k in range(3)
        ]))
    gets = [pltpu.make_async_copy(a, b, isem.at[i]) for i, (a, b, _) in enumerate(jobs)]
    for get in gets:
        get.start()
    puts = []
    for get, (_, _, todo) in zip(gets, jobs):
        get.wait()
        for a, b in todo:
            puts.append(pltpu.make_async_copy(a, b, osem.at[len(puts)]))
            puts[-1].start()
    heads = bias_q.shape[1]
    for k, out in (
        (6, gain_one), (7, shift_one), (3, bias_p), (1, gain_two), (2, shift_two), (0, bias_c),
    ):
        out[...] = small[k, :]
    half = bias_e.shape[0] // 2
    bias_e[:half] = small[4, :half]
    bias_e[half:] = small[5, :half]
    bias_q[...] = small[8:11, :heads]
    for p in range(pairs):
        tile = small[8:16, p * PAIR : (p + 1) * PAIR]
        both = tile + pltpu.roll(tile, PAIR - HALF // 2, 1)
        rope[2 * p] = both[3:5, : HALF // 2]
        rope[2 * p + 1] = pltpu.roll(both, HALF, 1)[3:5, : HALF // 2]
    for put in puts:
        put.wait()


def finish(mixed, pgrad, ff, pq, small, hidden):
    rows, width = mixed.shape
    mine = ff.shape[1]
    heads = pq.shape[2]
    shape = lambda *s: jax.ShapeDtypeStruct(s, F32)
    outs = [
        jax.ShapeDtypeStruct((rows, width), BF16), shape(rows, width), shape(3, mine, heads),
        shape(mine, heads), shape(mine, hidden), shape(mine, hidden), shape(width), shape(width),
        shape(3, heads), shape(heads // HALF, 2, HALF // 2), shape(width), shape(width),
        shape(width), shape(hidden), shape(width),
    ]
    any_spec = pl.BlockSpec(memory_space=ANY)
    vm_spec = pl.BlockSpec(memory_space=pltpu.VMEM)
    reads = 1 + 2 * (rows // R) + ff.shape[0] + pq.shape[0]
    writes = 2 * (rows // R) + 2 * ff.shape[0] + 3 * pq.shape[0] - 2
    big = (mixed, pgrad, ff, pq, small)
    return pl.pallas_call(
        finish_kernel,
        name="finish",
        out_shape=outs,
        in_specs=[any_spec] * 5,
        out_specs=[any_spec] * 6 + [vm_spec] * (len(outs) - 6),
        scratch_shapes=[pltpu.VMEM(v.shape, v.dtype) for v in big]
        + [pltpu.SemaphoreType.DMA((reads,)), pltpu.SemaphoreType.DMA((writes,))],
        compiler_params=pltpu.CompilerParams(vmem_limit_bytes=67043328),
    )(*big)


def body(
    fuse, parts,
    patches, image_grids, out_grad, first_gain, first_shift, qkv_weight, qkv_bias, rope_freqs,
    proj_weight, proj_bias, second_gain, second_shift, expand_weight, expand_bias,
    contract_weight, contract_bias,
):
    width = patches.shape[1]
    mixed, pgrad, ff, pq, small, _, _ = main_call(
        fuse,
        parts,
        (patches, out_grad, proj_weight, expand_weight, contract_weight, qkv_weight),
        image_grids.T,
        rope_freqs.transpose(1, 0, 2),
        qkv_bias,
        (first_gain, first_shift, proj_bias, second_gain, second_shift, expand_bias, contract_bias),
    )
    if not fuse:
        scatter = partial(lax.psum_scatter, axis_name="dp", scatter_dimension=1, tiled=True)
        ff = scatter(ff.reshape(ff.shape[0], width, ff.shape[-1]))
        pq = scatter(pq.reshape(pq.shape[0], width, pq.shape[-1]))
        small = lax.psum(small, "dp")
    (
        mixed, pgrad, qkv, proj, expand, contract, gain_one, shift_one, bias_q, rope,
        bias_p, gain_two, shift_two, bias_e, bias_c,
    ) = finish(mixed, pgrad, ff, pq, small, expand_bias.shape[0])
    return (
        mixed, pgrad, qkv, proj.T, expand, contract.T, gain_one, shift_one, bias_q,
        rope.transpose(1, 0, 2), bias_p, gain_two, shift_two, bias_e, bias_c,
    )


def solution(mesh):
    in_specs = (
        P("dp", None), P("dp", None), P("dp", None), P(), P(), P(None, None, "head"),
        P(None, "head"), P(None, "head", None), P("head", None), P(), P(), P(),
        P(None, "head"), P("head"), P("head", None), P(),
    )
    out_specs = (
        P("dp", None), P("dp", None), P(None, "dp", "head"), P("head", "dp"), P("dp", "head"),
        P("head", "dp"), P(), P(), P(None, "head"), P(None, "head", None), P(), P(), P(),
        P("head"), P(),
    )
    parts = mesh.shape["dp"]
    run = partial(body, parts == PARTS, parts)
    return jax.shard_map(run, mesh=mesh, in_specs=in_specs, out_specs=out_specs, check_vma=False)
```

```python
from functools import partial

import jax
import jax.numpy as jnp
from jax import lax
from jax.experimental import pallas as pl
from jax.experimental.pallas import tpu as pltpu
from jax.sharding import PartitionSpec as P

F32 = jnp.float32
BF16 = jnp.bfloat16
EPS = 1e-06
FAR = 2.0**100
R = 256
SUB = 64
PAIR = 128
HALF = 64
CHUNK = 256
MESH = pl.DeviceIdType.MESH
ANY = pl.ANY


def dot_nn(a, b):
    return lax.dot_general(a, b, (((1,), (0,)), ((), ())), preferred_element_type=F32)


def dot_nt(a, b):
    return lax.dot_general(a, b, (((1,), (1,)), ((), ())), preferred_element_type=F32)


def aligned(i, size):
    return pl.ds(pl.multiple_of(i * size, size), size)


def loop(count, fn):
    def step(i, carry):
        fn(i)
        return carry

    lax.fori_loop(0, count, step, 0)


def unit_of(rows):
    centred = rows - jnp.mean(rows, axis=-1, keepdims=True)
    inv = lax.rsqrt(jnp.mean(centred * centred, axis=-1, keepdims=True) + EPS)
    return centred * inv, inv


def norm_back(upstream, unit, inv, gain):
    scaled = upstream * gain
    return inv * (
        scaled
        - jnp.mean(scaled, axis=-1, keepdims=True)
        - unit * jnp.mean(scaled * unit, axis=-1, keepdims=True)
    )


def swap_halves(v, lane_first):
    return jnp.where(lane_first, pltpu.roll(v, PAIR - HALF // 2, 1), pltpu.roll(v, HALF // 2, 1))


def lane_ids(rows):
    return lax.broadcasted_iota(jnp.int32, (rows, PAIR), 1)


def head_mask(h):
    lane = lax.broadcasted_iota(jnp.int32, (1, PAIR), 1)
    return (lane // HALF == h).astype(F32)


def pieces(table):
    high = table.astype(BF16)
    rest = table - high.astype(F32)
    mid = rest.astype(BF16)
    low = (rest - mid.astype(F32)).astype(BF16)
    return jnp.concatenate([high, mid, low], axis=0)


def front_place(grids, slots, freqs, ohq, ohk, cossin, pos):
    rows_all, width_all = pos.shape[0], freqs[0].shape[1]
    side = lax.broadcasted_iota(jnp.int32, (32, 1), 0).astype(F32)
    ang_r = side * freqs[0]
    ang_c = side * freqs[1]
    table_r = pieces(jnp.concatenate([jnp.cos(ang_r), jnp.sin(ang_r)], axis=1))
    table_c = pieces(jnp.concatenate([jnp.cos(ang_c), jnp.sin(ang_c)], axis=1))

    def place(r):
        rows = aligned(r, 256)
        t = lax.broadcasted_iota(jnp.int32, (256, 1), 0) + r * 256
        seg = jnp.zeros((256, 1), jnp.int32)
        start = jnp.zeros((256, 1), jnp.int32)
        width = jnp.ones((256, 1), jnp.int32)
        end = jnp.int32(0)
        for s in range(slots):
            begun = t >= end
            start = jnp.where(begun, end, start)
            width = jnp.where(begun, jnp.maximum(grids[1, s], 1), width)
            end = end + grids[0, s] * grids[1, s]
            seg = jnp.where(t >= end, s + 1, seg)
        real = (seg < slots).astype(F32)
        off = (t - start).astype(F32)
        wide = width.astype(F32)
        grow = jnp.floor((off + 0.5) / wide) * real
        gcol = (off - grow * wide) * real
        lane = lane_ids(256)
        pos[rows, :] = jnp.where(lane == 0, real, jnp.where(lane == 1, grow, gcol))
        hot = lane % HALF == seg
        ohq[rows, :] = jnp.where(hot, 1.0, 0.0).astype(BF16)
        ohk[rows, :] = jnp.where(hot, 0.0, -FAR).astype(BF16)
        spot = (lax.broadcasted_iota(jnp.int32, (256, 96), 1) % 32).astype(F32)
        got_r = dot_nn(jnp.where(spot == grow, 1.0, 0.0).astype(BF16), table_r)
        got_c = dot_nn(jnp.where(spot == gcol, 1.0, 0.0).astype(BF16), table_c)
        cr, sr = got_r[:, :width_all], got_r[:, width_all:]
        cc, sc = got_c[:, :width_all], got_c[:, width_all:]
        cossin[rows, :width_all] = cr * cc - sr * sc
        cossin[rows, width_all:] = sr * cc + cr * sc

    loop(rows_all // 256, place)


def front_rows(x, gain, shift, w, b, q8, key, val, nf, cossin):
    rows_all, width_all = q8.shape
    pairs = width_all // PAIR

    def norm(r):
        rows = aligned(r, SUB)
        unit, _ = unit_of(x[rows, :].astype(F32))
        nf[rows, :] = (unit * gain + shift).astype(BF16)

    loop(rows_all // SUB, norm)

    def project(r):
        rows = aligned(r, R)
        lane_first = lane_ids(R) % HALF < HALF // 2
        sign = jnp.where(lane_first, -1.0, 1.0)
        for k, out in ((0, q8), (1, key)):
            got = dot_nn(nf[rows, :], w[:, k * width_all : (k + 1) * width_all]) + b[k : k + 1, :]
            for p in range(pairs):
                cols = slice(p * PAIR, (p + 1) * PAIR)
                part = got[:, cols]
                turned = part * cossin[rows, cols] + swap_halves(part, lane_first) * (
                    cossin[rows, width_all + p * PAIR : width_all + (p + 1) * PAIR] * sign
                )
                turned = turned.astype(BF16)
                if k == 0:
                    turned = turned * jnp.asarray(HALF**-0.5, BF16)
                out[rows, cols] = turned
        got = dot_nn(nf[rows, :], w[:, 2 * width_all : 3 * width_all])
        val[rows, :] = (got + b[2:3, :]).astype(BF16)

    loop(rows_all // R, project)


def front_heads(q8, key, val, ohq, ohk, att, lse, kxs, scs, lcol):
    rows_all, width_all = q8.shape
    blocks = rows_all // R
    masks = [head_mask(h).astype(BF16) for h in range(2)]

    def heads(p):
        cols = aligned(p, PAIR)
        for h in range(2):
            kxs[h][...] = key[:, cols] * masks[h] + ohk[...] * masks[1 - h]

        def scores(h, r):
            rows = aligned(r, R)
            scs[h][...] = dot_nt(q8[rows, cols] * masks[h] + ohq[rows, :] * masks[1 - h], kxs[h][...])

        def weigh(h, r):
            rows = aligned(r, R)
            top = jnp.max(scs[h][...], axis=-1, keepdims=True)
            total = jnp.zeros((R, PAIR), F32)
            got = jnp.zeros((R, PAIR), F32)
            for k in range(rows_all // R):
                keys = slice(k * R, (k + 1) * R)
                grown = jnp.exp(scs[h][:, keys] - top)
                for m in range(R // PAIR):
                    total = total + grown[:, m * PAIR : (m + 1) * PAIR]
                got = got + dot_nn(grown.astype(BF16), val[keys, cols])
            total = jnp.sum(total, axis=-1, keepdims=True)
            got = got * (1.0 / total)
            lane = lane_ids(R)
            if h == 0:
                att[rows, cols] = got
            else:
                att[rows, cols] = jnp.where(lane < HALF, att[rows, cols], got)
            lcol[rows, :] = jnp.where(lane == p * 2 + h, top + jnp.log(total), lcol[rows, :])

        scores(0, 0)

        def step(r):
            scores(1, r)
            weigh(0, r)
            scores(0, jnp.minimum(r + 1, blocks - 1))
            weigh(1, r)

        loop(blocks, step)

    loop(width_all // PAIR, heads)

    def turn(r):
        rows = aligned(r, PAIR)
        lse[:, rows] = jnp.transpose(lcol[rows, :])[: lse.shape[0], :]

    loop(rows_all // PAIR, turn)


PARTS = 16


def main_kernel(
    fuse, pairs, chunks,
    x_h, og_h, wp_h, we_h, wc_h, wq_h,
    grids, freqs, bias_q, *rest,
):
    (
    gain_one, shift_one, bias_p, gain_two, shift_two, bias_e, bias_c,
    mixed_h, pgrad_h, ff_h, pq_h, small_h, nf_h, cossin_h,
    att, q8, key, val, ohq, ohk, lse, pos, x, cot, wp, we, wc,
    acc_a, acc_b, xbuf, mid, cott, ns, nst, act, hgb, dgrad, delta,
    km, vm, kt, kmt, dk, dv, dqt, qkvg, cos, sin, sums,
    gf, gq, r1, r2, r3, small, small_r, sc0, sc1,
    lsem, xs, xr, credit, s1, e1, s2, e2, s3, e3, c1, c2, c3, ms, mr, osem, zs,
    ) = rest
    gain_one, shift_one, bias_p, gain_two, shift_two, bias_e, bias_c = (
        v[...].reshape(1, -1)
        for v in (gain_one, shift_one, bias_p, gain_two, shift_two, bias_e, bias_c)
    )
    me = lax.axis_index("dp")
    core = lax.axis_index("head")
    blocks = x.shape[0] // R
    subs = x.shape[0] // SUB
    mate = (me, 1 - core)
    if fuse:
        xx, yy, zz = me % 2, (me // 2) % 2, me // 4
        fst = xx * (1 - core) + yy * core
        snd = yy * (1 - core) + xx * core
        peer1 = (me + (1 - 2 * fst) * (1 + core), core)
        peer2 = (me + (1 - 2 * snd) * (2 - core), core)
        peers_z = [(((zz + j) % 4) * 4 + me % 4, core) for j in (1, 2, 3)]

        def where(z, f, s):
            return z * 4 + s * (2 - core) + f * (1 + core)

    def load(src, dst, i):
        copy = pltpu.make_async_copy(src, dst, lsem.at[i])
        copy.start()
        return copy

    heads = q8.shape[1]
    slots = grids.shape[1]
    get_x = load(x_h, x, 4)
    get_wq = [load(wq_h.at[k], we.at[:, pl.ds(k * heads, heads)], 7 + k) for k in range(3)]
    get_wp = load(wp_h, wp, 1)
    get_og = load(og_h, cot, 2)
    get_wc = load(wc_h, wc, 6)

    barrier = pltpu.get_barrier_semaphore()
    friends = [mate] + ([peer1, peer2] + peers_z if fuse else [])
    for friend in friends:
        pl.semaphore_signal(barrier, inc=1, device_id=friend, device_id_type=MESH)

    def exchange(src, r):
        return pltpu.make_async_remote_copy(
            src.at[aligned(r, R), :], xbuf.at[aligned(r, R), :], xs.at[r], xr.at[r],
            device_id=mate, device_id_type=MESH,
        )

    def send(src, r):
        exchange(src, r).start()

    def give_credit(r):
        pl.semaphore_signal(credit.at[r], inc=1, device_id=mate, device_id_type=MESH)

    def take_credit(r):
        pl.semaphore_wait(credit.at[r], 1)

    def remote(src, dst, ss, rs, peer):
        return pltpu.make_async_remote_copy(
            src, dst, ss, rs, device_id=peer, device_id_type=MESH
        )

    class Line:
        def __init__(self, grads, base, width, out, guard):
            self.g, self.base, self.n, self.out, self.guard = grads, base, width, out, guard

        def buf(self, buf, j, b):
            return buf.at[j, b, :, pl.ds(0, self.n)]

        def whole(self, buf, j):
            return buf.at[j, :, :, pl.ds(0, self.n)]

        def start1(self, j):
            if self.guard == "take":
                pl.semaphore_wait(c1.at[j], 1)

            def one(i):
                remote(
                    self.g.at[j, where(i // 2, 1 - fst, i % 2)], self.buf(r1, j, i),
                    s1.at[self.base + j], e1.at[self.base + j], peer1,
                ).start()

            loop(8, one)

        def give(self, sem, j, peers):
            if self.guard == "give":
                def go():
                    for peer in peers:
                        pl.semaphore_signal(sem.at[j], inc=1, device_id=peer, device_id_type=MESH)
                if isinstance(j, int):
                    if j < 4:
                        go()
                else:
                    pl.when(j < 4)(go)

        def finish1(self, j):
            remote(
                self.g.at[j, pl.ds(0, 8)], self.whole(r1, j),
                s1.at[self.base + j], e1.at[self.base + j], peer1,
            ).wait_recv()

            def one(i):
                b = where(i // 2, fst, i % 2)
                self.g[j, b] = self.g[j, b] + self.buf(r1, j, i)[...]

            loop(8, one)
            self.give(c1, j, [peer1])
            if self.guard == "take":
                pl.semaphore_wait(c2.at[j], 1)

            def two(i):
                remote(
                    self.g.at[j, where(i, fst, 1 - snd)], self.buf(r2, j, i),
                    s2.at[self.base + j], e2.at[self.base + j], peer2,
                ).start()

            loop(4, two)

        def finish2(self, j):
            remote(
                self.g.at[j, pl.ds(0, 4)], self.whole(r2, j),
                s2.at[self.base + j], e2.at[self.base + j], peer2,
            ).wait_recv()

            def one(i):
                b = where(i, fst, snd)
                self.g[j, b] = self.g[j, b] + self.buf(r2, j, i)[...]

            loop(4, one)
            self.give(c2, j, [peer2])
            if self.guard == "take":
                pl.semaphore_wait(c3.at[j], 3)
            for k in range(3):
                remote(
                    self.g.at[j, where((zz + k + 1) % 4, fst, snd)], self.buf(r3, j, k),
                    s3.at[self.base + j], e3.at[self.base + j], peers_z[k],
                ).start()

        def finish3(self, j):
            remote(
                self.g.at[j, pl.ds(0, 3)], self.whole(r3, j),
                s3.at[self.base + j], e3.at[self.base + j], peers_z[0],
            ).wait_recv()
            self.g[j, me] = (
                self.g[j, me]
                + self.buf(r3, j, 0)[...] + self.buf(r3, j, 1)[...] + self.buf(r3, j, 2)[...]
            )
            self.give(c3, j, peers_z)
            pltpu.make_async_copy(self.g.at[j, me], self.out.at[j], osem.at[self.base + j]).start()

        def drain(self, j):
            for src, dst, ss, rs, peer in (
                (self.g.at[j, pl.ds(0, 8)], self.whole(r1, j), s1, e1, peer1),
                (self.g.at[j, pl.ds(0, 4)], self.whole(r2, j), s2, e2, peer2),
                (self.g.at[j, pl.ds(0, 3)], self.whole(r3, j), s3, e3, peers_z[0]),
            ):
                remote(src, dst, ss.at[self.base + j], rs.at[self.base + j], peer).wait_send()
            pltpu.make_async_copy(self.g.at[j, me], self.out.at[j], osem.at[self.base + j]).wait()

    class Deep:
        def __init__(self, grads, j, out):
            self.g, self.j, self.out = grads, j, out

        def quarter(self, k):
            j = self.j
            src = self.g.at[j, pl.ds(((zz + k + 1) % 4) * 4, 4)]
            if k < 2:
                return remote(src, r1.at[j, pl.ds(4 * k, 4)], s1.at[j], e1.at[j], peers_z[k])
            return remote(src, r2.at[j], s2.at[j], e2.at[j], peers_z[k])

        def two(self):
            j = self.j
            return remote(self.g.at[j, pl.ds(0, 8)], r1.at[j], s1.at[j], e1.at[j], peers_z[0])

        def halves(self):
            j = self.j
            return remote(
                self.g.at[j, pl.ds(0, 2)], r3.at[j, pl.ds(0, 2)], s3.at[j], e3.at[j], peer1
            )

        def last(self):
            return remote(
                self.g.at[self.j, where(zz, fst, 1 - snd)], r3.at[self.j, 2], zs.at[0], zs.at[1],
                peer2,
            )

        def result(self):
            return pltpu.make_async_copy(
                self.g.at[self.j, me], self.out.at[self.j], osem.at[self.j]
            )

        def start(self):
            for k in range(3):
                self.quarter(k).start()

        def finish1(self):
            j = self.j
            self.two().wait_recv()
            self.quarter(2).wait_recv()

            def one(i):
                b = zz * 4 + i
                self.g[j, b] = self.g[j, b] + r1[j, i] + r1[j, 4 + i] + r2[j, i]

            loop(4, one)
            for s in range(2):
                remote(
                    self.g.at[j, where(zz, 1 - fst, s)], r3.at[j, s], s3.at[j], e3.at[j], peer1
                ).start()

        def finish2(self):
            j = self.j
            self.halves().wait_recv()
            for s in range(2):
                b = where(zz, fst, s)
                self.g[j, b] = self.g[j, b] + r3[j, s]
            self.last().start()

        def finish3(self):
            self.last().wait_recv()
            self.g[self.j, me] = self.g[self.j, me] + r3[self.j, 2]
            self.result().start()

        def drain(self):
            self.two().wait_send()
            self.quarter(2).wait_send()
            self.halves().wait_send()
            self.last().wait_send()
            self.result().wait()

    class Plain:
        def __init__(self, grads, base, width, out, guard):
            self.g, self.base, self.out = grads, base, out

        def copy(self, j):
            return pltpu.make_async_copy(self.g.at[j], self.out.at[j], osem.at[self.base + j])

        def start1(self, j):
            self.copy(j).start()

        def finish1(self, j):
            pass

        finish2 = finish3 = finish1

        def drain(self, j):
            self.copy(j).wait()

    kind = Line if fuse else Plain
    ff = kind(gf, 0, 2 * CHUNK, ff_h, "give")
    pq = kind(gq, chunks, 3 * PAIR, pq_h, "take")
    deep = Deep(gf, chunks - 1, ff_h)

    small[...] = jnp.zeros_like(small)
    sums[...] = jnp.zeros_like(sums)
    sums[7:8, :] = bias_e

    turns = []
    for axis in range(2):
        lines = [freqs[n, axis : axis + 1, :] for n in range(heads // HALF) for _ in range(2)]
        turns.append(jnp.concatenate(lines, axis=1))
    front_place(grids, slots, turns, ohq, ohk, acc_b, pos)
    get_x.wait()
    for copy in get_wq:
        copy.wait()
    front_rows(x, gain_one, shift_one, we, bias_q, q8, key, val, ns, acc_b)
    get_we = load(we_h, we, 5)
    put_nf = load(ns, nf_h, 10)
    put_cossin = load(acc_b.at[:, pl.ds(0, 2 * heads)], cossin_h, 11)
    front_heads(q8, key, val, ohq, ohk, att, lse, (km, vm), (sc0, sc1), dk)
    pl.semaphore_wait(barrier, len(friends))
    get_wp.wait()

    def project(r):
        acc_a[aligned(r, R), :] = dot_nn(att[aligned(r, R), :].astype(BF16), wp[...])
        send(acc_a, r)

    loop(blocks, project)

    get_og.wait()

    def mask_cot(r):
        rows = aligned(r, R)
        block = (cot[rows, :].astype(F32) * pos[rows, 0:1])
        small[0, 0:1, :] = small[0, 0:1, :] + jnp.sum(block, axis=0, keepdims=True)
        low = block.astype(BF16)
        cot[rows, :] = low
        cott[:, rows] = jnp.transpose(low)

    loop(blocks, mask_cot)
    put_nf.wait()
    put_cossin.wait()

    def second_norm(r):
        exchange(acc_a, r).wait()

        def sub(i):
            rows = pl.ds(pl.multiple_of(r * R + i * SUB, SUB), SUB)
            middle = x[rows, :].astype(F32) + ((acc_a[rows, :] + xbuf[rows, :]) + bias_p)
            unit, _ = unit_of(middle)
            mid[rows, :] = middle
            ns[rows, :] = (unit * gain_two + shift_two).astype(BF16)
            acc_b[rows, :] = 0.5 * (middle + bias_c)
            acc_a[rows, :] = jnp.zeros_like(middle)

        loop(R // SUB, sub)
        give_credit(r)
        nst[:, aligned(r, R)] = jnp.transpose(ns[aligned(r, R), :])

    loop(blocks, second_norm)
    get_we.wait()
    get_wc.wait()

    def feed(i):
        j = (i + chunks - 1) % chunks
        cols = aligned(j, CHUNK)

        def rows_of(r):
            rows = aligned(r, R)
            hidden = dot_nn(ns[rows, :], we[:, cols]) + sums[7:8, cols]
            upstream = dot_nt(cot[rows, :], wc[cols, :])
            phi = 0.5 * (1.0 + lax.erf(hidden * (0.5**0.5)))
            slope = phi + hidden * (jnp.exp(-0.5 * hidden * hidden) * (0.3989422804014327))
            active = (hidden * phi).astype(BF16)
            hgrad = (upstream * slope).astype(BF16)
            act[rows, :] = active
            hgb[rows, :] = hgrad
            sums[0:1, cols] = sums[0:1, cols] + jnp.sum(hgrad.astype(F32), axis=0, keepdims=True)
            acc_b[rows, :] = acc_b[rows, :] + dot_nn(active, wc[cols, :])
            acc_a[rows, :] = acc_a[rows, :] + dot_nt(hgrad, we[:, cols])

        loop(blocks, rows_of)
        got = dot_nn(cott[...], act[...])
        gf[j, :, :, pl.ds(0, CHUNK)] = got.reshape(gf.shape[1], gf.shape[2], CHUNK)
        got = dot_nn(nst[...], hgb[...])
        gf[j, :, :, pl.ds(CHUNK, CHUNK)] = got.reshape(gf.shape[1], gf.shape[2], CHUNK)
        if fuse:
            pl.when(i == 0)(deep.start)
            pl.when(i > 0)(lambda: ff.start1(j))
            pl.when(i == 4)(lambda: ff.finish1(0))
        else:
            ff.start1(j)

    loop(chunks, feed)

    def send_second(r):
        take_credit(r)
        send(acc_a, r)

    loop(blocks, send_second)
    get_nf = load(nf_h, ns, 0)
    ff.finish1(1)

    def second_back(r):
        exchange(acc_a, r).wait()

        def sub(i):
            rows = pl.ds(pl.multiple_of(r * R + i * SUB, SUB), SUB)
            up = acc_a[rows, :] + xbuf[rows, :]
            unit, inv = unit_of(mid[rows, :])
            small[0, 1:2, :] = small[0, 1:2, :] + jnp.sum(up * unit, axis=0, keepdims=True)
            small[0, 2:3, :] = small[0, 2:3, :] + jnp.sum(up, axis=0, keepdims=True)
            grad = cot[rows, :].astype(F32) + norm_back(up, unit, inv, gain_two)
            mid[rows, :] = grad
            low = grad.astype(BF16)
            cot[rows, :] = low
            small[0, 3:4, :] = small[0, 3:4, :] + jnp.sum(
                low.astype(F32), axis=0, keepdims=True
            )
            acc_a[rows, :] = jnp.zeros_like(up)

        loop(R // SUB, sub)
        give_credit(r)
        rows = aligned(r, R)
        cott[:, rows] = jnp.transpose(cot[rows, :])
        low = dot_nt(cot[rows, :], wp[...]).astype(BF16)
        dgrad[rows, :] = low
        prod = low.astype(F32) * att[rows, :]
        head = lax.broadcasted_iota(jnp.int32, (8, prod.shape[1]), 0)
        lane = lax.broadcasted_iota(jnp.int32, (8, prod.shape[1]), 1)
        pick = (lane // HALF == head).astype(F32)
        delta[:, rows] = lax.dot_general(
            pick, prod, (((1,), (1,)), ((), ())), precision=lax.Precision.HIGHEST,
            preferred_element_type=F32,
        )

    loop(blocks, second_back)
    ff.finish2(0)
    gq[0] = dot_nn(cott[...], att[...].astype(BF16)).reshape(gq.shape[1:])
    pq.start1(0)

    def send_mixed(r):
        take_credit(r)
        send(acc_b, r)

    loop(blocks, send_mixed)

    get_nf.wait()

    def turn_first(r):
        nst[:, aligned(r, R)] = jnp.transpose(ns[aligned(r, R), :])

    loop(blocks, turn_first)
    get_wq = [
        load(wq_h.at[k], we.at[:, pl.ds(k * pairs * PAIR, pairs * PAIR)], 4 + k) for k in range(3)
    ]
    kt[...] = jnp.transpose(key[...])

    def mixed_block(r):
        exchange(acc_b, r).wait()
        rows = aligned(r, R)
        ns[rows, :] = (acc_b[rows, :] + xbuf[rows, :]).astype(BF16)
        give_credit(r)
        pltpu.make_async_copy(ns.at[rows, :], mixed_h.at[rows, :], ms.at[r]).start()

    loop(blocks, mixed_block)
    for copy in get_wq:
        copy.wait()

    def pair_back(p):
        cols = aligned(p, PAIR)
        get_cos = load(cossin_h.at[:, cols], cos, 0)
        get_sin = load(cossin_h.at[:, aligned(pairs + p, PAIR)], sin, 1)
        dk[...] = jnp.zeros_like(dk)
        dv[...] = jnp.zeros_like(dv)
        dqt[...] = jnp.zeros_like(dqt)

        def head_back(h):
            mine = head_mask(h).astype(BF16)
            other = head_mask(1 - h).astype(BF16)
            km[...] = key[:, cols] * mine + ohk[...] * other
            vm[...] = val[:, cols] * mine
            spot = lax.broadcasted_iota(jnp.int32, (PAIR, 1), 0)
            kmt[...] = kt[cols, :] * (spot // HALF == h).astype(F32).astype(BF16)
            n = p * 2 + h

            def query_back(r):
                rows = aligned(r, R)
                qm = q8[rows, cols] * mine
                qx = qm + ohq[rows, :] * other
                do = dgrad[rows, cols]
                score = dot_nt(km[...], qx)
                prob = jnp.exp(score - lse[pl.ds(n, 1), rows])
                pgrad = dot_nt(vm[...], do)
                sgrad = (prob * (pgrad - delta[pl.ds(n, 1), rows])).astype(BF16)
                dv[...] = dv[...] + dot_nn(prob.astype(BF16), do * mine)
                dk[...] = dk[...] + dot_nn(sgrad, qm)
                dqt[:, rows] = dqt[:, rows] + dot_nn(kmt[...], sgrad)

            loop(blocks, query_back)
            if fuse:
                if h == 0:
                    ff.finish1(p + 2)
                    ff.finish2(p + 1)
                else:
                    pl.when(p == 0)(deep.finish1)
                    pl.when(p > 0)(lambda: ff.finish3(p - 1))

        head_back(0)
        head_back(1)
        get_cos.wait()
        get_sin.wait()

        def turn_back(r):
            rows = aligned(r, R)
            lane_first = lane_ids(R) % HALF < HALF // 2
            sign = jnp.where(lane_first, 1.0, -1.0)
            c, s = cos[rows, :], sin[rows, :]
            total = jnp.zeros((R, PAIR), F32)
            grads = []
            scale = HALF**-0.5
            for k, (grad, turned) in enumerate(
                (
                    (jnp.transpose(dqt[:, rows]) * scale, q8[rows, cols].astype(F32) * (1.0 / scale)),
                    (dk[rows, :], key[rows, cols].astype(F32)),
                )
            ):
                swapped = swap_halves(grad, lane_first) * sign
                total = total + swapped * turned
                grads.append((grad * c + swapped * s).astype(BF16))
            grads.append(dv[rows, :].astype(BF16))
            for k, low in enumerate(grads):
                qkvg[rows, k * PAIR : (k + 1) * PAIR] = low
                sums[k + 1 : k + 2, cols] = sums[k + 1 : k + 2, cols] + jnp.sum(
                    low.astype(F32), axis=0, keepdims=True
                )
            for k in range(2):
                sums[k + 4 : k + 5, cols] = sums[k + 4 : k + 5, cols] + jnp.sum(
                    total * pos[rows, k + 1 : k + 2], axis=0, keepdims=True
                )
            weight = jnp.concatenate(
                [we[:, aligned(k * pairs + p, PAIR)] for k in range(3)], axis=1
            )
            acc_a[rows, :] = acc_a[rows, :] + dot_nt(qkvg[rows, :], weight)

        loop(blocks, turn_back)
        gq[p + 1] = dot_nn(nst[...], qkvg[...]).reshape(gq.shape[1:])
        pq.start1(p + 1)

    loop(pairs, pair_back)

    def first_send(r):
        def sub(i):
            rows = pl.ds(pl.multiple_of(r * R + i * SUB, SUB), SUB)
            unit, _ = unit_of(x[rows, :].astype(F32))
            up = acc_a[rows, :]
            small[0, 6:7, :] = small[0, 6:7, :] + jnp.sum(up * unit, axis=0, keepdims=True)
            small[0, 7:8, :] = small[0, 7:8, :] + jnp.sum(up, axis=0, keepdims=True)

        take_credit(r)
        send(acc_a, r)
        loop(R // SUB, sub)

    loop(blocks, first_send)

    n = chunks * CHUNK // 2
    small[0, 4:5, :] = sums[0:1, 0:n]
    small[0, 5:6, :] = sums[0:1, n : 2 * n]
    m = pairs * PAIR
    for k in range(5):
        small[0, 8 + k : 9 + k, 0:m] = sums[1 + k : 2 + k, 0:m]

    def small_copy(i, k, peer):
        return remote(small.at[k], small_r.at[i], ms.at[4 + i], mr.at[i], peer)

    copy = small_copy(0, 0, mate)
    copy.start()
    if fuse:
        pq.finish1(0)
        deep.finish2()
        ff.finish2(4)
        ff.finish3(2)
    copy.wait()
    line = lax.broadcasted_iota(jnp.int32, small.shape[1:], 0)
    small[1] = small[0] + jnp.where((line == 6) | (line == 7), small_r[0], 0.0)
    if fuse:
        small_copy(1, 1, peer1).start()
    last = 4 if fuse else 1

    def first_back(r):
        exchange(acc_a, r).wait()

        def sub(i):
            rows = pl.ds(pl.multiple_of(r * R + i * SUB, SUB), SUB)
            unit, inv = unit_of(x[rows, :].astype(F32))
            up = acc_a[rows, :] + xbuf[rows, :]
            mid[rows, :] = mid[rows, :] + norm_back(up, unit, inv, gain_one)

        loop(R // SUB, sub)
        rows = aligned(r, R)
        pltpu.make_async_copy(mid.at[rows, :], pgrad_h.at[rows, :], xs.at[r]).start()

    loop(blocks, first_back)
    if fuse:
        pq.finish1(1)
        pq.finish2(0)
        ff.finish3(3)
        pq.finish1(2)
        pq.finish2(1)
        ff.finish3(4)
        deep.finish3()
        pq.finish3(0)
        pq.finish1(3)
        small_copy(1, 1, peer1).wait()
        small[2] = small[1] + small_r[1]
        small_copy(2, 2, peer2).start()
        pq.finish2(2)
        pq.finish3(1)
        small_copy(2, 2, peer2).wait()
        small[3] = small[2] + small_r[2]
        copies = [small_copy(3 + k, 3, peers_z[k]) for k in range(3)]
        for copy in copies:
            copy.start()
        pq.finish2(3)
        pq.finish3(2)
        for copy in copies:
            copy.wait()
        small[4] = small[3] + (small_r[3] + small_r[4] + small_r[5])
    out_small = pltpu.make_async_copy(small.at[last], small_h, lsem.at[0])
    out_small.start()
    if fuse:
        pq.finish3(3)
        deep.drain()
        loop(chunks - 1, ff.drain)
    else:
        loop(chunks, ff.drain)
    loop(pairs + 1, pq.drain)
    out_small.wait()

    def finish_out(r):
        rows = aligned(r, R)
        pltpu.make_async_copy(ns.at[rows, :], mixed_h.at[rows, :], ms.at[r]).wait()
        pltpu.make_async_copy(mid.at[rows, :], pgrad_h.at[rows, :], xs.at[r]).wait()

    loop(blocks, finish_out)


def main_call(fuse, parts, big, grids, freqs, bias_q, vectors):
    x, og, wp, we, wc, wq = big
    rows, width = x.shape
    heads = wq.shape[2]
    hidden = we.shape[1]
    pairs, chunks = heads // PAIR, hidden // CHUNK
    shape = jax.ShapeDtypeStruct
    part_rows = width // parts
    sent = parts if fuse else 0
    if fuse:
        ff_shape, pq_shape = (chunks, part_rows, 2 * CHUNK), (pairs + 1, part_rows, 3 * PAIR)
        grain = (parts, part_rows)
        slots = chunks
    else:
        ff_shape, pq_shape = (chunks, 1, width, 2 * CHUNK), (pairs + 1, 1, width, 3 * PAIR)
        grain = (1, width)
        slots = 1
    outs = [
        shape((rows, width), BF16), shape((rows, width), F32), shape(ff_shape, F32),
        shape(pq_shape, F32), shape((16, width), F32), shape((rows, width), BF16),
        shape((rows, 2 * heads), F32),
    ]
    any_spec = pl.BlockSpec(memory_space=ANY)
    vm_spec = pl.BlockSpec(memory_space=pltpu.VMEM)
    V = pltpu.VMEM
    DMA = pltpu.SemaphoreType.DMA
    REG = pltpu.SemaphoreType.REGULAR
    blocks = rows // R
    lines = chunks + pairs + 1
    recv = (lambda n: V((slots, n, part_rows, 2 * CHUNK), F32)) if fuse else (lambda n: V((1, 1, 8, PAIR), F32))
    scratch = [
        V((rows, heads), F32), V((rows, heads), BF16), V((rows, heads), BF16), V((rows, heads), BF16),
        V((rows, PAIR), BF16), V((rows, PAIR), BF16), V((8, rows), F32), V((rows, PAIR), F32),
        V((rows, width), BF16), V((rows, width), BF16), V((heads, width), BF16),
        V((width, hidden), BF16), V((hidden, width), BF16),
        V((rows, width), F32), V((rows, width), F32), V((rows, width), F32), V((rows, width), F32),
        V((width, rows), BF16), V((rows, width), BF16), V((width, rows), BF16),
        V((rows, CHUNK), BF16), V((rows, CHUNK), BF16), V((rows, heads), BF16), V((8, rows), F32),
        V((rows, PAIR), BF16), V((rows, PAIR), BF16), V((heads, rows), BF16), V((PAIR, rows), BF16),
        V((rows, PAIR), F32), V((rows, PAIR), F32), V((PAIR, rows), F32), V((rows, 3 * PAIR), BF16),
        V((rows, PAIR), F32), V((rows, PAIR), F32), V((8, hidden), F32),
        V((chunks, *grain, 2 * CHUNK), F32), V((pairs + 1, *grain, 3 * PAIR), F32),
        recv(8), recv(4), recv(3), V((5, 16, width), F32), V((6, 16, width), F32),
        V((R, rows), F32), V((R, rows), F32),
        DMA((16,)), DMA((blocks,)), DMA((blocks,)), REG((blocks,)),
        DMA((lines,)), DMA((lines,)), DMA((lines,)), DMA((lines,)), DMA((lines,)), DMA((lines,)),
        REG((4,)), REG((4,)), REG((4,)), DMA((10,)), DMA((6,)), DMA((lines,)), DMA((2,)),
    ]
    return pl.pallas_call(
        partial(main_kernel, fuse, pairs, chunks),
        name="main",
        out_shape=outs,
        in_specs=[any_spec] * len(big)
        + [pl.BlockSpec(memory_space=pltpu.SMEM)]
        + [vm_spec] * (2 + len(vectors)),
        out_specs=[any_spec] * len(outs),
        scratch_shapes=scratch,
        compiler_params=pltpu.CompilerParams(
            collective_id=0, has_side_effects=True, vmem_limit_bytes=67043328
        ),
    )(*big, grids, freqs, bias_q, *vectors)


def finish_kernel(
    mixed_h, pgrad_h, ff_h, pq_h, small_h,
    mixed_o, pgrad_o, qkv_o, proj_o, expand_o, contract_o,
    gain_one, shift_one, bias_q, rope, bias_p, gain_two, shift_two, bias_e, bias_c,
    mixed, pgrad, ff, pq, small, isem, osem,
):
    blocks = mixed.shape[0] // R
    chunks, pairs = ff.shape[0], pq.shape[0] - 1
    jobs = [(small_h, small, [])]
    for src, buf, dst in ((pgrad_h, pgrad, pgrad_o), (mixed_h, mixed, mixed_o)):
        for r in range(blocks):
            part = (pl.ds(r * R, R), slice(None))
            jobs.append((src.at[part], buf.at[part], [(buf.at[part], dst.at[part])]))
    for j in range(chunks):
        cols = pl.ds(j * CHUNK, CHUNK)
        jobs.append((ff_h.at[j], ff.at[j], [
            (ff.at[j, :, pl.ds(0, CHUNK)], contract_o.at[:, cols]),
            (ff.at[j, :, pl.ds(CHUNK, CHUNK)], expand_o.at[:, cols]),
        ]))
    jobs.append((pq_h.at[0], pq.at[0], [(pq.at[0], proj_o)]))
    for p in range(pairs):
        jobs.append((pq_h.at[p + 1], pq.at[p + 1], [
            (pq.at[p + 1, :, pl.ds(k * PAIR, PAIR)], qkv_o.at[k, :, pl.ds(p * PAIR, PAIR)])
            for k in range(3)
        ]))
    gets = [pltpu.make_async_copy(a, b, isem.at[i]) for i, (a, b, _) in enumerate(jobs)]
    for get in gets:
        get.start()
    puts = []
    for get, (_, _, todo) in zip(gets, jobs):
        get.wait()
        for a, b in todo:
            puts.append(pltpu.make_async_copy(a, b, osem.at[len(puts)]))
            puts[-1].start()
    heads = bias_q.shape[1]
    for k, out in (
        (6, gain_one), (7, shift_one), (3, bias_p), (1, gain_two), (2, shift_two), (0, bias_c),
    ):
        out[...] = small[k, :]
    half = bias_e.shape[0] // 2
    bias_e[:half] = small[4, :half]
    bias_e[half:] = small[5, :half]
    bias_q[...] = small[8:11, :heads]
    for p in range(pairs):
        tile = small[8:16, p * PAIR : (p + 1) * PAIR]
        both = tile + pltpu.roll(tile, PAIR - HALF // 2, 1)
        rope[2 * p] = both[3:5, : HALF // 2]
        rope[2 * p + 1] = pltpu.roll(both, HALF, 1)[3:5, : HALF // 2]
    for put in puts:
        put.wait()


def finish(mixed, pgrad, ff, pq, small, hidden):
    rows, width = mixed.shape
    mine = ff.shape[1]
    heads = pq.shape[2]
    shape = lambda *s: jax.ShapeDtypeStruct(s, F32)
    outs = [
        jax.ShapeDtypeStruct((rows, width), BF16), shape(rows, width), shape(3, mine, heads),
        shape(mine, heads), shape(mine, hidden), shape(mine, hidden), shape(width), shape(width),
        shape(3, heads), shape(heads // HALF, 2, HALF // 2), shape(width), shape(width),
        shape(width), shape(hidden), shape(width),
    ]
    any_spec = pl.BlockSpec(memory_space=ANY)
    vm_spec = pl.BlockSpec(memory_space=pltpu.VMEM)
    reads = 1 + 2 * (rows // R) + ff.shape[0] + pq.shape[0]
    writes = 2 * (rows // R) + 2 * ff.shape[0] + 3 * pq.shape[0] - 2
    big = (mixed, pgrad, ff, pq, small)
    return pl.pallas_call(
        finish_kernel,
        name="finish",
        out_shape=outs,
        in_specs=[any_spec] * 5,
        out_specs=[any_spec] * 6 + [vm_spec] * (len(outs) - 6),
        scratch_shapes=[pltpu.VMEM(v.shape, v.dtype) for v in big]
        + [pltpu.SemaphoreType.DMA((reads,)), pltpu.SemaphoreType.DMA((writes,))],
        compiler_params=pltpu.CompilerParams(vmem_limit_bytes=67043328),
    )(*big)


def body(
    fuse, parts,
    patches, image_grids, out_grad, first_gain, first_shift, qkv_weight, qkv_bias, rope_freqs,
    proj_weight, proj_bias, second_gain, second_shift, expand_weight, expand_bias,
    contract_weight, contract_bias,
):
    width = patches.shape[1]
    mixed, pgrad, ff, pq, small, _, _ = main_call(
        fuse,
        parts,
        (patches, out_grad, proj_weight, expand_weight, contract_weight, qkv_weight),
        image_grids.T,
        rope_freqs.transpose(1, 0, 2),
        qkv_bias,
        (first_gain, first_shift, proj_bias, second_gain, second_shift, expand_bias, contract_bias),
    )
    if not fuse:
        scatter = partial(lax.psum_scatter, axis_name="dp", scatter_dimension=1, tiled=True)
        ff = scatter(ff.reshape(ff.shape[0], width, ff.shape[-1]))
        pq = scatter(pq.reshape(pq.shape[0], width, pq.shape[-1]))
        small = lax.psum(small, "dp")
    (
        mixed, pgrad, qkv, proj, expand, contract, gain_one, shift_one, bias_q, rope,
        bias_p, gain_two, shift_two, bias_e, bias_c,
    ) = finish(mixed, pgrad, ff, pq, small, expand_bias.shape[0])
    return (
        mixed, pgrad, qkv, proj.T, expand, contract.T, gain_one, shift_one, bias_q,
        rope.transpose(1, 0, 2), bias_p, gain_two, shift_two, bias_e, bias_c,
    )


def solution(mesh):
    in_specs = (
        P("dp", None), P("dp", None), P("dp", None), P(), P(), P(None, None, "head"),
        P(None, "head"), P(None, "head", None), P("head", None), P(), P(), P(),
        P(None, "head"), P("head"), P("head", None), P(),
    )
    out_specs = (
        P("dp", None), P("dp", None), P(None, "dp", "head"), P("head", "dp"), P("dp", "head"),
        P("head", "dp"), P(), P(), P(None, "head"), P(None, "head", None), P(), P(), P(),
        P("head"), P(),
    )
    parts = mesh.shape["dp"]
    run = partial(body, parts == PARTS, parts)
    return jax.shard_map(run, mesh=mesh, in_specs=in_specs, out_specs=out_specs, check_vma=False)
```

```python
from functools import partial

import jax
import jax.numpy as jnp
from jax import lax
from jax.experimental import pallas as pl
from jax.experimental.pallas import tpu as pltpu
from jax.sharding import PartitionSpec as P

F32 = jnp.float32
BF16 = jnp.bfloat16
EPS = 1e-06
FAR = 2.0**100
R = 256
QR = 512
SUB = 64
PAIR = 128
HALF = 64
CHUNK = 256
MESH = pl.DeviceIdType.MESH
ANY = pl.ANY


def dot_nn(a, b):
    return lax.dot_general(a, b, (((1,), (0,)), ((), ())), preferred_element_type=F32)


def dot_nt(a, b):
    return lax.dot_general(a, b, (((1,), (1,)), ((), ())), preferred_element_type=F32)


def aligned(i, size):
    return pl.ds(pl.multiple_of(i * size, size), size)


def loop(count, fn):
    def step(i, carry):
        fn(i)
        return carry

    lax.fori_loop(0, count, step, 0)


def unit_of(rows):
    centred = rows - jnp.mean(rows, axis=-1, keepdims=True)
    inv = lax.rsqrt(jnp.mean(centred * centred, axis=-1, keepdims=True) + EPS)
    return centred * inv, inv


def norm_back(upstream, unit, inv, gain):
    scaled = upstream * gain
    return inv * (
        scaled
        - jnp.mean(scaled, axis=-1, keepdims=True)
        - unit * jnp.mean(scaled * unit, axis=-1, keepdims=True)
    )


def swap_halves(v, lane_first):
    return jnp.where(lane_first, pltpu.roll(v, PAIR - HALF // 2, 1), pltpu.roll(v, HALF // 2, 1))


def lane_ids(rows):
    return lax.broadcasted_iota(jnp.int32, (rows, PAIR), 1)


def head_mask(h):
    lane = lax.broadcasted_iota(jnp.int32, (1, PAIR), 1)
    return (lane // HALF == h).astype(F32)


def pieces(table):
    high = table.astype(BF16)
    rest = table - high.astype(F32)
    mid = rest.astype(BF16)
    low = (rest - mid.astype(F32)).astype(BF16)
    return jnp.concatenate([high, mid, low], axis=0)


def front_place(grids, slots, freqs, ohq, ohk, cossin, pos):
    rows_all, width_all = pos.shape[0], freqs[0].shape[1]
    side = lax.broadcasted_iota(jnp.int32, (32, 1), 0).astype(F32)
    ang_r = side * freqs[0]
    ang_c = side * freqs[1]
    table_r = pieces(jnp.concatenate([jnp.cos(ang_r), jnp.sin(ang_r)], axis=1))
    table_c = pieces(jnp.concatenate([jnp.cos(ang_c), jnp.sin(ang_c)], axis=1))

    def place(r):
        rows = aligned(r, 256)
        t = lax.broadcasted_iota(jnp.int32, (256, 1), 0) + r * 256
        seg = jnp.zeros((256, 1), jnp.int32)
        start = jnp.zeros((256, 1), jnp.int32)
        width = jnp.ones((256, 1), jnp.int32)
        end = jnp.int32(0)
        for s in range(slots):
            begun = t >= end
            start = jnp.where(begun, end, start)
            width = jnp.where(begun, jnp.maximum(grids[1, s], 1), width)
            end = end + grids[0, s] * grids[1, s]
            seg = jnp.where(t >= end, s + 1, seg)
        real = (seg < slots).astype(F32)
        off = (t - start).astype(F32)
        wide = width.astype(F32)
        grow = jnp.floor((off + 0.5) / wide) * real
        gcol = (off - grow * wide) * real
        lane = lane_ids(256)
        pos[rows, :] = jnp.where(lane == 0, real, jnp.where(lane == 1, grow, gcol))
        hot = lane % HALF == seg
        ohq[rows, :] = jnp.where(hot, 1.0, 0.0).astype(BF16)
        ohk[rows, :] = jnp.where(hot, 0.0, -FAR).astype(BF16)
        spot = (lax.broadcasted_iota(jnp.int32, (256, 96), 1) % 32).astype(F32)
        got_r = dot_nn(jnp.where(spot == grow, 1.0, 0.0).astype(BF16), table_r)
        got_c = dot_nn(jnp.where(spot == gcol, 1.0, 0.0).astype(BF16), table_c)
        cr, sr = got_r[:, :width_all], got_r[:, width_all:]
        cc, sc = got_c[:, :width_all], got_c[:, width_all:]
        cossin[rows, :width_all] = cr * cc - sr * sc
        cossin[rows, width_all:] = sr * cc + cr * sc

    loop(rows_all // 256, place)


def front_rows(x, gain, shift, w, b, q8, key, val, nf, cossin):
    rows_all, width_all = q8.shape
    pairs = width_all // PAIR

    def norm(r):
        rows = aligned(r, SUB)
        unit, _ = unit_of(x[rows, :].astype(F32))
        nf[rows, :] = (unit * gain + shift).astype(BF16)

    loop(rows_all // SUB, norm)

    def project(r):
        rows = aligned(r, R)
        lane_first = lane_ids(R) % HALF < HALF // 2
        sign = jnp.where(lane_first, -1.0, 1.0)
        for k, out in ((0, q8), (1, key)):
            got = dot_nn(nf[rows, :], w[:, k * width_all : (k + 1) * width_all]) + b[k : k + 1, :]
            for p in range(pairs):
                cols = slice(p * PAIR, (p + 1) * PAIR)
                part = got[:, cols]
                turned = part * cossin[rows, cols] + swap_halves(part, lane_first) * (
                    cossin[rows, width_all + p * PAIR : width_all + (p + 1) * PAIR] * sign
                )
                turned = turned.astype(BF16)
                if k == 0:
                    turned = turned * jnp.asarray(HALF**-0.5, BF16)
                out[rows, cols] = turned
        got = dot_nn(nf[rows, :], w[:, 2 * width_all : 3 * width_all])
        val[rows, :] = (got + b[2:3, :]).astype(BF16)

    loop(rows_all // R, project)


def front_heads(q8, key, val, ohq, ohk, att, kxs, scs, lcol):
    rows_all, width_all = q8.shape
    blocks, pieces_all, wide = rows_all // QR, rows_all // R, scs[0].shape[1] // R
    masks = [head_mask(h).astype(BF16) for h in range(2)]

    def piece(h, k):
        at = (k // wide) * QR
        return scs[h].at[at : at + QR, (k % wide) * R : (k % wide + 1) * R]

    def heads(p):
        cols = aligned(p, PAIR)
        for h in range(2):
            kxs[h][...] = key[:, cols] * masks[h] + ohk[...] * masks[1 - h]

        def scores(h, r):
            rows = aligned(r, QR)
            qx = q8[rows, cols] * masks[h] + ohq[rows, :] * masks[1 - h]
            for k in range(pieces_all):
                piece(h, k)[...] = dot_nt(qx, kxs[h][k * R : (k + 1) * R, :])

        def weigh(h, r):
            rows = aligned(r, QR)
            top = piece(h, 0)[...]
            for k in range(1, pieces_all):
                top = jnp.maximum(top, piece(h, k)[...])
            top = jnp.max(top, axis=-1, keepdims=True)
            total = jnp.zeros((QR, PAIR), F32)
            got = jnp.zeros((QR, PAIR), F32)
            for k in range(pieces_all):
                grown = jnp.exp(piece(h, k)[...] - top)
                for m in range(R // PAIR):
                    total = total + grown[:, m * PAIR : (m + 1) * PAIR]
                got = got + dot_nn(grown.astype(BF16), val[k * R : (k + 1) * R, cols])
            total = jnp.sum(total, axis=-1, keepdims=True)
            got = got * (1.0 / total)
            lane = lane_ids(QR)
            if h == 0:
                att[rows, cols] = got
            else:
                att[rows, cols] = jnp.where(lane < HALF, att[rows, cols], got)
            lcol[rows, :] = jnp.where(lane == p * 2 + h, top + jnp.log(total), lcol[rows, :])

        scores(0, 0)

        def step(r):
            scores(1, r)
            weigh(0, r)
            scores(0, jnp.minimum(r + 1, blocks - 1))
            weigh(1, r)

        loop(blocks, step)

    loop(width_all // PAIR, heads)


PARTS = 16


def main_kernel(
    fuse, pairs, chunks,
    x_h, og_h, wp_h, we_h, wc_h, wq_h,
    grids, freqs, bias_q, *rest,
):
    (
    gain_one, shift_one, bias_p, gain_two, shift_two, bias_e, bias_c,
    mixed_h, pgrad_h, ff_h, pq_h, small_h, nf_h, cossin_h,
    att, q8, key, val, ohq, ohk, lse, pos, x, cot, wp, we, wc,
    acc_a, acc_b, xbuf, mid, cott, ns, nst, act, hgb, dgrad, delta,
    km, vm, kt, kmt, dk, dv, dqt, qkvg, cos, sin, sums,
    gf, gq, r1, r2, r3, small, small_r,
    lsem, xs, xr, credit, s1, e1, s2, e2, s3, e3, c1, c2, c3, ms, mr, osem, zs,
    ) = rest
    gain_one, shift_one, bias_p, gain_two, shift_two, bias_e, bias_c = (
        v[...].reshape(1, -1)
        for v in (gain_one, shift_one, bias_p, gain_two, shift_two, bias_e, bias_c)
    )
    me = lax.axis_index("dp")
    core = lax.axis_index("head")
    blocks = x.shape[0] // R
    subs = x.shape[0] // SUB
    mate = (me, 1 - core)
    if fuse:
        xx, yy, zz = me % 2, (me // 2) % 2, me // 4
        fst = xx * (1 - core) + yy * core
        snd = yy * (1 - core) + xx * core
        peer1 = (me + (1 - 2 * fst) * (1 + core), core)
        peer2 = (me + (1 - 2 * snd) * (2 - core), core)
        peers_z = [(((zz + j) % 4) * 4 + me % 4, core) for j in (1, 2, 3)]

        def where(z, f, s):
            return z * 4 + s * (2 - core) + f * (1 + core)

    def load(src, dst, i):
        copy = pltpu.make_async_copy(src, dst, lsem.at[i])
        copy.start()
        return copy

    heads = q8.shape[1]
    slots = grids.shape[1]
    get_x = load(x_h, x, 4)
    get_wq = [load(wq_h.at[k], we.at[:, pl.ds(k * heads, heads)], 7 + k) for k in range(3)]
    get_wp = load(wp_h, wp, 1)
    get_og = load(og_h, cot, 2)
    get_wc = load(wc_h, wc, 6)

    barrier = pltpu.get_barrier_semaphore()
    friends = [mate] + ([peer1, peer2] + peers_z if fuse else [])
    for friend in friends:
        pl.semaphore_signal(barrier, inc=1, device_id=friend, device_id_type=MESH)

    def exchange(src, r):
        return pltpu.make_async_remote_copy(
            src.at[aligned(r, R), :], xbuf.at[aligned(r, R), :], xs.at[r], xr.at[r],
            device_id=mate, device_id_type=MESH,
        )

    def send(src, r):
        exchange(src, r).start()

    def give_credit(r):
        pl.semaphore_signal(credit.at[r], inc=1, device_id=mate, device_id_type=MESH)

    def take_credit(r):
        pl.semaphore_wait(credit.at[r], 1)

    def remote(src, dst, ss, rs, peer):
        return pltpu.make_async_remote_copy(
            src, dst, ss, rs, device_id=peer, device_id_type=MESH
        )

    class Line:
        def __init__(self, grads, base, width, out, guard, parts):
            self.g, self.base, self.out, self.guard = grads, base, out, guard
            self.n, self.parts = width // parts, parts

        def cols(self, k):
            return pl.ds(k * self.n, self.n)

        def at(self, j, k):
            return self.base + j * self.parts + k

        def step(self, j, k, first, src, dst, ss, rs, peer):
            i = self.at(j, k)
            return remote(
                self.g.at[j, src, :, self.cols(k)], first.at[j, dst, :, self.cols(k)],
                ss.at[i], rs.at[i], peer,
            )

        def whole(self, j, k, n, ss, rs, buf, peer):
            return self.step(j, k, buf, pl.ds(0, n), pl.ds(0, n), ss, rs, peer)

        def add(self, j, k, b, got):
            c = self.cols(k)
            self.g[j, b, :, c] = self.g[j, b, :, c] + got

        def start1(self, j):
            if self.guard == "take":
                pl.semaphore_wait(c1.at[j], 1)
            for k in range(self.parts):

                def one(i, k=k):
                    b = where(i // 2, 1 - fst, i % 2)
                    self.step(j, k, r1, b, i, s1, e1, peer1).start()

                loop(8, one)

        def give(self, sem, j, peers):
            if self.guard == "give":
                def go():
                    for peer in peers:
                        pl.semaphore_signal(sem.at[j], inc=1, device_id=peer, device_id_type=MESH)
                if isinstance(j, int):
                    if j < 4:
                        go()
                else:
                    pl.when(j < 4)(go)

        def finish1(self, j, k=0):
            self.whole(j, k, 8, s1, e1, r1, peer1).wait_recv()
            c = self.cols(k)

            def one(i):
                self.add(j, k, where(i // 2, fst, i % 2), r1[j, i, :, c])

            loop(8, one)
            self.give(c1, j, [peer1])
            if self.guard == "take" and k == 0:
                pl.semaphore_wait(c2.at[j], 1)

            def two(i):
                self.step(j, k, r2, where(i, fst, 1 - snd), i, s2, e2, peer2).start()

            loop(4, two)

        def finish2(self, j, k=0):
            self.whole(j, k, 4, s2, e2, r2, peer2).wait_recv()
            c = self.cols(k)

            def one(i):
                self.add(j, k, where(i, fst, snd), r2[j, i, :, c])

            loop(4, one)
            self.give(c2, j, [peer2])
            if self.guard == "take" and k == 0:
                pl.semaphore_wait(c3.at[j], 3)
            for m in range(3):
                b = where((zz + m + 1) % 4, fst, snd)
                self.step(j, k, r3, b, m, s3, e3, peers_z[m]).start()

        def result(self, j, k):
            c = self.cols(k)
            return pltpu.make_async_copy(
                self.g.at[j, me, :, c], self.out.at[j, :, c], osem.at[self.at(j, k)]
            )

        def finish3(self, j, k=0):
            self.whole(j, k, 3, s3, e3, r3, peers_z[0]).wait_recv()
            c = self.cols(k)
            self.add(j, k, me, r3[j, 0, :, c] + r3[j, 1, :, c] + r3[j, 2, :, c])
            self.give(c3, j, peers_z)
            self.result(j, k).start()

        def drain(self, j):
            for k in range(self.parts):
                self.whole(j, k, 8, s1, e1, r1, peer1).wait_send()
                self.whole(j, k, 4, s2, e2, r2, peer2).wait_send()
                self.whole(j, k, 3, s3, e3, r3, peers_z[0]).wait_send()
                self.result(j, k).wait()

    class Deep:
        def __init__(self, grads, j, out):
            self.g, self.j, self.out = grads, j, out

        def quarter(self, k):
            j = self.j
            src = self.g.at[j, pl.ds(((zz + k + 1) % 4) * 4, 4)]
            if k < 2:
                return remote(src, r1.at[j, pl.ds(4 * k, 4)], s1.at[j], e1.at[j], peers_z[k])
            return remote(src, r2.at[j], s2.at[j], e2.at[j], peers_z[k])

        def two(self):
            j = self.j
            return remote(self.g.at[j, pl.ds(0, 8)], r1.at[j], s1.at[j], e1.at[j], peers_z[0])

        def halves(self):
            j = self.j
            return remote(
                self.g.at[j, pl.ds(0, 2)], r3.at[j, pl.ds(0, 2)], s3.at[j], e3.at[j], peer1
            )

        def last(self):
            return remote(
                self.g.at[self.j, where(zz, fst, 1 - snd)], r3.at[self.j, 2], zs.at[0], zs.at[1],
                peer2,
            )

        def result(self):
            return pltpu.make_async_copy(
                self.g.at[self.j, me], self.out.at[self.j], osem.at[self.j]
            )

        def start(self):
            for k in range(3):
                self.quarter(k).start()

        def finish1(self):
            j = self.j
            self.two().wait_recv()
            self.quarter(2).wait_recv()

            def one(i):
                b = zz * 4 + i
                self.g[j, b] = self.g[j, b] + r1[j, i] + r1[j, 4 + i] + r2[j, i]

            loop(4, one)
            for s in range(2):
                remote(
                    self.g.at[j, where(zz, 1 - fst, s)], r3.at[j, s], s3.at[j], e3.at[j], peer1
                ).start()

        def finish2(self):
            j = self.j
            self.halves().wait_recv()
            for s in range(2):
                b = where(zz, fst, s)
                self.g[j, b] = self.g[j, b] + r3[j, s]
            self.last().start()

        def finish3(self):
            self.last().wait_recv()
            self.g[self.j, me] = self.g[self.j, me] + r3[self.j, 2]
            self.result().start()

        def drain(self):
            self.two().wait_send()
            self.quarter(2).wait_send()
            self.halves().wait_send()
            self.last().wait_send()
            self.result().wait()

    class Plain:
        def __init__(self, grads, base, width, out, guard, parts):
            self.g, self.base, self.out = grads, base, out

        def copy(self, j):
            return pltpu.make_async_copy(self.g.at[j], self.out.at[j], osem.at[self.base + j])

        def start1(self, j):
            self.copy(j).start()

        def finish1(self, j):
            pass

        finish2 = finish3 = finish1

        def drain(self, j):
            self.copy(j).wait()

    kind = Line if fuse else Plain
    ff = kind(gf, 0, 2 * CHUNK, ff_h, "give", 1)
    pq = kind(gq, chunks, 3 * PAIR, pq_h, "take", 3)
    deep = Deep(gf, chunks - 1, ff_h)

    small[...] = jnp.zeros_like(small)
    sums[...] = jnp.zeros_like(sums)
    sums[7:8, :] = bias_e

    turns = []
    for axis in range(2):
        lines = [freqs[n, axis : axis + 1, :] for n in range(heads // HALF) for _ in range(2)]
        turns.append(jnp.concatenate(lines, axis=1))
    front_place(grids, slots, turns, ohq, ohk, acc_b, pos)
    get_x.wait()
    for copy in get_wq:
        copy.wait()
    front_rows(x, gain_one, shift_one, we, bias_q, q8, key, val, ns, acc_b)
    get_we = load(we_h, we, 5)
    put_nf = load(ns, nf_h, 10)
    put_cossin = load(acc_b.at[:, pl.ds(0, 2 * heads)], cossin_h, 11)
    front_heads(q8, key, val, ohq, ohk, att, (km, vm), (acc_a, mid), dk)
    pl.semaphore_wait(barrier, len(friends))
    get_wp.wait()

    def project(r):
        acc_a[aligned(r, R), :] = dot_nn(att[aligned(r, R), :].astype(BF16), wp[...])
        send(acc_a, r)

    loop(blocks, project)

    def turn(r):
        rows = aligned(r, PAIR)
        lse[:, rows] = jnp.transpose(dk[rows, :])[: lse.shape[0], :]

    loop(x.shape[0] // PAIR, turn)

    get_og.wait()

    def mask_cot(r):
        rows = aligned(r, R)
        block = (cot[rows, :].astype(F32) * pos[rows, 0:1])
        small[0, 0:1, :] = small[0, 0:1, :] + jnp.sum(block, axis=0, keepdims=True)
        low = block.astype(BF16)
        cot[rows, :] = low
        cott[:, rows] = jnp.transpose(low)

    loop(blocks, mask_cot)
    put_nf.wait()
    put_cossin.wait()

    def second_norm(r):
        exchange(acc_a, r).wait()

        def sub(i):
            rows = pl.ds(pl.multiple_of(r * R + i * SUB, SUB), SUB)
            middle = x[rows, :].astype(F32) + ((acc_a[rows, :] + xbuf[rows, :]) + bias_p)
            unit, _ = unit_of(middle)
            mid[rows, :] = middle
            ns[rows, :] = (unit * gain_two + shift_two).astype(BF16)
            acc_b[rows, :] = 0.5 * (middle + bias_c)
            acc_a[rows, :] = jnp.zeros_like(middle)

        loop(R // SUB, sub)
        give_credit(r)
        nst[:, aligned(r, R)] = jnp.transpose(ns[aligned(r, R), :])

    loop(blocks, second_norm)
    get_we.wait()
    get_wc.wait()

    def feed(i):
        none, one = 1 - (i + chunks - 1) // chunks, 1 - (i + chunks - 2) // chunks
        j = i - 1 + none + (chunks - 1) * (one - none)
        cols = aligned(j, CHUNK)

        def rows_of(r):
            rows = aligned(r, R)
            hidden = dot_nn(ns[rows, :], we[:, cols]) + sums[7:8, cols]
            upstream = dot_nt(cot[rows, :], wc[cols, :])
            phi = 0.5 * (1.0 + lax.erf(hidden * (0.5**0.5)))
            slope = phi + hidden * (jnp.exp(-0.5 * hidden * hidden) * (0.3989422804014327))
            active = (hidden * phi).astype(BF16)
            hgrad = (upstream * slope).astype(BF16)
            act[rows, :] = active
            hgb[rows, :] = hgrad
            sums[0:1, cols] = sums[0:1, cols] + jnp.sum(hgrad.astype(F32), axis=0, keepdims=True)
            acc_b[rows, :] = acc_b[rows, :] + dot_nn(active, wc[cols, :])
            acc_a[rows, :] = acc_a[rows, :] + dot_nt(hgrad, we[:, cols])

        loop(blocks, rows_of)
        got = dot_nn(cott[...], act[...])
        gf[j, :, :, pl.ds(0, CHUNK)] = got.reshape(gf.shape[1], gf.shape[2], CHUNK)
        got = dot_nn(nst[...], hgb[...])
        gf[j, :, :, pl.ds(CHUNK, CHUNK)] = got.reshape(gf.shape[1], gf.shape[2], CHUNK)
        if fuse:
            pl.when(i == 1)(deep.start)
            pl.when(i != 1)(lambda: ff.start1(j))
            pl.when(i == 4)(lambda: ff.finish1(0))
        else:
            ff.start1(j)

    loop(chunks, feed)

    def send_second(r):
        take_credit(r)
        send(acc_a, r)

    loop(blocks, send_second)
    get_nf = load(nf_h, ns, 0)
    ff.finish1(1)

    def second_back(r):
        exchange(acc_a, r).wait()

        def sub(i):
            rows = pl.ds(pl.multiple_of(r * R + i * SUB, SUB), SUB)
            up = acc_a[rows, :] + xbuf[rows, :]
            unit, inv = unit_of(mid[rows, :])
            small[0, 1:2, :] = small[0, 1:2, :] + jnp.sum(up * unit, axis=0, keepdims=True)
            small[0, 2:3, :] = small[0, 2:3, :] + jnp.sum(up, axis=0, keepdims=True)
            grad = cot[rows, :].astype(F32) + norm_back(up, unit, inv, gain_two)
            mid[rows, :] = grad
            low = grad.astype(BF16)
            cot[rows, :] = low
            small[0, 3:4, :] = small[0, 3:4, :] + jnp.sum(
                low.astype(F32), axis=0, keepdims=True
            )
            acc_a[rows, :] = jnp.zeros_like(up)

        loop(R // SUB, sub)
        give_credit(r)
        rows = aligned(r, R)
        cott[:, rows] = jnp.transpose(cot[rows, :])
        low = dot_nt(cot[rows, :], wp[...]).astype(BF16)
        dgrad[rows, :] = low
        prod = low.astype(F32) * att[rows, :]
        head = lax.broadcasted_iota(jnp.int32, (8, prod.shape[1]), 0)
        lane = lax.broadcasted_iota(jnp.int32, (8, prod.shape[1]), 1)
        pick = (lane // HALF == head).astype(F32)
        delta[:, rows] = lax.dot_general(
            pick, prod, (((1,), (1,)), ((), ())), precision=lax.Precision.HIGHEST,
            preferred_element_type=F32,
        )

    loop(blocks, second_back)
    ff.finish2(0)

    def small_copy(i, k, peer, late=1):
        rows = pl.ds(8 * late, 8)
        return remote(
            small.at[k, rows], small_r.at[i, rows], ms.at[4 + 6 * late + i], mr.at[6 * late + i],
            peer,
        )

    early, late = slice(0, 8), slice(8, 16)
    n = chunks * CHUNK // 2
    small[0, 4:5, :] = sums[0:1, 0:n]
    small[0, 5:6, :] = sums[0:1, n : 2 * n]
    small[1, early] = small[0, early]

    def early_one():
        small_copy(1, 1, peer1, 0).wait()
        small[2, early] = small[1, early] + small_r[1, early]
        small_copy(2, 2, peer2, 0).start()

    def early_two():
        small_copy(2, 2, peer2, 0).wait()
        small[3, early] = small[2, early] + small_r[2, early]
        for k in range(3):
            small_copy(3 + k, 3, peers_z[k], 0).start()

    def early_three():
        for k in range(3):
            small_copy(3 + k, 3, peers_z[k], 0).wait()
        small[4, early] = small[3, early] + (small_r[3, early] + small_r[4, early] + small_r[5, early])

    if fuse:
        small_copy(1, 1, peer1, 0).start()
    gq[0] = dot_nn(cott[...], att[...].astype(BF16)).reshape(gq.shape[1:])
    pq.start1(0)

    def send_mixed(r):
        take_credit(r)
        send(acc_b, r)

    loop(blocks, send_mixed)

    get_nf.wait()

    def turn_first(r):
        nst[:, aligned(r, R)] = jnp.transpose(ns[aligned(r, R), :])

    loop(blocks, turn_first)
    get_wq = [
        load(wq_h.at[k], we.at[:, pl.ds(k * pairs * PAIR, pairs * PAIR)], 4 + k) for k in range(3)
    ]
    kt[...] = jnp.transpose(key[...])

    def mixed_block(r):
        exchange(acc_b, r).wait()
        rows = aligned(r, R)
        ns[rows, :] = (acc_b[rows, :] + xbuf[rows, :]).astype(BF16)
        give_credit(r)
        pltpu.make_async_copy(ns.at[rows, :], mixed_h.at[rows, :], ms.at[r]).start()

    loop(blocks, mixed_block)
    for copy in get_wq:
        copy.wait()

    def pair_back(p):
        cols = aligned(p, PAIR)
        get_cos = load(cossin_h.at[:, cols], cos, 0)
        get_sin = load(cossin_h.at[:, aligned(pairs + p, PAIR)], sin, 1)
        dk[...] = jnp.zeros_like(dk)
        dv[...] = jnp.zeros_like(dv)
        dqt[...] = jnp.zeros_like(dqt)

        def head_back(h):
            mine = head_mask(h).astype(BF16)
            other = head_mask(1 - h).astype(BF16)
            km[...] = key[:, cols] * mine + ohk[...] * other
            vm[...] = val[:, cols] * mine
            spot = lax.broadcasted_iota(jnp.int32, (PAIR, 1), 0)
            kmt[...] = kt[cols, :] * (spot // HALF == h).astype(F32).astype(BF16)
            n = p * 2 + h

            def query_back(r):
                rows = aligned(r, R)
                qm = q8[rows, cols] * mine
                qx = qm + ohq[rows, :] * other
                do = dgrad[rows, cols]
                score = dot_nt(km[...], qx)
                prob = jnp.exp(score - lse[pl.ds(n, 1), rows])
                pgrad = dot_nt(vm[...], do)
                sgrad = (prob * (pgrad - delta[pl.ds(n, 1), rows])).astype(BF16)
                dv[...] = dv[...] + dot_nn(prob.astype(BF16), do * mine)
                dk[...] = dk[...] + dot_nn(sgrad, qm)
                dqt[:, rows] = dqt[:, rows] + dot_nn(kmt[...], sgrad)

            loop(blocks, query_back)
            if fuse:
                if h == 0:
                    ff.finish1(p + 2)
                    ff.finish2(p + 1)
                else:
                    pl.when(p == 0)(deep.finish1)
                    pl.when(p > 0)(lambda: ff.finish3(p - 1))
                    pl.when(p == pairs - 1)(early_one)

        head_back(0)
        head_back(1)
        get_cos.wait()
        get_sin.wait()

        def turn_back(r):
            rows = aligned(r, R)
            lane_first = lane_ids(R) % HALF < HALF // 2
            sign = jnp.where(lane_first, 1.0, -1.0)
            c, s = cos[rows, :], sin[rows, :]
            total = jnp.zeros((R, PAIR), F32)
            grads = []
            scale = HALF**-0.5
            for k, (grad, turned) in enumerate(
                (
                    (jnp.transpose(dqt[:, rows]) * scale, q8[rows, cols].astype(F32) * (1.0 / scale)),
                    (dk[rows, :], key[rows, cols].astype(F32)),
                )
            ):
                swapped = swap_halves(grad, lane_first) * sign
                total = total + swapped * turned
                grads.append((grad * c + swapped * s).astype(BF16))
            grads.append(dv[rows, :].astype(BF16))
            for k, low in enumerate(grads):
                qkvg[rows, k * PAIR : (k + 1) * PAIR] = low
                sums[k + 1 : k + 2, cols] = sums[k + 1 : k + 2, cols] + jnp.sum(
                    low.astype(F32), axis=0, keepdims=True
                )
            for k in range(2):
                sums[k + 4 : k + 5, cols] = sums[k + 4 : k + 5, cols] + jnp.sum(
                    total * pos[rows, k + 1 : k + 2], axis=0, keepdims=True
                )
            weight = jnp.concatenate(
                [we[:, aligned(k * pairs + p, PAIR)] for k in range(3)], axis=1
            )
            acc_a[rows, :] = acc_a[rows, :] + dot_nt(qkvg[rows, :], weight)

        loop(blocks, turn_back)
        gq[p + 1] = dot_nn(nst[...], qkvg[...]).reshape(gq.shape[1:])
        pq.start1(p + 1)

    loop(pairs, pair_back)

    def first_send(r):
        def sub(i):
            rows = pl.ds(pl.multiple_of(r * R + i * SUB, SUB), SUB)
            unit, _ = unit_of(x[rows, :].astype(F32))
            up = acc_a[rows, :]
            small[0, 8:9, :] = small[0, 8:9, :] + jnp.sum(up * unit, axis=0, keepdims=True)
            small[0, 9:10, :] = small[0, 9:10, :] + jnp.sum(up, axis=0, keepdims=True)

        take_credit(r)
        send(acc_a, r)
        loop(R // SUB, sub)

    loop(blocks, first_send)

    m = pairs * PAIR
    for k in range(5):
        small[0, 10 + k : 11 + k, 0:m] = sums[1 + k : 2 + k, 0:m]

    parts = [(j, k) for j in range(pairs + 1) for k in range(3)]
    count = len(parts)
    copy = small_copy(0, 0, mate)
    copy.start()
    if fuse:
        for part in parts[:3]:
            pq.finish1(*part)
        deep.finish2()
        ff.finish2(4)
        ff.finish3(2)
    copy.wait()
    line = lax.broadcasted_iota(jnp.int32, (8, small.shape[2]), 0)
    small[1, late] = small[0, late] + jnp.where(line < 2, small_r[0, late], 0.0)
    if fuse:
        small_copy(1, 1, peer1).start()
    last = 4 if fuse else 1

    def first_back(r):
        exchange(acc_a, r).wait()

        def sub(i):
            rows = pl.ds(pl.multiple_of(r * R + i * SUB, SUB), SUB)
            unit, inv = unit_of(x[rows, :].astype(F32))
            up = acc_a[rows, :] + xbuf[rows, :]
            mid[rows, :] = mid[rows, :] + norm_back(up, unit, inv, gain_one)

        loop(R // SUB, sub)
        rows = aligned(r, R)
        pltpu.make_async_copy(mid.at[rows, :], pgrad_h.at[rows, :], xs.at[r]).start()

    loop(blocks, first_back)
    if fuse:
        early_two()
        sent = done = 0
        for i in range(3, count):
            pq.finish1(*parts[i])
            while sent < i - 1:
                pq.finish2(*parts[sent])
                sent += 1
            if i == 4:
                ff.finish3(3)
            if i == 7:
                ff.finish3(4)
                deep.finish3()
            while done < i - 6:
                pq.finish3(*parts[done])
                done += 1
        small_copy(1, 1, peer1).wait()
        early_three()
        small[2, late] = small[1, late] + small_r[1, late]
        small_copy(2, 2, peer2).start()
        pq.finish2(*parts[count - 2])
        small_copy(2, 2, peer2).wait()
        small[3, late] = small[2, late] + small_r[2, late]
        copies = [small_copy(3 + k, 3, peers_z[k]) for k in range(3)]
        for copy in copies:
            copy.start()
        pq.finish2(*parts[count - 1])
        for part in parts[done : count - 1]:
            pq.finish3(*part)
        for copy in copies:
            copy.wait()
        small[4, late] = small[3, late] + (small_r[3, late] + small_r[4, late] + small_r[5, late])
    out_small = pltpu.make_async_copy(small.at[last], small_h, lsem.at[0])
    out_small.start()
    if fuse:
        pq.finish3(*parts[count - 1])
        deep.drain()
        loop(chunks - 1, ff.drain)
    else:
        loop(chunks, ff.drain)
    loop(pairs + 1, pq.drain)
    out_small.wait()

    def finish_out(r):
        rows = aligned(r, R)
        pltpu.make_async_copy(ns.at[rows, :], mixed_h.at[rows, :], ms.at[r]).wait()
        pltpu.make_async_copy(mid.at[rows, :], pgrad_h.at[rows, :], xs.at[r]).wait()

    loop(blocks, finish_out)


def main_call(fuse, parts, big, grids, freqs, bias_q, vectors):
    x, og, wp, we, wc, wq = big
    rows, width = x.shape
    heads = wq.shape[2]
    hidden = we.shape[1]
    pairs, chunks = heads // PAIR, hidden // CHUNK
    shape = jax.ShapeDtypeStruct
    part_rows = width // parts
    sent = parts if fuse else 0
    if fuse:
        ff_shape, pq_shape = (chunks, part_rows, 2 * CHUNK), (pairs + 1, part_rows, 3 * PAIR)
        grain = (parts, part_rows)
        slots = chunks
    else:
        ff_shape, pq_shape = (chunks, 1, width, 2 * CHUNK), (pairs + 1, 1, width, 3 * PAIR)
        grain = (1, width)
        slots = 1
    outs = [
        shape((rows, width), BF16), shape((rows, width), F32), shape(ff_shape, F32),
        shape(pq_shape, F32), shape((16, width), F32), shape((rows, width), BF16),
        shape((rows, 2 * heads), F32),
    ]
    any_spec = pl.BlockSpec(memory_space=ANY)
    vm_spec = pl.BlockSpec(memory_space=pltpu.VMEM)
    V = pltpu.VMEM
    DMA = pltpu.SemaphoreType.DMA
    REG = pltpu.SemaphoreType.REGULAR
    blocks = rows // R
    lines = chunks + 3 * (pairs + 1)
    recv = (lambda n: V((slots, n, part_rows, 2 * CHUNK), F32)) if fuse else (lambda n: V((1, 1, 8, PAIR), F32))
    scratch = [
        V((rows, heads), F32), V((rows, heads), BF16), V((rows, heads), BF16), V((rows, heads), BF16),
        V((rows, PAIR), BF16), V((rows, PAIR), BF16), V((8, rows), F32), V((rows, PAIR), F32),
        V((rows, width), BF16), V((rows, width), BF16), V((heads, width), BF16),
        V((width, hidden), BF16), V((hidden, width), BF16),
        V((rows, width), F32), V((rows, width), F32), V((rows, width), F32), V((rows, width), F32),
        V((width, rows), BF16), V((rows, width), BF16), V((width, rows), BF16),
        V((rows, CHUNK), BF16), V((rows, CHUNK), BF16), V((rows, heads), BF16), V((8, rows), F32),
        V((rows, PAIR), BF16), V((rows, PAIR), BF16), V((heads, rows), BF16), V((PAIR, rows), BF16),
        V((rows, PAIR), F32), V((rows, PAIR), F32), V((PAIR, rows), F32), V((rows, 3 * PAIR), BF16),
        V((rows, PAIR), F32), V((rows, PAIR), F32), V((8, hidden), F32),
        V((chunks, *grain, 2 * CHUNK), F32), V((pairs + 1, *grain, 3 * PAIR), F32),
        recv(8), recv(4), recv(3), V((5, 16, width), F32), V((6, 16, width), F32),
        DMA((16,)), DMA((blocks,)), DMA((blocks,)), REG((blocks,)),
        DMA((lines,)), DMA((lines,)), DMA((lines,)), DMA((lines,)), DMA((lines,)), DMA((lines,)),
        REG((4,)), REG((4,)), REG((4,)), DMA((16,)), DMA((12,)), DMA((lines,)), DMA((2,)),
    ]
    return pl.pallas_call(
        partial(main_kernel, fuse, pairs, chunks),
        name="main",
        out_shape=outs,
        in_specs=[any_spec] * len(big)
        + [pl.BlockSpec(memory_space=pltpu.SMEM)]
        + [vm_spec] * (2 + len(vectors)),
        out_specs=[any_spec] * len(outs),
        scratch_shapes=scratch,
        compiler_params=pltpu.CompilerParams(
            collective_id=0, has_side_effects=True, vmem_limit_bytes=67043328
        ),
    )(*big, grids, freqs, bias_q, *vectors)


def finish_kernel(
    mixed_h, pgrad_h, ff_h, pq_h, small_h,
    mixed_o, pgrad_o, qkv_o, proj_o, expand_o, contract_o,
    *rest,
):
    tiny_o, (mixed, pgrad, ff, pq, small), tiny, (isem, osem, tsem) = (
        rest[:9], rest[9:14], rest[14:23], rest[23:],
    )
    gain_one, shift_one, bias_q, rope, bias_p, gain_two, shift_two, bias_e, bias_c = tiny
    blocks = mixed.shape[0] // R
    chunks, pairs = ff.shape[0], pq.shape[0] - 1
    jobs = [(small_h, small, [])]
    for src, buf, dst in ((pgrad_h, pgrad, pgrad_o), (mixed_h, mixed, mixed_o)):
        for r in range(blocks):
            part = (pl.ds(r * R, R), slice(None))
            jobs.append((src.at[part], buf.at[part], [(buf.at[part], dst.at[part])]))
    for j in range(chunks):
        cols = pl.ds(j * CHUNK, CHUNK)
        jobs.append((ff_h.at[j], ff.at[j], [
            (ff.at[j, :, pl.ds(0, CHUNK)], contract_o.at[:, cols]),
            (ff.at[j, :, pl.ds(CHUNK, CHUNK)], expand_o.at[:, cols]),
        ]))
    jobs.append((pq_h.at[0], pq.at[0], [(pq.at[0], proj_o)]))
    for p in range(pairs):
        jobs.append((pq_h.at[p + 1], pq.at[p + 1], [
            (pq.at[p + 1, :, pl.ds(k * PAIR, PAIR)], qkv_o.at[k, :, pl.ds(p * PAIR, PAIR)])
            for k in range(3)
        ]))
    gets = [pltpu.make_async_copy(a, b, isem.at[i]) for i, (a, b, _) in enumerate(jobs)]
    for get in gets:
        get.start()
    gets[0].wait()
    heads = bias_q.shape[1]
    for k, out in (
        (8, gain_one), (9, shift_one), (3, bias_p), (1, gain_two), (2, shift_two), (0, bias_c),
    ):
        out[...] = small[k, :]
    half = bias_e.shape[0] // 2
    bias_e[:half] = small[4, :half]
    bias_e[half:] = small[5, :half]
    bias_q[...] = small[10:13, :heads]
    for p in range(pairs):
        tile = small[8:16, p * PAIR : (p + 1) * PAIR]
        both = tile + pltpu.roll(tile, PAIR - HALF // 2, 1)
        rope[2 * p] = both[5:7, : HALF // 2]
        rope[2 * p + 1] = pltpu.roll(both, HALF, 1)[5:7, : HALF // 2]
    last = [pltpu.make_async_copy(a, b, tsem.at[i]) for i, (a, b) in enumerate(zip(tiny, tiny_o))]
    for put in last:
        put.start()
    puts = []
    for get, (_, _, todo) in list(zip(gets, jobs))[1:]:
        get.wait()
        for a, b in todo:
            puts.append(pltpu.make_async_copy(a, b, osem.at[len(puts)]))
            puts[-1].start()
    for put in puts + last:
        put.wait()


def finish(mixed, pgrad, ff, pq, small, hidden):
    rows, width = mixed.shape
    mine = ff.shape[1]
    heads = pq.shape[2]
    shape = lambda *s: jax.ShapeDtypeStruct(s, F32)
    outs = [
        jax.ShapeDtypeStruct((rows, width), BF16), shape(rows, width), shape(3, mine, heads),
        shape(mine, heads), shape(mine, hidden), shape(mine, hidden), shape(width), shape(width),
        shape(3, heads), shape(heads // HALF, 2, HALF // 2), shape(width), shape(width),
        shape(width), shape(hidden), shape(width),
    ]
    any_spec = pl.BlockSpec(memory_space=ANY)
    reads = 1 + 2 * (rows // R) + ff.shape[0] + pq.shape[0]
    writes = 2 * (rows // R) + 2 * ff.shape[0] + 3 * pq.shape[0] - 2
    big = (mixed, pgrad, ff, pq, small)
    return pl.pallas_call(
        finish_kernel,
        name="finish",
        out_shape=outs,
        in_specs=[any_spec] * 5,
        out_specs=[any_spec] * len(outs),
        scratch_shapes=[pltpu.VMEM(v.shape, v.dtype) for v in (*big, *outs[6:])]
        + [pltpu.SemaphoreType.DMA((n,)) for n in (reads, writes, 9)],
        compiler_params=pltpu.CompilerParams(vmem_limit_bytes=67043328),
    )(*big)


def body(
    fuse, parts,
    patches, image_grids, out_grad, first_gain, first_shift, qkv_weight, qkv_bias, rope_freqs,
    proj_weight, proj_bias, second_gain, second_shift, expand_weight, expand_bias,
    contract_weight, contract_bias,
):
    width = patches.shape[1]
    mixed, pgrad, ff, pq, small, _, _ = main_call(
        fuse,
        parts,
        (patches, out_grad, proj_weight, expand_weight, contract_weight, qkv_weight),
        image_grids.T,
        rope_freqs.transpose(1, 0, 2),
        qkv_bias,
        (first_gain, first_shift, proj_bias, second_gain, second_shift, expand_bias, contract_bias),
    )
    if not fuse:
        scatter = partial(lax.psum_scatter, axis_name="dp", scatter_dimension=1, tiled=True)
        ff = scatter(ff.reshape(ff.shape[0], width, ff.shape[-1]))
        pq = scatter(pq.reshape(pq.shape[0], width, pq.shape[-1]))
        small = lax.psum(small, "dp")
    (
        mixed, pgrad, qkv, proj, expand, contract, gain_one, shift_one, bias_q, rope,
        bias_p, gain_two, shift_two, bias_e, bias_c,
    ) = finish(mixed, pgrad, ff, pq, small, expand_bias.shape[0])
    return (
        mixed, pgrad, qkv, proj.T, expand, contract.T, gain_one, shift_one, bias_q,
        rope.transpose(1, 0, 2), bias_p, gain_two, shift_two, bias_e, bias_c,
    )


def solution(mesh):
    in_specs = (
        P("dp", None), P("dp", None), P("dp", None), P(), P(), P(None, None, "head"),
        P(None, "head"), P(None, "head", None), P("head", None), P(), P(), P(),
        P(None, "head"), P("head"), P("head", None), P(),
    )
    out_specs = (
        P("dp", None), P("dp", None), P(None, "dp", "head"), P("head", "dp"), P("dp", "head"),
        P("head", "dp"), P(), P(), P(None, "head"), P(None, "head", None), P(), P(), P(),
        P("head"), P(),
    )
    parts = mesh.shape["dp"]
    run = partial(body, parts == PARTS, parts)
    return jax.shard_map(run, mesh=mesh, in_specs=in_specs, out_specs=out_specs, check_vma=False)
```

```python
from functools import partial

import jax
import jax.numpy as jnp
from jax import lax
from jax.experimental import pallas as pl
from jax.experimental.pallas import tpu as pltpu
from jax.sharding import PartitionSpec as P

F32 = jnp.float32
BF16 = jnp.bfloat16
EPS = 1e-06
FAR = 2.0**100
R = 256
QR = 512
SUB = 64
PAIR = 128
HALF = 64
CHUNK = 256
MESH = pl.DeviceIdType.MESH
ANY = pl.ANY


def dot_nn(a, b):
    return lax.dot_general(a, b, (((1,), (0,)), ((), ())), preferred_element_type=F32)


def dot_nt(a, b):
    return lax.dot_general(a, b, (((1,), (1,)), ((), ())), preferred_element_type=F32)


def aligned(i, size):
    return pl.ds(pl.multiple_of(i * size, size), size)


def loop(count, fn):
    def step(i, carry):
        fn(i)
        return carry

    lax.fori_loop(0, count, step, 0)


def unit_of(rows):
    centred = rows - jnp.mean(rows, axis=-1, keepdims=True)
    inv = lax.rsqrt(jnp.mean(centred * centred, axis=-1, keepdims=True) + EPS)
    return centred * inv, inv


def norm_back(upstream, unit, inv, gain):
    scaled = upstream * gain
    return inv * (
        scaled
        - jnp.mean(scaled, axis=-1, keepdims=True)
        - unit * jnp.mean(scaled * unit, axis=-1, keepdims=True)
    )


def swap_halves(v, lane_first):
    return jnp.where(lane_first, pltpu.roll(v, PAIR - HALF // 2, 1), pltpu.roll(v, HALF // 2, 1))


def lane_ids(rows):
    return lax.broadcasted_iota(jnp.int32, (rows, PAIR), 1)


def head_mask(h):
    lane = lax.broadcasted_iota(jnp.int32, (1, PAIR), 1)
    return (lane // HALF == h).astype(F32)


def pieces(table):
    high = table.astype(BF16)
    rest = table - high.astype(F32)
    mid = rest.astype(BF16)
    low = (rest - mid.astype(F32)).astype(BF16)
    return jnp.concatenate([high, mid, low], axis=0)


def front_place(grids, slots, freqs, ohq, ohk, cossin, pos):
    rows_all, width_all = pos.shape[0], freqs[0].shape[1]
    side = lax.broadcasted_iota(jnp.int32, (32, 1), 0).astype(F32)
    ang_r = side * freqs[0]
    ang_c = side * freqs[1]
    table_r = pieces(jnp.concatenate([jnp.cos(ang_r), jnp.sin(ang_r)], axis=1))
    table_c = pieces(jnp.concatenate([jnp.cos(ang_c), jnp.sin(ang_c)], axis=1))

    def place(r):
        rows = aligned(r, 256)
        t = lax.broadcasted_iota(jnp.int32, (256, 1), 0) + r * 256
        seg = jnp.zeros((256, 1), jnp.int32)
        start = jnp.zeros((256, 1), jnp.int32)
        width = jnp.ones((256, 1), jnp.int32)
        end = jnp.int32(0)
        for s in range(slots):
            begun = t >= end
            start = jnp.where(begun, end, start)
            width = jnp.where(begun, jnp.maximum(grids[1, s], 1), width)
            end = end + grids[0, s] * grids[1, s]
            seg = jnp.where(t >= end, s + 1, seg)
        real = (seg < slots).astype(F32)
        off = (t - start).astype(F32)
        wide = width.astype(F32)
        grow = jnp.floor((off + 0.5) / wide) * real
        gcol = (off - grow * wide) * real
        lane = lane_ids(256)
        pos[rows, :] = jnp.where(lane == 0, real, jnp.where(lane == 1, grow, gcol))
        hot = lane % HALF == seg
        ohq[rows, :] = jnp.where(hot, 1.0, 0.0).astype(BF16)
        ohk[rows, :] = jnp.where(hot, 0.0, -FAR).astype(BF16)
        spot = (lax.broadcasted_iota(jnp.int32, (256, 96), 1) % 32).astype(F32)
        got_r = dot_nn(jnp.where(spot == grow, 1.0, 0.0).astype(BF16), table_r)
        got_c = dot_nn(jnp.where(spot == gcol, 1.0, 0.0).astype(BF16), table_c)
        cr, sr = got_r[:, :width_all], got_r[:, width_all:]
        cc, sc = got_c[:, :width_all], got_c[:, width_all:]
        cossin[rows, :width_all] = cr * cc - sr * sc
        cossin[rows, width_all:] = sr * cc + cr * sc

    loop(rows_all // 256, place)


def front_rows(x, gain, shift, w, b, q8, key, val, nf, cossin):
    rows_all, width_all = q8.shape
    pairs = width_all // PAIR

    def norm(r):
        rows = aligned(r, SUB)
        unit, _ = unit_of(x[rows, :].astype(F32))
        nf[rows, :] = (unit * gain + shift).astype(BF16)

    loop(rows_all // SUB, norm)

    def project(r):
        rows = aligned(r, QR)
        lane_first = lane_ids(QR) % HALF < HALF // 2
        sign = jnp.where(lane_first, -1.0, 1.0)
        for k, out in ((0, q8), (1, key)):
            got = dot_nn(nf[rows, :], w[:, k * width_all : (k + 1) * width_all]) + b[k : k + 1, :]
            for p in range(pairs):
                cols = slice(p * PAIR, (p + 1) * PAIR)
                part = got[:, cols]
                turned = part * cossin[rows, cols] + swap_halves(part, lane_first) * (
                    cossin[rows, width_all + p * PAIR : width_all + (p + 1) * PAIR] * sign
                )
                turned = turned.astype(BF16)
                if k == 0:
                    turned = turned * jnp.asarray(HALF**-0.5, BF16)
                out[rows, cols] = turned
        got = dot_nn(nf[rows, :], w[:, 2 * width_all : 3 * width_all])
        val[rows, :] = (got + b[2:3, :]).astype(BF16)

    loop(rows_all // QR, project)


def front_heads(q8, key, val, ohq, ohk, att, kxs, scs, lcol, after):
    rows_all, width_all = q8.shape
    blocks, pieces_all, wide = rows_all // QR, rows_all // R, scs[0].shape[1] // R
    masks = [head_mask(h).astype(BF16) for h in range(2)]

    def piece(h, k):
        at = (k // wide) * QR
        return scs[h].at[at : at + QR, (k % wide) * R : (k % wide + 1) * R]

    pairs = width_all // PAIR

    def keys(h, p):
        kxs[h][...] = key[:, aligned(p, PAIR)] * masks[h] + ohk[...] * masks[1 - h]

    def scores(h, r, p):
        rows = aligned(r, QR)
        qx = q8[rows, aligned(p, PAIR)] * masks[h] + ohq[rows, :] * masks[1 - h]
        for k in range(pieces_all):
            piece(h, k)[...] = dot_nt(qx, kxs[h][k * R : (k + 1) * R, :])

    def weigh(h, r, p):
        rows, cols = aligned(r, QR), aligned(p, PAIR)
        top = piece(h, 0)[...]
        for k in range(1, pieces_all):
            top = jnp.maximum(top, piece(h, k)[...])
        top = jnp.max(top, axis=-1, keepdims=True)
        total = jnp.zeros((QR, PAIR), F32)
        got = jnp.zeros((QR, PAIR), F32)
        for k in range(pieces_all):
            grown = jnp.exp(piece(h, k)[...] - top)
            for m in range(R // PAIR):
                total = total + grown[:, m * PAIR : (m + 1) * PAIR]
            got = got + dot_nn(grown.astype(BF16), val[k * R : (k + 1) * R, cols])
        total = jnp.sum(total, axis=-1, keepdims=True)
        got = got * (1.0 / total)
        lane = lane_ids(QR)
        if h == 0:
            att[rows, cols] = got
        else:
            att[rows, cols] = jnp.where(lane < HALF, att[rows, cols], got)
        lcol[rows, :] = jnp.where(lane == p * 2 + h, top + jnp.log(total), lcol[rows, :])

    keys(0, 0)
    keys(1, 0)
    scores(0, 0, 0)

    def half(r):
        def step(p):
            n = jnp.minimum(r * pairs + p + 1, blocks * pairs - 1)
            scores(1, r, p)
            weigh(0, r, p)
            keys(0, n % pairs)
            scores(0, n // pairs, n % pairs)
            weigh(1, r, p)
            keys(1, n % pairs)

        loop(pairs, step)
        after(r)

    loop(blocks, half)


PARTS = 16


def main_kernel(
    fuse, pairs, chunks,
    x_h, og_h, wp_h, we_h, wc_h, wq_h,
    grids, freqs, bias_q, *rest,
):
    (
    gain_one, shift_one, bias_p, gain_two, shift_two, bias_e, bias_c,
    mixed_h, pgrad_h, ff_h, pq_h, small_h, nf_h, cossin_h,
    att, q8, key, val, ohq, ohk, lse, pos, x, cot, wp, we, wc,
    acc_a, acc_b, xbuf, mid, cott, ns, nst, act, hgb, dgrad, delta,
    km, vm, kt, kmt, dk, dv, dqt, qkvg, cos, sin, sums,
    gf, gq, r1, r2, r3, small, small_r,
    lsem, xs, xr, credit, s1, e1, s2, e2, s3, e3, c1, c2, c3, ms, mr, osem, zs, s4, e4,
    ) = rest
    gain_one, shift_one, bias_p, gain_two, shift_two, bias_e, bias_c = (
        v[...].reshape(1, -1)
        for v in (gain_one, shift_one, bias_p, gain_two, shift_two, bias_e, bias_c)
    )
    me = lax.axis_index("dp")
    core = lax.axis_index("head")
    blocks = x.shape[0] // R
    subs = x.shape[0] // SUB
    mate = (me, 1 - core)
    if fuse:
        xx, yy, zz = me % 2, (me // 2) % 2, me // 4
        fst = xx * (1 - core) + yy * core
        snd = yy * (1 - core) + xx * core
        peer1 = (me + (1 - 2 * fst) * (1 + core), core)
        peer2 = (me + (1 - 2 * snd) * (2 - core), core)
        peers_z = [(((zz + j) % 4) * 4 + me % 4, core) for j in (1, 2, 3)]
        odd, across = zz % 2, (zz + 2) % 4
        near = ((zz + 1 - 2 * odd) * 4 + me % 4, core)
        far = (across * 4 + me % 4, core)

        def where(z, f, s):
            return z * 4 + s * (2 - core) + f * (1 + core)

    def load(src, dst, i):
        copy = pltpu.make_async_copy(src, dst, lsem.at[i])
        copy.start()
        return copy

    heads = q8.shape[1]
    slots = grids.shape[1]
    get_x = load(x_h, x, 4)
    get_wq = [load(wq_h.at[k], we.at[:, pl.ds(k * heads, heads)], 7 + k) for k in range(3)]
    get_wp = load(wp_h, wp, 1)
    get_og = load(og_h, cot, 2)
    get_wc = load(wc_h, wc, 6)

    barrier = pltpu.get_barrier_semaphore()
    friends = [mate] + ([peer1, peer2] + peers_z if fuse else [])
    for friend in friends:
        pl.semaphore_signal(barrier, inc=1, device_id=friend, device_id_type=MESH)

    def exchange(src, r):
        return pltpu.make_async_remote_copy(
            src.at[aligned(r, R), :], xbuf.at[aligned(r, R), :], xs.at[r], xr.at[r],
            device_id=mate, device_id_type=MESH,
        )

    def send(src, r):
        exchange(src, r).start()

    def give_credit(r):
        pl.semaphore_signal(credit.at[r], inc=1, device_id=mate, device_id_type=MESH)

    def take_credit(r):
        pl.semaphore_wait(credit.at[r], 1)

    def remote(src, dst, ss, rs, peer):
        return pltpu.make_async_remote_copy(
            src, dst, ss, rs, device_id=peer, device_id_type=MESH
        )

    class Line:
        def __init__(self, grads, base, width, out, guard, parts):
            self.g, self.base, self.out, self.guard = grads, base, out, guard
            self.n, self.parts = width // parts, parts

        def cols(self, k):
            return pl.ds(k * self.n, self.n)

        def at(self, j, k):
            return self.base + j * self.parts + k

        def step(self, j, k, first, src, dst, ss, rs, peer):
            i = self.at(j, k)
            return remote(
                self.g.at[j, src, :, self.cols(k)], first.at[j, dst, :, self.cols(k)],
                ss.at[i], rs.at[i], peer,
            )

        def whole(self, j, k, n, ss, rs, buf, peer):
            return self.step(j, k, buf, pl.ds(0, n), pl.ds(0, n), ss, rs, peer)

        def add(self, j, k, b, got):
            c = self.cols(k)
            self.g[j, b, :, c] = self.g[j, b, :, c] + got

        def start1(self, j):
            if self.guard == "take":
                pl.semaphore_wait(c1.at[j], 1)
            for k in range(self.parts):

                def one(i, k=k):
                    b = where(i // 2, 1 - fst, i % 2)
                    self.step(j, k, r1, b, i, s1, e1, peer1).start()

                loop(8, one)

        def give(self, sem, j, peers):
            if self.guard == "give":
                def go():
                    for peer in peers:
                        pl.semaphore_signal(sem.at[j], inc=1, device_id=peer, device_id_type=MESH)
                if isinstance(j, int):
                    if j < 4:
                        go()
                else:
                    pl.when(j < 4)(go)

        def finish1(self, j, k=0):
            self.whole(j, k, 8, s1, e1, r1, peer1).wait_recv()
            c = self.cols(k)

            def one(i):
                self.add(j, k, where(i // 2, fst, i % 2), r1[j, i, :, c])

            loop(8, one)
            self.give(c1, j, [peer1])
            if self.guard == "take" and k == 0:
                pl.semaphore_wait(c2.at[j], 1)

            def two(i):
                self.step(j, k, r2, where(i, fst, 1 - snd), i, s2, e2, peer2).start()

            loop(4, two)

        def finish2(self, j, k=0):
            self.whole(j, k, 4, s2, e2, r2, peer2).wait_recv()
            c = self.cols(k)

            def one(i):
                self.add(j, k, where(i, fst, snd), r2[j, i, :, c])

            loop(4, one)
            self.give(c2, j, [peer2])
            if self.guard == "take" and k == 0:
                pl.semaphore_wait(c3.at[j], 3)
            for m in range(3):
                b = where((zz + m + 1) % 4, fst, snd)
                self.step(j, k, r3, b, m, s3, e3, peers_z[m]).start()

        def result(self, j, k):
            c = self.cols(k)
            return pltpu.make_async_copy(
                self.g.at[j, me, :, c], self.out.at[j, :, c], osem.at[self.at(j, k)]
            )

        def finish3(self, j, k=0):
            self.whole(j, k, 3, s3, e3, r3, peers_z[0]).wait_recv()
            c = self.cols(k)
            self.add(j, k, me, r3[j, 0, :, c] + r3[j, 1, :, c] + r3[j, 2, :, c])
            self.give(c3, j, peers_z)
            self.result(j, k).start()

        def drain(self, j):
            for k in range(self.parts):
                self.whole(j, k, 8, s1, e1, r1, peer1).wait_send()
                self.whole(j, k, 4, s2, e2, r2, peer2).wait_send()
                self.whole(j, k, 3, s3, e3, r3, peers_z[0]).wait_send()
                self.result(j, k).wait()

    class Two(Line):
        def finish2(self, j, k=0):
            self.whole(j, k, 4, s2, e2, r2, peer2).wait_recv()
            c = self.cols(k)

            def one(i):
                self.add(j, k, where(i, fst, snd), r2[j, i, :, c])

            loop(4, one)
            self.give(c2, j, [peer2])
            for m in range(2):
                b = where(1 - odd + 2 * m, fst, snd)
                self.step(j, k, r3, b, m, s3, e3, near).start()

        def finish3(self, j, k=0):
            self.whole(j, k, 2, s3, e3, r3, near).wait_recv()
            c = self.cols(k)
            for m in range(2):
                self.add(j, k, where(odd + 2 * m, fst, snd), r3[j, m, :, c])
            self.step(j, k, r3, where(across, fst, snd), 2, s4, e4, far).start()

        def finish4(self, j, k=0):
            self.step(j, k, r3, 0, 2, s4, e4, far).wait_recv()
            self.add(j, k, me, r3[j, 2, :, self.cols(k)])
            self.give(c3, j, peers_z)
            self.result(j, k).start()

        def drain(self, j):
            for k in range(self.parts):
                self.whole(j, k, 8, s1, e1, r1, peer1).wait_send()
                self.whole(j, k, 4, s2, e2, r2, peer2).wait_send()
                self.whole(j, k, 2, s3, e3, r3, near).wait_send()
                self.step(j, k, r3, 0, 2, s4, e4, far).wait_send()
                self.result(j, k).wait()

    class Deep:
        def __init__(self, grads, j, out, line):
            self.g, self.j, self.out, self.line = grads, j, out, line

        def one(self):
            j = self.j
            return remote(self.g.at[j, pl.ds(0, 8)], r1.at[j], s1.at[j], e1.at[j], near)

        def two(self):
            j = self.j
            return remote(self.g.at[j, pl.ds(across * 4, 4)], r2.at[j], s2.at[j], e2.at[j], far)

        def three(self):
            j = self.j
            return remote(
                self.g.at[j, pl.ds(0, 2)], r3.at[j, pl.ds(0, 2)], s3.at[j], e3.at[j], peer1
            )

        def four(self):
            return remote(
                self.g.at[self.j, where(zz, fst, 1 - snd)], r3.at[self.j, 2],
                zs.at[2 * self.line], zs.at[2 * self.line + 1], peer2,
            )

        def result(self):
            return pltpu.make_async_copy(
                self.g.at[self.j, me], self.out.at[self.j], osem.at[self.j]
            )

        def start(self):
            j = self.j
            for m in range(2):
                remote(
                    self.g.at[j, pl.ds((1 - odd + 2 * m) * 4, 4)], r1.at[j, pl.ds(4 * m, 4)],
                    s1.at[j], e1.at[j], near,
                ).start()

        def finish1(self):
            j = self.j
            self.one().wait_recv()

            def add(i):
                b = (odd + 2 * (i // 4)) * 4 + i % 4
                self.g[j, b] = self.g[j, b] + r1[j, i]

            loop(8, add)
            self.two().start()

        def finish2(self):
            j = self.j
            self.two().wait_recv()

            def add(i):
                self.g[j, zz * 4 + i] = self.g[j, zz * 4 + i] + r2[j, i]

            loop(4, add)
            for s in range(2):
                remote(
                    self.g.at[j, where(zz, 1 - fst, s)], r3.at[j, s], s3.at[j], e3.at[j], peer1
                ).start()

        def finish3(self):
            j = self.j
            self.three().wait_recv()
            for s in range(2):
                b = where(zz, fst, s)
                self.g[j, b] = self.g[j, b] + r3[j, s]
            self.four().start()

        def finish4(self):
            self.four().wait_recv()
            self.g[self.j, me] = self.g[self.j, me] + r3[self.j, 2]
            self.result().start()

        def drain(self):
            for copy in (self.one(), self.two(), self.three(), self.four()):
                copy.wait_send()
            self.result().wait()

    class Plain:
        def __init__(self, grads, base, width, out, guard, parts):
            self.g, self.base, self.out = grads, base, out

        def copy(self, j):
            return pltpu.make_async_copy(self.g.at[j], self.out.at[j], osem.at[self.base + j])

        def start1(self, j):
            self.copy(j).start()

        def finish1(self, j):
            pass

        finish2 = finish3 = finish1

        def drain(self, j):
            self.copy(j).wait()

    kind = Line if fuse else Plain
    ff = (Two if fuse else Plain)(gf, 0, 2 * CHUNK, ff_h, "give", 1)
    pq = kind(gq, chunks, 3 * PAIR, pq_h, "take", 3)
    deep = [Deep(gf, chunks - 1 - n, ff_h, n) for n in range(2)]

    small[...] = jnp.zeros_like(small)
    sums[...] = jnp.zeros_like(sums)
    sums[7:8, :] = bias_e

    turns = []
    for axis in range(2):
        lines = [freqs[n, axis : axis + 1, :] for n in range(heads // HALF) for _ in range(2)]
        turns.append(jnp.concatenate(lines, axis=1))
    front_place(grids, slots, turns, ohq, ohk, acc_b, pos)
    put_cossin = load(acc_b.at[:, pl.ds(0, 2 * heads)], cossin_h, 11)
    get_x.wait()
    for copy in get_wq:
        copy.wait()
    front_rows(x, gain_one, shift_one, we, bias_q, q8, key, val, ns, acc_b)
    get_we = load(we_h, we, 5)
    put_nf = load(ns, nf_h, 10)
    put_cossin.wait()
    get_wp.wait()
    pl.semaphore_wait(barrier, len(friends))

    def project(r):
        for n in range(QR // R):
            rows = aligned(r * (QR // R) + n, R)
            acc_a[rows, :] = dot_nn(att[rows, :].astype(BF16), wp[...])
            send(acc_a, r * (QR // R) + n)

    front_heads(q8, key, val, ohq, ohk, att, (km, vm), (mid, acc_b), dk, project)

    def turn(r):
        rows = aligned(r, PAIR)
        lse[:, rows] = jnp.transpose(dk[rows, :])[: lse.shape[0], :]

    loop(x.shape[0] // PAIR, turn)

    get_og.wait()

    def mask_cot(r):
        rows = aligned(r, R)
        block = (cot[rows, :].astype(F32) * pos[rows, 0:1])
        small[0, 0:1, :] = small[0, 0:1, :] + jnp.sum(block, axis=0, keepdims=True)
        low = block.astype(BF16)
        cot[rows, :] = low
        cott[:, rows] = jnp.transpose(low)

    loop(blocks, mask_cot)
    put_nf.wait()

    def second_norm(r):
        exchange(acc_a, r).wait()

        def sub(i):
            rows = pl.ds(pl.multiple_of(r * R + i * SUB, SUB), SUB)
            middle = x[rows, :].astype(F32) + ((acc_a[rows, :] + xbuf[rows, :]) + bias_p)
            unit, _ = unit_of(middle)
            mid[rows, :] = middle
            ns[rows, :] = (unit * gain_two + shift_two).astype(BF16)
            acc_b[rows, :] = 0.5 * (middle + bias_c)
            acc_a[rows, :] = jnp.zeros_like(middle)

        loop(R // SUB, sub)
        give_credit(r)
        nst[:, aligned(r, R)] = jnp.transpose(ns[aligned(r, R), :])

    loop(blocks, second_norm)
    get_we.wait()
    get_wc.wait()

    def feed(i):
        none, upto = 1 - (i + chunks - 1) // chunks, 1 - (i + chunks - 3) // chunks
        j = (i - 2) * (1 - upto) + (chunks - i) * (upto - none)
        cols = aligned(j, CHUNK)

        def rows_of(r):
            rows = aligned(r, QR)
            hidden = dot_nn(ns[rows, :], we[:, cols]) + sums[7:8, cols]
            upstream = dot_nt(cot[rows, :], wc[cols, :])
            phi = 0.5 * (1.0 + lax.erf(hidden * (0.5**0.5)))
            slope = phi + hidden * (jnp.exp(-0.5 * hidden * hidden) * (0.3989422804014327))
            active = (hidden * phi).astype(BF16)
            hgrad = (upstream * slope).astype(BF16)
            act[rows, :] = active
            hgb[rows, :] = hgrad
            sums[0:1, cols] = sums[0:1, cols] + jnp.sum(hgrad.astype(F32), axis=0, keepdims=True)
            acc_b[rows, :] = acc_b[rows, :] + dot_nn(active, wc[cols, :])
            acc_a[rows, :] = acc_a[rows, :] + dot_nt(hgrad, we[:, cols])

            def leave():
                for n in range(QR // R):
                    take_credit(r * (QR // R) + n)
                    send(acc_a, r * (QR // R) + n)

            pl.when(i == chunks - 1)(leave)

        loop(x.shape[0] // QR, rows_of)
        got = dot_nn(cott[...], act[...])
        gf[j, :, :, pl.ds(0, CHUNK)] = got.reshape(gf.shape[1], gf.shape[2], CHUNK)
        got = dot_nn(nst[...], hgb[...])
        gf[j, :, :, pl.ds(CHUNK, CHUNK)] = got.reshape(gf.shape[1], gf.shape[2], CHUNK)
        if fuse:
            pl.when(i == 1)(deep[0].start)
            pl.when(i == 2)(deep[1].start)
            pl.when((i != 1) & (i != 2))(lambda: ff.start1(j))
            pl.when(i == 4)(lambda: ff.finish1(0))
        else:
            ff.start1(j)

    loop(chunks, feed)

    get_nf = load(nf_h, ns, 0)
    get_wq = [
        load(wq_h.at[k], we.at[:, pl.ds(k * pairs * PAIR, pairs * PAIR)], 4 + k) for k in range(3)
    ]
    kt[...] = jnp.transpose(key[...])
    get_nf.wait()

    def turn_first(r):
        nst[:, aligned(r, R)] = jnp.transpose(ns[aligned(r, R), :])

    loop(blocks, turn_first)
    if fuse:
        deep[0].finish1()
        ff.finish1(1)

    def second_back(r):
        exchange(acc_a, r).wait()

        def sub(i):
            rows = pl.ds(pl.multiple_of(r * R + i * SUB, SUB), SUB)
            up = acc_a[rows, :] + xbuf[rows, :]
            unit, inv = unit_of(mid[rows, :])
            small[0, 1:2, :] = small[0, 1:2, :] + jnp.sum(up * unit, axis=0, keepdims=True)
            small[0, 2:3, :] = small[0, 2:3, :] + jnp.sum(up, axis=0, keepdims=True)
            grad = cot[rows, :].astype(F32) + norm_back(up, unit, inv, gain_two)
            mid[rows, :] = grad
            low = grad.astype(BF16)
            cot[rows, :] = low
            small[0, 3:4, :] = small[0, 3:4, :] + jnp.sum(
                low.astype(F32), axis=0, keepdims=True
            )

        loop(R // SUB, sub)
        give_credit(r)
        rows = aligned(r, R)
        cott[:, rows] = jnp.transpose(cot[rows, :])
        low = dot_nt(cot[rows, :], wp[...]).astype(BF16)
        dgrad[rows, :] = low
        prod = low.astype(F32) * att[rows, :]
        head = lax.broadcasted_iota(jnp.int32, (8, prod.shape[1]), 0)
        lane = lax.broadcasted_iota(jnp.int32, (8, prod.shape[1]), 1)
        pick = (lane // HALF == head).astype(F32)
        delta[:, rows] = lax.dot_general(
            pick, prod, (((1,), (1,)), ((), ())), precision=lax.Precision.HIGHEST,
            preferred_element_type=F32,
        )

    loop(blocks, second_back)
    if fuse:
        ff.finish2(0)

    def small_copy(i, k, peer, late=1):
        rows = pl.ds(8 * late, 8)
        return remote(
            small.at[k, rows], small_r.at[i, rows], ms.at[4 + 6 * late + i], mr.at[6 * late + i],
            peer,
        )

    early, late = slice(0, 8), slice(8, 16)
    n = chunks * CHUNK // 2
    small[0, 4:5, :] = sums[0:1, 0:n]
    small[0, 5:6, :] = sums[0:1, n : 2 * n]
    small[1, early] = small[0, early]

    def early_one():
        small_copy(1, 1, peer1, 0).wait()
        small[2, early] = small[1, early] + small_r[1, early]
        small_copy(2, 2, peer2, 0).start()

    def early_two():
        small_copy(2, 2, peer2, 0).wait()
        small[3, early] = small[2, early] + small_r[2, early]
        for k in range(3):
            small_copy(3 + k, 3, peers_z[k], 0).start()

    def early_three():
        for k in range(3):
            small_copy(3 + k, 3, peers_z[k], 0).wait()
        small[4, early] = small[3, early] + (small_r[3, early] + small_r[4, early] + small_r[5, early])

    if fuse:
        small_copy(1, 1, peer1, 0).start()
    gq[0] = dot_nn(cott[...], att[...].astype(BF16)).reshape(gq.shape[1:])
    pq.start1(0)
    if fuse:
        ff.finish1(2)

    def send_mixed(r):
        take_credit(r)
        send(acc_b, r)

    loop(blocks, send_mixed)

    def mixed_block(r):
        exchange(acc_b, r).wait()
        rows = aligned(r, R)
        ns[rows, :] = (acc_b[rows, :] + xbuf[rows, :]).astype(BF16)
        give_credit(r)
        pltpu.make_async_copy(ns.at[rows, :], mixed_h.at[rows, :], ms.at[r]).start()

    def thrice(step, j):
        for k in range(3):
            step(j, k)

    def gap0():
        ff.finish2(1)

    def gap1():
        deep[1].finish1()
        ff.finish1(3)

    def gap2():
        deep[0].finish2()
        ff.finish3(0)
        ff.finish2(2)

    def gap3():
        ff.finish3(1)
        thrice(pq.finish1, 0)

    def gap4():
        deep[1].finish2()
        ff.finish2(3)
        ff.finish4(0)

    def gap5():
        early_one()
        thrice(pq.finish2, 0)
        thrice(pq.finish1, 1)

    between = (gap0, gap1, gap2, gap3, gap4, gap5)

    def pair_back(p):
        cols = aligned(p, PAIR)
        get_cos = load(cossin_h.at[:, cols], cos, 0)
        get_sin = load(cossin_h.at[:, aligned(pairs + p, PAIR)], sin, 1)
        dk[...] = jnp.zeros_like(dk)
        dv[...] = jnp.zeros_like(dv)
        dqt[...] = jnp.zeros_like(dqt)

        def head_back(h):
            mine = head_mask(h).astype(BF16)
            other = head_mask(1 - h).astype(BF16)
            km[...] = key[:, cols] * mine + ohk[...] * other
            vm[...] = val[:, cols] * mine
            spot = lax.broadcasted_iota(jnp.int32, (PAIR, 1), 0)
            kmt[...] = kt[cols, :] * (spot // HALF == h).astype(F32).astype(BF16)
            n = p * 2 + h

            def query_back(r):
                rows = aligned(r, R)
                qm = q8[rows, cols] * mine
                qx = qm + ohq[rows, :] * other
                do = dgrad[rows, cols]
                score = dot_nt(km[...], qx)
                prob = jnp.exp(score - lse[pl.ds(n, 1), rows])
                pgrad = dot_nt(vm[...], do)
                sgrad = (prob * (pgrad - delta[pl.ds(n, 1), rows])).astype(BF16)
                dv[...] = dv[...] + dot_nn(prob.astype(BF16), do * mine)
                dk[...] = dk[...] + dot_nn(sgrad, qm)
                dqt[:, rows] = dqt[:, rows] + dot_nn(kmt[...], sgrad)

            loop(blocks, query_back)
            if fuse:
                for q in range(3):
                    pl.when(p == q)(lambda q=q: between[2 * q + h]())

        head_back(0)
        head_back(1)
        get_cos.wait()
        get_sin.wait()

        def turn_back(r):
            rows = aligned(r, R)
            lane_first = lane_ids(R) % HALF < HALF // 2
            sign = jnp.where(lane_first, 1.0, -1.0)
            c, s = cos[rows, :], sin[rows, :]
            total = jnp.zeros((R, PAIR), F32)
            grads = []
            scale = HALF**-0.5
            for k, (grad, turned) in enumerate(
                (
                    (jnp.transpose(dqt[:, rows]) * scale, q8[rows, cols].astype(F32) * (1.0 / scale)),
                    (dk[rows, :], key[rows, cols].astype(F32)),
                )
            ):
                swapped = swap_halves(grad, lane_first) * sign
                total = total + swapped * turned
                grads.append((grad * c + swapped * s).astype(BF16))
            grads.append(dv[rows, :].astype(BF16))
            for k, low in enumerate(grads):
                qkvg[p, rows, k * PAIR : (k + 1) * PAIR] = low
                sums[k + 1 : k + 2, cols] = sums[k + 1 : k + 2, cols] + jnp.sum(
                    low.astype(F32), axis=0, keepdims=True
                )
            for k in range(2):
                sums[k + 4 : k + 5, cols] = sums[k + 4 : k + 5, cols] + jnp.sum(
                    total * pos[rows, k + 1 : k + 2], axis=0, keepdims=True
                )

        loop(blocks, turn_back)
        gq[p + 1] = dot_nn(nst[...], qkvg[p]).reshape(gq.shape[1:])
        pq.start1(p + 1)

    loop(pairs, pair_back)

    def first_send(r):
        def sub(i):
            rows = pl.ds(pl.multiple_of(r * R + i * SUB, SUB), SUB)
            unit, _ = unit_of(x[rows, :].astype(F32))
            up = acc_a[rows, :]
            small[0, 8:9, :] = small[0, 8:9, :] + jnp.sum(up * unit, axis=0, keepdims=True)
            small[0, 9:10, :] = small[0, 9:10, :] + jnp.sum(up, axis=0, keepdims=True)

        rows = aligned(r, R)
        total = jnp.zeros((R, acc_a.shape[1]), F32)
        for p in range(pairs):
            weight = jnp.concatenate(
                [we[:, (k * pairs + p) * PAIR : (k * pairs + p + 1) * PAIR] for k in range(3)],
                axis=1,
            )
            total = total + dot_nt(qkvg[p, rows, :], weight)
        acc_a[rows, :] = total
        take_credit(r)
        send(acc_a, r)
        loop(R // SUB, sub)

    if fuse:
        deep[0].finish3()
        ff.finish3(2)
        ff.finish4(1)
        thrice(pq.finish2, 1)
    loop(blocks, mixed_block)
    for copy in get_wq:
        copy.wait()
    loop(blocks, first_send)

    m = pairs * PAIR
    for k in range(5):
        small[0, 10 + k : 11 + k, 0:m] = sums[1 + k : 2 + k, 0:m]

    copy = small_copy(0, 0, mate)
    copy.start()
    if fuse:
        thrice(pq.finish1, 2)
        deep[1].finish3()
        ff.finish3(3)
        ff.finish4(2)
    copy.wait()
    line = lax.broadcasted_iota(jnp.int32, (8, small.shape[2]), 0)
    small[1, late] = small[0, late] + jnp.where(line < 2, small_r[0, late], 0.0)
    if fuse:
        small_copy(1, 1, peer1).start()
        thrice(pq.finish2, 2)
    last = 4 if fuse else 1

    def first_back(r):
        exchange(acc_a, r).wait()

        def sub(i):
            rows = pl.ds(pl.multiple_of(r * R + i * SUB, SUB), SUB)
            unit, inv = unit_of(x[rows, :].astype(F32))
            up = acc_a[rows, :] + xbuf[rows, :]
            mid[rows, :] = mid[rows, :] + norm_back(up, unit, inv, gain_one)

        loop(R // SUB, sub)
        rows = aligned(r, R)
        pltpu.make_async_copy(mid.at[rows, :], pgrad_h.at[rows, :], xs.at[r]).start()

    loop(blocks, first_back)
    if fuse:
        early_two()
        ff.finish4(3)
        thrice(pq.finish3, 0)
        pq.finish1(3, 0)
        pq.finish1(3, 1)
        pq.finish2(3, 0)
        thrice(pq.finish3, 1)
        pq.finish1(3, 2)
        small_copy(1, 1, peer1).wait()
        small[2, late] = small[1, late] + small_r[1, late]
        small_copy(2, 2, peer2).start()
        pq.finish2(3, 1)
        pq.finish2(3, 2)
        deep[0].finish4()
        deep[1].finish4()
        early_three()
        small_copy(2, 2, peer2).wait()
        small[3, late] = small[2, late] + small_r[2, late]
        copies = [small_copy(3 + k, 3, peers_z[k]) for k in range(3)]
        for copy in copies:
            copy.start()
        thrice(pq.finish3, 2)
        thrice(pq.finish3, 3)
        for copy in copies:
            copy.wait()
        small[4, late] = small[3, late] + (small_r[3, late] + small_r[4, late] + small_r[5, late])
    out_small = pltpu.make_async_copy(small.at[last], small_h, lsem.at[0])
    out_small.start()
    if fuse:
        deep[0].drain()
        deep[1].drain()
        loop(chunks - 2, ff.drain)
    else:
        loop(chunks, ff.drain)
    loop(pairs + 1, pq.drain)
    out_small.wait()

    def finish_out(r):
        rows = aligned(r, R)
        pltpu.make_async_copy(ns.at[rows, :], mixed_h.at[rows, :], ms.at[r]).wait()
        pltpu.make_async_copy(mid.at[rows, :], pgrad_h.at[rows, :], xs.at[r]).wait()

    loop(blocks, finish_out)


def main_call(fuse, parts, big, grids, freqs, bias_q, vectors):
    x, og, wp, we, wc, wq = big
    rows, width = x.shape
    heads = wq.shape[2]
    hidden = we.shape[1]
    pairs, chunks = heads // PAIR, hidden // CHUNK
    shape = jax.ShapeDtypeStruct
    part_rows = width // parts
    sent = parts if fuse else 0
    if fuse:
        ff_shape, pq_shape = (chunks, part_rows, 2 * CHUNK), (pairs + 1, part_rows, 3 * PAIR)
        grain = (parts, part_rows)
        slots = chunks
    else:
        ff_shape, pq_shape = (chunks, 1, width, 2 * CHUNK), (pairs + 1, 1, width, 3 * PAIR)
        grain = (1, width)
        slots = 1
    outs = [
        shape((rows, width), BF16), shape((rows, width), F32), shape(ff_shape, F32),
        shape(pq_shape, F32), shape((16, width), F32), shape((rows, width), BF16),
        shape((rows, 2 * heads), F32),
    ]
    any_spec = pl.BlockSpec(memory_space=ANY)
    vm_spec = pl.BlockSpec(memory_space=pltpu.VMEM)
    V = pltpu.VMEM
    DMA = pltpu.SemaphoreType.DMA
    REG = pltpu.SemaphoreType.REGULAR
    blocks = rows // R
    lines = chunks + 3 * (pairs + 1)
    recv = (lambda n: V((slots, n, part_rows, 2 * CHUNK), F32)) if fuse else (lambda n: V((1, 1, 8, PAIR), F32))
    scratch = [
        V((rows, heads), F32), V((rows, heads), BF16), V((rows, heads), BF16), V((rows, heads), BF16),
        V((rows, PAIR), BF16), V((rows, PAIR), BF16), V((8, rows), F32), V((rows, PAIR), F32),
        V((rows, width), BF16), V((rows, width), BF16), V((heads, width), BF16),
        V((width, hidden), BF16), V((hidden, width), BF16),
        V((rows, width), F32), V((rows, width), F32), V((rows, width), F32), V((rows, width), F32),
        V((width, rows), BF16), V((rows, width), BF16), V((width, rows), BF16),
        V((rows, CHUNK), BF16), V((rows, CHUNK), BF16), V((rows, heads), BF16), V((8, rows), F32),
        V((rows, PAIR), BF16), V((rows, PAIR), BF16), V((heads, rows), BF16), V((PAIR, rows), BF16),
        V((rows, PAIR), F32), V((rows, PAIR), F32), V((PAIR, rows), F32), V((pairs, rows, 3 * PAIR), BF16),
        V((rows, PAIR), F32), V((rows, PAIR), F32), V((8, hidden), F32),
        V((chunks, *grain, 2 * CHUNK), F32), V((pairs + 1, *grain, 3 * PAIR), F32),
        recv(8), recv(4), recv(3), V((5, 16, width), F32), V((6, 16, width), F32),
        DMA((16,)), DMA((blocks,)), DMA((blocks,)), REG((blocks,)),
        DMA((lines,)), DMA((lines,)), DMA((lines,)), DMA((lines,)), DMA((lines,)), DMA((lines,)),
        REG((4,)), REG((4,)), REG((4,)), DMA((16,)), DMA((12,)), DMA((lines,)), DMA((4,)), DMA((chunks,)), DMA((chunks,)),
    ]
    return pl.pallas_call(
        partial(main_kernel, fuse, pairs, chunks),
        name="main",
        out_shape=outs,
        in_specs=[any_spec] * len(big)
        + [pl.BlockSpec(memory_space=pltpu.SMEM)]
        + [vm_spec] * (2 + len(vectors)),
        out_specs=[any_spec] * len(outs),
        scratch_shapes=scratch,
        compiler_params=pltpu.CompilerParams(
            collective_id=0, has_side_effects=True, vmem_limit_bytes=67043328
        ),
    )(*big, grids, freqs, bias_q, *vectors)


def finish_kernel(
    mixed_h, pgrad_h, ff_h, pq_h, small_h,
    mixed_o, pgrad_o, qkv_o, proj_o, expand_o, contract_o,
    *rest,
):
    tiny_o, (mixed, pgrad, ff, pq, small), tiny, (isem, osem, tsem) = (
        rest[:9], rest[9:14], rest[14:23], rest[23:],
    )
    gain_one, shift_one, bias_q, rope, bias_p, gain_two, shift_two, bias_e, bias_c = tiny
    blocks = mixed.shape[0] // R
    chunks, pairs = ff.shape[0], pq.shape[0] - 1
    jobs = [(small_h, small, [])]
    for src, buf, dst in ((pgrad_h, pgrad, pgrad_o), (mixed_h, mixed, mixed_o)):
        for r in range(blocks):
            part = (pl.ds(r * R, R), slice(None))
            jobs.append((src.at[part], buf.at[part], [(buf.at[part], dst.at[part])]))
    for j in range(chunks):
        cols = pl.ds(j * CHUNK, CHUNK)
        jobs.append((ff_h.at[j], ff.at[j], [
            (ff.at[j, :, pl.ds(0, CHUNK)], contract_o.at[:, cols]),
            (ff.at[j, :, pl.ds(CHUNK, CHUNK)], expand_o.at[:, cols]),
        ]))
    jobs.append((pq_h.at[0], pq.at[0], [(pq.at[0], proj_o)]))
    for p in range(pairs):
        jobs.append((pq_h.at[p + 1], pq.at[p + 1], [
            (pq.at[p + 1, :, pl.ds(k * PAIR, PAIR)], qkv_o.at[k, :, pl.ds(p * PAIR, PAIR)])
            for k in range(3)
        ]))
    gets = [pltpu.make_async_copy(a, b, isem.at[i]) for i, (a, b, _) in enumerate(jobs)]
    for get in gets:
        get.start()
    gets[0].wait()
    heads = bias_q.shape[1]
    for k, out in (
        (8, gain_one), (9, shift_one), (3, bias_p), (1, gain_two), (2, shift_two), (0, bias_c),
    ):
        out[...] = small[k, :]
    half = bias_e.shape[0] // 2
    bias_e[:half] = small[4, :half]
    bias_e[half:] = small[5, :half]
    bias_q[...] = small[10:13, :heads]
    for p in range(pairs):
        tile = small[8:16, p * PAIR : (p + 1) * PAIR]
        both = tile + pltpu.roll(tile, PAIR - HALF // 2, 1)
        rope[2 * p] = both[5:7, : HALF // 2]
        rope[2 * p + 1] = pltpu.roll(both, HALF, 1)[5:7, : HALF // 2]
    last = [pltpu.make_async_copy(a, b, tsem.at[i]) for i, (a, b) in enumerate(zip(tiny, tiny_o))]
    for put in last:
        put.start()
    puts = []
    for get, (_, _, todo) in list(zip(gets, jobs))[1:]:
        get.wait()
        for a, b in todo:
            puts.append(pltpu.make_async_copy(a, b, osem.at[len(puts)]))
            puts[-1].start()
    for put in puts + last:
        put.wait()


def finish(mixed, pgrad, ff, pq, small, hidden):
    rows, width = mixed.shape
    mine = ff.shape[1]
    heads = pq.shape[2]
    shape = lambda *s: jax.ShapeDtypeStruct(s, F32)
    outs = [
        jax.ShapeDtypeStruct((rows, width), BF16), shape(rows, width), shape(3, mine, heads),
        shape(mine, heads), shape(mine, hidden), shape(mine, hidden), shape(width), shape(width),
        shape(3, heads), shape(heads // HALF, 2, HALF // 2), shape(width), shape(width),
        shape(width), shape(hidden), shape(width),
    ]
    any_spec = pl.BlockSpec(memory_space=ANY)
    reads = 1 + 2 * (rows // R) + ff.shape[0] + pq.shape[0]
    writes = 2 * (rows // R) + 2 * ff.shape[0] + 3 * pq.shape[0] - 2
    big = (mixed, pgrad, ff, pq, small)
    return pl.pallas_call(
        finish_kernel,
        name="finish",
        out_shape=outs,
        in_specs=[any_spec] * 5,
        out_specs=[any_spec] * len(outs),
        scratch_shapes=[pltpu.VMEM(v.shape, v.dtype) for v in (*big, *outs[6:])]
        + [pltpu.SemaphoreType.DMA((n,)) for n in (reads, writes, 9)],
        compiler_params=pltpu.CompilerParams(vmem_limit_bytes=67043328),
    )(*big)


def body(
    fuse, parts,
    patches, image_grids, out_grad, first_gain, first_shift, qkv_weight, qkv_bias, rope_freqs,
    proj_weight, proj_bias, second_gain, second_shift, expand_weight, expand_bias,
    contract_weight, contract_bias,
):
    width = patches.shape[1]
    mixed, pgrad, ff, pq, small, _, _ = main_call(
        fuse,
        parts,
        (patches, out_grad, proj_weight, expand_weight, contract_weight, qkv_weight),
        image_grids.T,
        rope_freqs.transpose(1, 0, 2),
        qkv_bias,
        (first_gain, first_shift, proj_bias, second_gain, second_shift, expand_bias, contract_bias),
    )
    if not fuse:
        scatter = partial(lax.psum_scatter, axis_name="dp", scatter_dimension=1, tiled=True)
        ff = scatter(ff.reshape(ff.shape[0], width, ff.shape[-1]))
        pq = scatter(pq.reshape(pq.shape[0], width, pq.shape[-1]))
        small = lax.psum(small, "dp")
    (
        mixed, pgrad, qkv, proj, expand, contract, gain_one, shift_one, bias_q, rope,
        bias_p, gain_two, shift_two, bias_e, bias_c,
    ) = finish(mixed, pgrad, ff, pq, small, expand_bias.shape[0])
    return (
        mixed, pgrad, qkv, proj.T, expand, contract.T, gain_one, shift_one, bias_q,
        rope.transpose(1, 0, 2), bias_p, gain_two, shift_two, bias_e, bias_c,
    )


def solution(mesh):
    in_specs = (
        P("dp", None), P("dp", None), P("dp", None), P(), P(), P(None, None, "head"),
        P(None, "head"), P(None, "head", None), P("head", None), P(), P(), P(),
        P(None, "head"), P("head"), P("head", None), P(),
    )
    out_specs = (
        P("dp", None), P("dp", None), P(None, "dp", "head"), P("head", "dp"), P("dp", "head"),
        P("head", "dp"), P(), P(), P(None, "head"), P(None, "head", None), P(), P(), P(),
        P("head"), P(),
    )
    parts = mesh.shape["dp"]
    run = partial(body, parts == PARTS, parts)
    return jax.shard_map(run, mesh=mesh, in_specs=in_specs, out_specs=out_specs, check_vma=False)
```

```python
from functools import partial

import jax
import jax.numpy as jnp
from jax import lax
from jax.experimental import pallas as pl
from jax.experimental.pallas import tpu as pltpu
from jax.sharding import PartitionSpec as P

F32 = jnp.float32
BF16 = jnp.bfloat16
EPS = 1e-06
FAR = 2.0**100
R = 256
QR = 512
SUB = 64
PAIR = 128
HALF = 64
CHUNK = 256
MESH = pl.DeviceIdType.MESH
ANY = pl.ANY


def dot_nn(a, b):
    return lax.dot_general(a, b, (((1,), (0,)), ((), ())), preferred_element_type=F32)


def dot_nt(a, b):
    return lax.dot_general(a, b, (((1,), (1,)), ((), ())), preferred_element_type=F32)


def aligned(i, size):
    return pl.ds(pl.multiple_of(i * size, size), size)


def loop(count, fn):
    def step(i, carry):
        fn(i)
        return carry

    lax.fori_loop(0, count, step, 0)


def unit_of(rows):
    centred = rows - jnp.mean(rows, axis=-1, keepdims=True)
    inv = lax.rsqrt(jnp.mean(centred * centred, axis=-1, keepdims=True) + EPS)
    return centred * inv, inv


def norm_back(upstream, unit, inv, gain):
    scaled = upstream * gain
    return inv * (
        scaled
        - jnp.mean(scaled, axis=-1, keepdims=True)
        - unit * jnp.mean(scaled * unit, axis=-1, keepdims=True)
    )


def swap_halves(v, lane_first):
    return jnp.where(lane_first, pltpu.roll(v, PAIR - HALF // 2, 1), pltpu.roll(v, HALF // 2, 1))


def lane_ids(rows):
    return lax.broadcasted_iota(jnp.int32, (rows, PAIR), 1)


def head_mask(h):
    lane = lax.broadcasted_iota(jnp.int32, (1, PAIR), 1)
    return (lane // HALF == h).astype(F32)


def pieces(table):
    high = table.astype(BF16)
    rest = table - high.astype(F32)
    mid = rest.astype(BF16)
    low = (rest - mid.astype(F32)).astype(BF16)
    return jnp.concatenate([high, mid, low], axis=0)


def front_place(grids, slots, freqs, ohq, ohk, cossin, pos):
    rows_all, width_all = pos.shape[0], freqs[0].shape[1]
    side = lax.broadcasted_iota(jnp.int32, (32, 1), 0).astype(F32)
    ang_r = side * freqs[0]
    ang_c = side * freqs[1]
    table_r = pieces(jnp.concatenate([jnp.cos(ang_r), jnp.sin(ang_r)], axis=1))
    table_c = pieces(jnp.concatenate([jnp.cos(ang_c), jnp.sin(ang_c)], axis=1))

    def place(r):
        rows = aligned(r, 256)
        t = lax.broadcasted_iota(jnp.int32, (256, 1), 0) + r * 256
        seg = jnp.zeros((256, 1), jnp.int32)
        start = jnp.zeros((256, 1), jnp.int32)
        width = jnp.ones((256, 1), jnp.int32)
        end = jnp.int32(0)
        for s in range(slots):
            begun = t >= end
            start = jnp.where(begun, end, start)
            width = jnp.where(begun, jnp.maximum(grids[1, s], 1), width)
            end = end + grids[0, s] * grids[1, s]
            seg = jnp.where(t >= end, s + 1, seg)
        real = (seg < slots).astype(F32)
        off = (t - start).astype(F32)
        wide = width.astype(F32)
        grow = jnp.floor((off + 0.5) / wide) * real
        gcol = (off - grow * wide) * real
        lane = lane_ids(256)
        pos[rows, :] = jnp.where(lane == 0, real, jnp.where(lane == 1, grow, gcol))
        hot = lane % HALF == seg
        ohq[rows, :] = jnp.where(hot, 1.0, 0.0).astype(BF16)
        ohk[rows, :] = jnp.where(hot, 0.0, -FAR).astype(BF16)
        spot = (lax.broadcasted_iota(jnp.int32, (256, 96), 1) % 32).astype(F32)
        got_r = dot_nn(jnp.where(spot == grow, 1.0, 0.0).astype(BF16), table_r)
        got_c = dot_nn(jnp.where(spot == gcol, 1.0, 0.0).astype(BF16), table_c)
        cr, sr = got_r[:, :width_all], got_r[:, width_all:]
        cc, sc = got_c[:, :width_all], got_c[:, width_all:]
        cossin[rows, :width_all] = cr * cc - sr * sc
        cossin[rows, width_all:] = sr * cc + cr * sc

    loop(rows_all // 256, place)


def front_rows(x, gain, shift, w, b, q8, key, val, nf, cossin):
    rows_all, width_all = q8.shape
    pairs = width_all // PAIR

    def norm(r):
        rows = aligned(r, SUB)
        unit, _ = unit_of(x[rows, :].astype(F32))
        nf[rows, :] = (unit * gain + shift).astype(BF16)

    loop(rows_all // SUB, norm)

    def project(r):
        rows = aligned(r, QR)
        lane_first = lane_ids(QR) % HALF < HALF // 2
        sign = jnp.where(lane_first, -1.0, 1.0)
        for k, out in ((0, q8), (1, key)):
            got = dot_nn(nf[rows, :], w[:, k * width_all : (k + 1) * width_all]) + b[k : k + 1, :]
            for p in range(pairs):
                cols = slice(p * PAIR, (p + 1) * PAIR)
                part = got[:, cols]
                turned = part * cossin[rows, cols] + swap_halves(part, lane_first) * (
                    cossin[rows, width_all + p * PAIR : width_all + (p + 1) * PAIR] * sign
                )
                turned = turned.astype(BF16)
                if k == 0:
                    turned = turned * jnp.asarray(HALF**-0.5, BF16)
                out[rows, cols] = turned
        got = dot_nn(nf[rows, :], w[:, 2 * width_all : 3 * width_all])
        val[rows, :] = (got + b[2:3, :]).astype(BF16)

    loop(rows_all // QR, project)


def front_heads(q8, key, val, ohq, ohk, att, kxs, scs, lcol, after):
    rows_all, width_all = q8.shape
    blocks, pieces_all, wide = rows_all // QR, rows_all // R, scs[0].shape[1] // R
    masks = [head_mask(h).astype(BF16) for h in range(2)]

    def piece(h, k):
        at = (k // wide) * QR
        return scs[h].at[at : at + QR, (k % wide) * R : (k % wide + 1) * R]

    pairs = width_all // PAIR

    def keys(h, p):
        kxs[h][...] = key[:, aligned(p, PAIR)] * masks[h] + ohk[...] * masks[1 - h]

    def scores(h, r, p):
        rows = aligned(r, QR)
        qx = q8[rows, aligned(p, PAIR)] * masks[h] + ohq[rows, :] * masks[1 - h]
        for k in range(pieces_all):
            piece(h, k)[...] = dot_nt(qx, kxs[h][k * R : (k + 1) * R, :])

    def weigh(h, r, p):
        rows, cols = aligned(r, QR), aligned(p, PAIR)
        top = piece(h, 0)[...]
        for k in range(1, pieces_all):
            top = jnp.maximum(top, piece(h, k)[...])
        top = jnp.max(top, axis=-1, keepdims=True)
        total = jnp.zeros((QR, PAIR), F32)
        got = jnp.zeros((QR, PAIR), F32)
        for k in range(pieces_all):
            grown = jnp.exp(piece(h, k)[...] - top)
            for m in range(R // PAIR):
                total = total + grown[:, m * PAIR : (m + 1) * PAIR]
            got = got + dot_nn(grown.astype(BF16), val[k * R : (k + 1) * R, cols])
        total = jnp.sum(total, axis=-1, keepdims=True)
        got = got * (1.0 / total)
        lane = lane_ids(QR)
        if h == 0:
            att[rows, cols] = got
        else:
            att[rows, cols] = jnp.where(lane < HALF, att[rows, cols], got)
        lcol[rows, :] = jnp.where(lane == p * 2 + h, top + jnp.log(total), lcol[rows, :])

    keys(0, 0)
    keys(1, 0)
    scores(0, 0, 0)

    def half(r):
        def step(p):
            n = jnp.minimum(r * pairs + p + 1, blocks * pairs - 1)
            scores(1, r, p)
            weigh(0, r, p)
            keys(0, n % pairs)
            scores(0, n // pairs, n % pairs)
            weigh(1, r, p)
            keys(1, n % pairs)

        loop(pairs, step)
        after(r)

    loop(blocks, half)


PARTS = 16


def main_kernel(
    fuse, pairs, chunks,
    x_h, og_h, wp_h, we_h, wc_h, wq_h,
    grids, freqs, bias_q, *rest,
):
    (
    gain_one, shift_one, bias_p, gain_two, shift_two, bias_e, bias_c,
    mixed_h, pgrad_h, ff_h, pq_h, small_h, nf_h, cossin_h,
    att, q8, key, val, ohq, ohk, lse, pos, x, cot, wp, we, wc,
    acc_a, acc_b, xbuf, mid, cott, ns, nst, act, hgb, dgrad, delta,
    km, vm, kt, kmt, dk, dv, dqt, qkvg, cos, sin, sums,
    gf, gq, r1, r2, r3, small, small_r,
    lsem, xs, xr, credit, s1, e1, s2, e2, s3, e3, c1, c2, c3, ms, mr, osem, zs, s4, e4,
    ) = rest
    gain_one, shift_one, bias_p, gain_two, shift_two, bias_e, bias_c = (
        v[...].reshape(1, -1)
        for v in (gain_one, shift_one, bias_p, gain_two, shift_two, bias_e, bias_c)
    )
    me = lax.axis_index("dp")
    core = lax.axis_index("head")
    blocks = x.shape[0] // R
    subs = x.shape[0] // SUB
    mate = (me, 1 - core)
    if fuse:
        xx, yy, zz = me % 2, (me // 2) % 2, me // 4
        fst = xx * (1 - core) + yy * core
        snd = yy * (1 - core) + xx * core
        peer1 = (me + (1 - 2 * fst) * (1 + core), core)
        peer2 = (me + (1 - 2 * snd) * (2 - core), core)
        peers_z = [(((zz + j) % 4) * 4 + me % 4, core) for j in (1, 2, 3)]
        odd, across = zz % 2, (zz + 2) % 4
        near = ((zz + 1 - 2 * odd) * 4 + me % 4, core)
        far = (across * 4 + me % 4, core)

        def where(z, f, s):
            return z * 4 + s * (2 - core) + f * (1 + core)

    def load(src, dst, i):
        copy = pltpu.make_async_copy(src, dst, lsem.at[i])
        copy.start()
        return copy

    heads = q8.shape[1]
    slots = grids.shape[1]
    get_x = load(x_h, x, 4)
    get_wq = [load(wq_h.at[k], we.at[:, pl.ds(k * heads, heads)], 7 + k) for k in range(3)]
    get_wp = load(wp_h, wp, 1)
    get_og = load(og_h, cot, 2)
    get_wc = load(wc_h, wc, 6)

    barrier = pltpu.get_barrier_semaphore()
    friends = [mate] + ([peer1, peer2] + peers_z if fuse else [])
    for friend in friends:
        pl.semaphore_signal(barrier, inc=1, device_id=friend, device_id_type=MESH)

    def exchange(src, r):
        return pltpu.make_async_remote_copy(
            src.at[aligned(r, R), :], xbuf.at[aligned(r, R), :], xs.at[r], xr.at[r],
            device_id=mate, device_id_type=MESH,
        )

    def send(src, r):
        exchange(src, r).start()

    def give_credit(r):
        pl.semaphore_signal(credit.at[r], inc=1, device_id=mate, device_id_type=MESH)

    def take_credit(r):
        pl.semaphore_wait(credit.at[r], 1)

    def remote(src, dst, ss, rs, peer):
        return pltpu.make_async_remote_copy(
            src, dst, ss, rs, device_id=peer, device_id_type=MESH
        )

    class Line:
        def __init__(self, grads, base, width, out, guard, parts):
            self.g, self.base, self.out, self.guard = grads, base, out, guard
            self.n, self.parts = width // parts, parts

        def cols(self, k):
            return pl.ds(k * self.n, self.n)

        def at(self, j, k):
            return self.base + j * self.parts + k

        def step(self, j, k, first, src, dst, ss, rs, peer):
            i = self.at(j, k)
            return remote(
                self.g.at[j, src, :, self.cols(k)], first.at[j, dst, :, self.cols(k)],
                ss.at[i], rs.at[i], peer,
            )

        def whole(self, j, k, n, ss, rs, buf, peer):
            return self.step(j, k, buf, pl.ds(0, n), pl.ds(0, n), ss, rs, peer)

        def add(self, j, k, b, got):
            c = self.cols(k)
            self.g[j, b, :, c] = self.g[j, b, :, c] + got

        def start1(self, j):
            if self.guard == "take":
                pl.semaphore_wait(c1.at[j], 1)
            for k in range(self.parts):

                def one(i, k=k):
                    b = where(i // 2, 1 - fst, i % 2)
                    self.step(j, k, r1, b, i, s1, e1, peer1).start()

                loop(8, one)

        def give(self, sem, j, peers):
            if self.guard == "give":
                def go():
                    for peer in peers:
                        pl.semaphore_signal(sem.at[j], inc=1, device_id=peer, device_id_type=MESH)
                if isinstance(j, int):
                    if j < 4:
                        go()
                else:
                    pl.when(j < 4)(go)

        def finish1(self, j, k=0):
            self.whole(j, k, 8, s1, e1, r1, peer1).wait_recv()
            c = self.cols(k)

            def one(i):
                self.add(j, k, where(i // 2, fst, i % 2), r1[j, i, :, c])

            loop(8, one)
            self.give(c1, j, [peer1])
            if self.guard == "take" and k == 0:
                pl.semaphore_wait(c2.at[j], 1)

            def two(i):
                self.step(j, k, r2, where(i, fst, 1 - snd), i, s2, e2, peer2).start()

            loop(4, two)

        def finish2(self, j, k=0):
            self.whole(j, k, 4, s2, e2, r2, peer2).wait_recv()
            c = self.cols(k)

            def one(i):
                self.add(j, k, where(i, fst, snd), r2[j, i, :, c])

            loop(4, one)
            self.give(c2, j, [peer2])
            if self.guard == "take" and k == 0:
                pl.semaphore_wait(c3.at[j], 3)
            for m in range(3):
                b = where((zz + m + 1) % 4, fst, snd)
                self.step(j, k, r3, b, m, s3, e3, peers_z[m]).start()

        def result(self, j, k):
            c = self.cols(k)
            return pltpu.make_async_copy(
                self.g.at[j, me, :, c], self.out.at[j, :, c], osem.at[self.at(j, k)]
            )

        def finish3(self, j, k=0):
            self.whole(j, k, 3, s3, e3, r3, peers_z[0]).wait_recv()
            c = self.cols(k)
            self.add(j, k, me, r3[j, 0, :, c] + r3[j, 1, :, c] + r3[j, 2, :, c])
            self.give(c3, j, peers_z)
            self.result(j, k).start()

        def drain(self, j):
            for k in range(self.parts):
                self.whole(j, k, 8, s1, e1, r1, peer1).wait_send()
                self.whole(j, k, 4, s2, e2, r2, peer2).wait_send()
                self.whole(j, k, 3, s3, e3, r3, peers_z[0]).wait_send()
                self.result(j, k).wait()

    class Two(Line):
        def finish2(self, j, k=0):
            self.whole(j, k, 4, s2, e2, r2, peer2).wait_recv()
            c = self.cols(k)

            def one(i):
                self.add(j, k, where(i, fst, snd), r2[j, i, :, c])

            loop(4, one)
            self.give(c2, j, [peer2])
            for m in range(2):
                b = where(1 - odd + 2 * m, fst, snd)
                self.step(j, k, r3, b, m, s3, e3, near).start()

        def finish3(self, j, k=0):
            self.whole(j, k, 2, s3, e3, r3, near).wait_recv()
            c = self.cols(k)
            for m in range(2):
                self.add(j, k, where(odd + 2 * m, fst, snd), r3[j, m, :, c])
            self.step(j, k, r3, where(across, fst, snd), 2, s4, e4, far).start()

        def finish4(self, j, k=0):
            self.step(j, k, r3, 0, 2, s4, e4, far).wait_recv()
            self.add(j, k, me, r3[j, 2, :, self.cols(k)])
            self.give(c3, j, peers_z)
            self.result(j, k).start()

        def drain(self, j):
            for k in range(self.parts):
                self.whole(j, k, 8, s1, e1, r1, peer1).wait_send()
                self.whole(j, k, 4, s2, e2, r2, peer2).wait_send()
                self.whole(j, k, 2, s3, e3, r3, near).wait_send()
                self.step(j, k, r3, 0, 2, s4, e4, far).wait_send()
                self.result(j, k).wait()

    class Deep:
        def __init__(self, grads, j, out, line):
            self.g, self.j, self.out, self.line = grads, j, out, line

        def one(self):
            j = self.j
            return remote(self.g.at[j, pl.ds(0, 8)], r1.at[j], s1.at[j], e1.at[j], near)

        def two(self):
            j = self.j
            return remote(self.g.at[j, pl.ds(across * 4, 4)], r2.at[j], s2.at[j], e2.at[j], far)

        def three(self):
            j = self.j
            return remote(
                self.g.at[j, pl.ds(0, 2)], r3.at[j, pl.ds(0, 2)], s3.at[j], e3.at[j], peer1
            )

        def four(self):
            return remote(
                self.g.at[self.j, where(zz, fst, 1 - snd)], r3.at[self.j, 2],
                zs.at[2 * self.line], zs.at[2 * self.line + 1], peer2,
            )

        def result(self):
            return pltpu.make_async_copy(
                self.g.at[self.j, me], self.out.at[self.j], osem.at[self.j]
            )

        def start(self):
            j = self.j
            for m in range(2):
                remote(
                    self.g.at[j, pl.ds((1 - odd + 2 * m) * 4, 4)], r1.at[j, pl.ds(4 * m, 4)],
                    s1.at[j], e1.at[j], near,
                ).start()

        def finish1(self):
            j = self.j
            self.one().wait_recv()

            def add(i):
                b = (odd + 2 * (i // 4)) * 4 + i % 4
                self.g[j, b] = self.g[j, b] + r1[j, i]

            loop(8, add)
            self.two().start()

        def finish2(self):
            j = self.j
            self.two().wait_recv()

            def add(i):
                self.g[j, zz * 4 + i] = self.g[j, zz * 4 + i] + r2[j, i]

            loop(4, add)
            for s in range(2):
                remote(
                    self.g.at[j, where(zz, 1 - fst, s)], r3.at[j, s], s3.at[j], e3.at[j], peer1
                ).start()

        def finish3(self):
            j = self.j
            self.three().wait_recv()
            for s in range(2):
                b = where(zz, fst, s)
                self.g[j, b] = self.g[j, b] + r3[j, s]
            self.four().start()

        def finish4(self):
            self.four().wait_recv()
            self.g[self.j, me] = self.g[self.j, me] + r3[self.j, 2]
            self.result().start()

        def drain(self):
            for copy in (self.one(), self.two(), self.three(), self.four()):
                copy.wait_send()
            self.result().wait()

    class Plain:
        def __init__(self, grads, base, width, out, guard, parts):
            self.g, self.base, self.out = grads, base, out

        def copy(self, j):
            return pltpu.make_async_copy(self.g.at[j], self.out.at[j], osem.at[self.base + j])

        def start1(self, j):
            self.copy(j).start()

        def finish1(self, j):
            pass

        finish2 = finish3 = finish1

        def drain(self, j):
            self.copy(j).wait()

    kind = Line if fuse else Plain
    ff = (Two if fuse else Plain)(gf, 0, 2 * CHUNK, ff_h, "give", 1)
    pq = kind(gq, chunks, 3 * PAIR, pq_h, "take", 3)
    deep = [Deep(gf, chunks - 1 - n, ff_h, n) for n in range(2)]

    small[...] = jnp.zeros_like(small)
    sums[...] = jnp.zeros_like(sums)
    sums[7:8, :] = bias_e

    turns = []
    for axis in range(2):
        lines = [freqs[n, axis : axis + 1, :] for n in range(heads // HALF) for _ in range(2)]
        turns.append(jnp.concatenate(lines, axis=1))
    front_place(grids, slots, turns, ohq, ohk, acc_b, pos)
    put_cossin = load(acc_b.at[:, pl.ds(0, 2 * heads)], cossin_h, 11)
    get_x.wait()
    for copy in get_wq:
        copy.wait()
    front_rows(x, gain_one, shift_one, we, bias_q, q8, key, val, ns, acc_b)
    get_we = load(we_h, we, 5)
    put_nf = load(ns, nf_h, 10)
    put_cossin.wait()
    get_wp.wait()
    pl.semaphore_wait(barrier, len(friends))

    def project(r):
        for n in range(QR // R):
            rows = aligned(r * (QR // R) + n, R)
            acc_a[rows, :] = dot_nn(att[rows, :].astype(BF16), wp[...])
            send(acc_a, r * (QR // R) + n)

    front_heads(q8, key, val, ohq, ohk, att, (km, vm), (mid, acc_b), dk, project)

    def turn(r):
        rows = aligned(r, PAIR)
        lse[:, rows] = jnp.transpose(dk[rows, :])[: lse.shape[0], :]

    loop(x.shape[0] // PAIR, turn)

    get_og.wait()

    def mask_cot(r):
        rows = aligned(r, R)
        block = (cot[rows, :].astype(F32) * pos[rows, 0:1])
        small[0, 0:1, :] = small[0, 0:1, :] + jnp.sum(block, axis=0, keepdims=True)
        low = block.astype(BF16)
        cot[rows, :] = low
        cott[:, rows] = jnp.transpose(low)

    loop(blocks, mask_cot)
    put_nf.wait()

    def second_norm(r):
        exchange(acc_a, r).wait()

        def sub(i):
            rows = pl.ds(pl.multiple_of(r * R + i * SUB, SUB), SUB)
            middle = x[rows, :].astype(F32) + ((acc_a[rows, :] + xbuf[rows, :]) + bias_p)
            unit, _ = unit_of(middle)
            mid[rows, :] = middle
            ns[rows, :] = (unit * gain_two + shift_two).astype(BF16)
            acc_b[rows, :] = 0.5 * (middle + bias_c)
            acc_a[rows, :] = jnp.zeros_like(middle)

        loop(R // SUB, sub)
        give_credit(r)
        nst[:, aligned(r, R)] = jnp.transpose(ns[aligned(r, R), :])

    loop(blocks, second_norm)
    get_we.wait()
    get_wc.wait()

    def feed(i):
        none, upto = 1 - (i + chunks - 1) // chunks, 1 - (i + chunks - 3) // chunks
        j = (i - 2) * (1 - upto) + (chunks - i) * (upto - none)
        cols = aligned(j, CHUNK)

        def rows_of(r):
            rows = aligned(r, QR)
            hidden = dot_nn(ns[rows, :], we[:, cols]) + sums[7:8, cols]
            upstream = dot_nt(cot[rows, :], wc[cols, :])
            phi = 0.5 * (1.0 + lax.erf(hidden * (0.5**0.5)))
            slope = phi + hidden * (jnp.exp(-0.5 * hidden * hidden) * (0.3989422804014327))
            active = (hidden * phi).astype(BF16)
            hgrad = (upstream * slope).astype(BF16)
            act[rows, :] = active
            hgb[rows, :] = hgrad
            sums[0:1, cols] = sums[0:1, cols] + jnp.sum(hgrad.astype(F32), axis=0, keepdims=True)
            acc_b[rows, :] = acc_b[rows, :] + dot_nn(active, wc[cols, :])
            acc_a[rows, :] = acc_a[rows, :] + dot_nt(hgrad, we[:, cols])

            def leave():
                for n in range(QR // R):
                    take_credit(r * (QR // R) + n)
                    send(acc_a, r * (QR // R) + n)

            pl.when(i == chunks - 1)(leave)

        loop(x.shape[0] // QR, rows_of)
        got = dot_nn(cott[...], act[...])
        gf[j, :, :, pl.ds(0, CHUNK)] = got.reshape(gf.shape[1], gf.shape[2], CHUNK)
        got = dot_nn(nst[...], hgb[...])
        gf[j, :, :, pl.ds(CHUNK, CHUNK)] = got.reshape(gf.shape[1], gf.shape[2], CHUNK)
        if fuse:
            pl.when(i == 1)(deep[0].start)
            pl.when(i == 2)(deep[1].start)
            pl.when((i != 1) & (i != 2))(lambda: ff.start1(j))
            pl.when(i == 4)(lambda: ff.finish1(0))
        else:
            ff.start1(j)

    loop(chunks, feed)
    if fuse:
        deep[0].finish1()
        ff.finish1(1)

    get_nf = load(nf_h, ns, 0)
    get_wq = [
        load(wq_h.at[k], we.at[:, pl.ds(k * pairs * PAIR, pairs * PAIR)], 4 + k) for k in range(3)
    ]
    kt[...] = jnp.transpose(key[...])
    get_nf.wait()

    def turn_first(r):
        nst[:, aligned(r, R)] = jnp.transpose(ns[aligned(r, R), :])

    loop(blocks, turn_first)

    def second_back(r):
        exchange(acc_a, r).wait()

        def sub(i):
            rows = pl.ds(pl.multiple_of(r * R + i * SUB, SUB), SUB)
            up = acc_a[rows, :] + xbuf[rows, :]
            unit, inv = unit_of(mid[rows, :])
            small[0, 1:2, :] = small[0, 1:2, :] + jnp.sum(up * unit, axis=0, keepdims=True)
            small[0, 2:3, :] = small[0, 2:3, :] + jnp.sum(up, axis=0, keepdims=True)
            grad = cot[rows, :].astype(F32) + norm_back(up, unit, inv, gain_two)
            mid[rows, :] = grad
            low = grad.astype(BF16)
            cot[rows, :] = low
            small[0, 3:4, :] = small[0, 3:4, :] + jnp.sum(
                low.astype(F32), axis=0, keepdims=True
            )

        loop(R // SUB, sub)
        give_credit(r)
        rows = aligned(r, R)
        cott[:, rows] = jnp.transpose(cot[rows, :])
        low = dot_nt(cot[rows, :], wp[...]).astype(BF16)
        dgrad[rows, :] = low
        prod = low.astype(F32) * att[rows, :]
        head = lax.broadcasted_iota(jnp.int32, (8, prod.shape[1]), 0)
        lane = lax.broadcasted_iota(jnp.int32, (8, prod.shape[1]), 1)
        pick = (lane // HALF == head).astype(F32)
        delta[:, rows] = lax.dot_general(
            pick, prod, (((1,), (1,)), ((), ())), precision=lax.Precision.HIGHEST,
            preferred_element_type=F32,
        )

    loop(blocks, second_back)
    if fuse:
        ff.finish2(0)

    def small_copy(i, k, peer, late=1):
        rows = pl.ds(8 * late, 8)
        return remote(
            small.at[k, rows], small_r.at[i, rows], ms.at[4 + 6 * late + i], mr.at[6 * late + i],
            peer,
        )

    early, late = slice(0, 8), slice(8, 16)
    n = chunks * CHUNK // 2
    small[0, 4:5, :] = sums[0:1, 0:n]
    small[0, 5:6, :] = sums[0:1, n : 2 * n]
    small[1, early] = small[0, early]

    def early_one():
        small_copy(1, 1, peer1, 0).wait()
        small[2, early] = small[1, early] + small_r[1, early]
        small_copy(2, 2, peer2, 0).start()

    def early_two():
        small_copy(2, 2, peer2, 0).wait()
        small[3, early] = small[2, early] + small_r[2, early]
        for k in range(3):
            small_copy(3 + k, 3, peers_z[k], 0).start()

    def early_three():
        for k in range(3):
            small_copy(3 + k, 3, peers_z[k], 0).wait()
        small[4, early] = small[3, early] + (small_r[3, early] + small_r[4, early] + small_r[5, early])

    if fuse:
        small_copy(1, 1, peer1, 0).start()
    gq[0] = dot_nn(cott[...], att[...].astype(BF16)).reshape(gq.shape[1:])
    pq.start1(0)
    if fuse:
        ff.finish1(2)

    def send_mixed(r):
        take_credit(r)
        send(acc_b, r)

    loop(blocks, send_mixed)

    def mixed_block(r):
        exchange(acc_b, r).wait()
        rows = aligned(r, R)
        ns[rows, :] = (acc_b[rows, :] + xbuf[rows, :]).astype(BF16)
        give_credit(r)
        pltpu.make_async_copy(ns.at[rows, :], mixed_h.at[rows, :], ms.at[r]).start()

    def thrice(step, j):
        for k in range(3):
            step(j, k)

    def gap0():
        ff.finish2(1)

    def gap1():
        deep[1].finish1()
        ff.finish1(3)

    def gap2():
        deep[0].finish2()
        ff.finish3(0)
        ff.finish2(2)

    def gap3():
        thrice(pq.finish1, 0)
        ff.finish3(1)

    def gap4():
        deep[1].finish2()
        ff.finish2(3)
        ff.finish4(0)

    def gap5():
        thrice(pq.finish2, 0)
        thrice(pq.finish1, 1)
        early_one()

    between = (gap0, gap1, gap2, gap3, gap4, gap5)

    def pair_back(p):
        cols = aligned(p, PAIR)
        get_cos = load(cossin_h.at[:, cols], cos, 0)
        get_sin = load(cossin_h.at[:, aligned(pairs + p, PAIR)], sin, 1)
        dk[...] = jnp.zeros_like(dk)
        dv[...] = jnp.zeros_like(dv)
        dqt[...] = jnp.zeros_like(dqt)

        def head_back(h):
            mine = head_mask(h).astype(BF16)
            other = head_mask(1 - h).astype(BF16)
            km[...] = key[:, cols] * mine + ohk[...] * other
            vm[...] = val[:, cols] * mine
            spot = lax.broadcasted_iota(jnp.int32, (PAIR, 1), 0)
            kmt[...] = kt[cols, :] * (spot // HALF == h).astype(F32).astype(BF16)
            n = p * 2 + h

            def query_back(r):
                rows = aligned(r, R)
                qm = q8[rows, cols] * mine
                qx = qm + ohq[rows, :] * other
                do = dgrad[rows, cols]
                score = dot_nt(km[...], qx)
                prob = jnp.exp(score - lse[pl.ds(n, 1), rows])
                pgrad = dot_nt(vm[...], do)
                sgrad = (prob * (pgrad - delta[pl.ds(n, 1), rows])).astype(BF16)
                dv[...] = dv[...] + dot_nn(prob.astype(BF16), do * mine)
                dk[...] = dk[...] + dot_nn(sgrad, qm)
                dqt[:, rows] = dqt[:, rows] + dot_nn(kmt[...], sgrad)

            loop(blocks, query_back)
            if fuse:
                for q in range(3):
                    pl.when(p == q)(lambda q=q: between[2 * q + h]())

        head_back(0)
        head_back(1)
        get_cos.wait()
        get_sin.wait()

        def turn_back(r):
            rows = aligned(r, R)
            lane_first = lane_ids(R) % HALF < HALF // 2
            sign = jnp.where(lane_first, 1.0, -1.0)
            c, s = cos[rows, :], sin[rows, :]
            total = jnp.zeros((R, PAIR), F32)
            grads = []
            scale = HALF**-0.5
            for k, (grad, turned) in enumerate(
                (
                    (jnp.transpose(dqt[:, rows]) * scale, q8[rows, cols].astype(F32) * (1.0 / scale)),
                    (dk[rows, :], key[rows, cols].astype(F32)),
                )
            ):
                swapped = swap_halves(grad, lane_first) * sign
                total = total + swapped * turned
                grads.append((grad * c + swapped * s).astype(BF16))
            grads.append(dv[rows, :].astype(BF16))
            for k, low in enumerate(grads):
                qkvg[p, rows, k * PAIR : (k + 1) * PAIR] = low
                sums[k + 1 : k + 2, cols] = sums[k + 1 : k + 2, cols] + jnp.sum(
                    low.astype(F32), axis=0, keepdims=True
                )
            for k in range(2):
                sums[k + 4 : k + 5, cols] = sums[k + 4 : k + 5, cols] + jnp.sum(
                    total * pos[rows, k + 1 : k + 2], axis=0, keepdims=True
                )

        loop(blocks, turn_back)
        gq[p + 1] = dot_nn(nst[...], qkvg[p]).reshape(gq.shape[1:])
        pq.start1(p + 1)

    loop(pairs, pair_back)

    def first_send(r):
        def sub(i):
            rows = pl.ds(pl.multiple_of(r * R + i * SUB, SUB), SUB)
            unit, _ = unit_of(x[rows, :].astype(F32))
            up = acc_a[rows, :]
            small[0, 8:9, :] = small[0, 8:9, :] + jnp.sum(up * unit, axis=0, keepdims=True)
            small[0, 9:10, :] = small[0, 9:10, :] + jnp.sum(up, axis=0, keepdims=True)

        rows = aligned(r, R)
        total = jnp.zeros((R, acc_a.shape[1]), F32)
        for p in range(pairs):
            weight = jnp.concatenate(
                [we[:, (k * pairs + p) * PAIR : (k * pairs + p + 1) * PAIR] for k in range(3)],
                axis=1,
            )
            total = total + dot_nt(qkvg[p, rows, :], weight)
        acc_a[rows, :] = total
        take_credit(r)
        send(acc_a, r)
        loop(R // SUB, sub)

    if fuse:
        ff.finish3(2)
        ff.finish4(1)
        thrice(pq.finish2, 1)
        deep[0].finish3()
        pq.finish1(2, 0)
    loop(blocks, mixed_block)
    for copy in get_wq:
        copy.wait()
    loop(blocks, first_send)

    m = pairs * PAIR
    for k in range(5):
        small[0, 10 + k : 11 + k, 0:m] = sums[1 + k : 2 + k, 0:m]

    copy = small_copy(0, 0, mate)
    copy.start()
    if fuse:
        pq.finish1(2, 1)
        pq.finish1(2, 2)
        deep[1].finish3()
        ff.finish3(3)
        ff.finish4(2)
    copy.wait()
    line = lax.broadcasted_iota(jnp.int32, (8, small.shape[2]), 0)
    small[1, late] = small[0, late] + jnp.where(line < 2, small_r[0, late], 0.0)
    if fuse:
        small_copy(1, 1, peer1).start()
        thrice(pq.finish2, 2)
    last = 4 if fuse else 1

    def first_back(r):
        exchange(acc_a, r).wait()

        def sub(i):
            rows = pl.ds(pl.multiple_of(r * R + i * SUB, SUB), SUB)
            unit, inv = unit_of(x[rows, :].astype(F32))
            up = acc_a[rows, :] + xbuf[rows, :]
            mid[rows, :] = mid[rows, :] + norm_back(up, unit, inv, gain_one)

        loop(R // SUB, sub)
        rows = aligned(r, R)
        pltpu.make_async_copy(mid.at[rows, :], pgrad_h.at[rows, :], xs.at[r]).start()

    if fuse:
        early_two()
        ff.finish4(3)
        thrice(pq.finish3, 0)
        pq.finish1(3, 0)
        pq.finish1(3, 1)
        pq.finish2(3, 0)
        thrice(pq.finish3, 1)
        pq.finish1(3, 2)
        small_copy(1, 1, peer1).wait()
        small[2, late] = small[1, late] + small_r[1, late]
        small_copy(2, 2, peer2).start()
        pq.finish2(3, 1)
        pq.finish2(3, 2)
        deep[0].finish4()
        deep[1].finish4()
        early_three()
        small_copy(2, 2, peer2).wait()
        small[3, late] = small[2, late] + small_r[2, late]
        copies = [small_copy(3 + k, 3, peers_z[k]) for k in range(3)]
        for copy in copies:
            copy.start()
        loop(blocks, first_back)
        thrice(pq.finish3, 2)
        thrice(pq.finish3, 3)
        for copy in copies:
            copy.wait()
        small[4, late] = small[3, late] + (small_r[3, late] + small_r[4, late] + small_r[5, late])
    if not fuse:
        loop(blocks, first_back)
    out_small = pltpu.make_async_copy(small.at[last], small_h, lsem.at[0])
    out_small.start()
    if fuse:
        deep[0].drain()
        deep[1].drain()
        loop(chunks - 2, ff.drain)
    else:
        loop(chunks, ff.drain)
    loop(pairs + 1, pq.drain)
    out_small.wait()

    def finish_out(r):
        rows = aligned(r, R)
        pltpu.make_async_copy(ns.at[rows, :], mixed_h.at[rows, :], ms.at[r]).wait()
        pltpu.make_async_copy(mid.at[rows, :], pgrad_h.at[rows, :], xs.at[r]).wait()

    loop(blocks, finish_out)


def main_call(fuse, parts, big, grids, freqs, bias_q, vectors):
    x, og, wp, we, wc, wq = big
    rows, width = x.shape
    heads = wq.shape[2]
    hidden = we.shape[1]
    pairs, chunks = heads // PAIR, hidden // CHUNK
    shape = jax.ShapeDtypeStruct
    part_rows = width // parts
    sent = parts if fuse else 0
    if fuse:
        ff_shape, pq_shape = (chunks, part_rows, 2 * CHUNK), (pairs + 1, part_rows, 3 * PAIR)
        grain = (parts, part_rows)
        slots = chunks
    else:
        ff_shape, pq_shape = (chunks, 1, width, 2 * CHUNK), (pairs + 1, 1, width, 3 * PAIR)
        grain = (1, width)
        slots = 1
    outs = [
        shape((rows, width), BF16), shape((rows, width), F32), shape(ff_shape, F32),
        shape(pq_shape, F32), shape((16, width), F32), shape((rows, width), BF16),
        shape((rows, 2 * heads), F32),
    ]
    any_spec = pl.BlockSpec(memory_space=ANY)
    vm_spec = pl.BlockSpec(memory_space=pltpu.VMEM)
    V = pltpu.VMEM
    DMA = pltpu.SemaphoreType.DMA
    REG = pltpu.SemaphoreType.REGULAR
    blocks = rows // R
    lines = chunks + 3 * (pairs + 1)
    recv = (lambda n: V((slots, n, part_rows, 2 * CHUNK), F32)) if fuse else (lambda n: V((1, 1, 8, PAIR), F32))
    scratch = [
        V((rows, heads), F32), V((rows, heads), BF16), V((rows, heads), BF16), V((rows, heads), BF16),
        V((rows, PAIR), BF16), V((rows, PAIR), BF16), V((8, rows), F32), V((rows, PAIR), F32),
        V((rows, width), BF16), V((rows, width), BF16), V((heads, width), BF16),
        V((width, hidden), BF16), V((hidden, width), BF16),
        V((rows, width), F32), V((rows, width), F32), V((rows, width), F32), V((rows, width), F32),
        V((width, rows), BF16), V((rows, width), BF16), V((width, rows), BF16),
        V((rows, CHUNK), BF16), V((rows, CHUNK), BF16), V((rows, heads), BF16), V((8, rows), F32),
        V((rows, PAIR), BF16), V((rows, PAIR), BF16), V((heads, rows), BF16), V((PAIR, rows), BF16),
        V((rows, PAIR), F32), V((rows, PAIR), F32), V((PAIR, rows), F32), V((pairs, rows, 3 * PAIR), BF16),
        V((rows, PAIR), F32), V((rows, PAIR), F32), V((8, hidden), F32),
        V((chunks, *grain, 2 * CHUNK), F32), V((pairs + 1, *grain, 3 * PAIR), F32),
        recv(8), recv(4), recv(3), V((5, 16, width), F32), V((6, 16, width), F32),
        DMA((16,)), DMA((blocks,)), DMA((blocks,)), REG((blocks,)),
        DMA((lines,)), DMA((lines,)), DMA((lines,)), DMA((lines,)), DMA((lines,)), DMA((lines,)),
        REG((4,)), REG((4,)), REG((4,)), DMA((16,)), DMA((12,)), DMA((lines,)), DMA((4,)), DMA((chunks,)), DMA((chunks,)),
    ]
    return pl.pallas_call(
        partial(main_kernel, fuse, pairs, chunks),
        name="main",
        out_shape=outs,
        in_specs=[any_spec] * len(big)
        + [pl.BlockSpec(memory_space=pltpu.SMEM)]
        + [vm_spec] * (2 + len(vectors)),
        out_specs=[any_spec] * len(outs),
        scratch_shapes=scratch,
        compiler_params=pltpu.CompilerParams(
            collective_id=0, has_side_effects=True, vmem_limit_bytes=67043328
        ),
    )(*big, grids, freqs, bias_q, *vectors)


def finish_kernel(
    mixed_h, pgrad_h, ff_h, pq_h, small_h,
    mixed_o, pgrad_o, qkv_o, proj_o, expand_o, contract_o,
    *rest,
):
    tiny_o, (mixed, pgrad, ff, pq, small), tiny, (isem, osem, tsem) = (
        rest[:9], rest[9:14], rest[14:23], rest[23:],
    )
    gain_one, shift_one, bias_q, rope, bias_p, gain_two, shift_two, bias_e, bias_c = tiny
    blocks = mixed.shape[0] // R
    chunks, pairs = ff.shape[0], pq.shape[0] - 1
    jobs = [(small_h, small, [])]
    for src, buf, dst in ((pgrad_h, pgrad, pgrad_o), (mixed_h, mixed, mixed_o)):
        for r in range(blocks):
            part = (pl.ds(r * R, R), slice(None))
            jobs.append((src.at[part], buf.at[part], [(buf.at[part], dst.at[part])]))
    for j in range(chunks):
        cols = pl.ds(j * CHUNK, CHUNK)
        jobs.append((ff_h.at[j], ff.at[j], [
            (ff.at[j, :, pl.ds(0, CHUNK)], contract_o.at[:, cols]),
            (ff.at[j, :, pl.ds(CHUNK, CHUNK)], expand_o.at[:, cols]),
        ]))
    jobs.append((pq_h.at[0], pq.at[0], [(pq.at[0], proj_o)]))
    for p in range(pairs):
        jobs.append((pq_h.at[p + 1], pq.at[p + 1], [
            (pq.at[p + 1, :, pl.ds(k * PAIR, PAIR)], qkv_o.at[k, :, pl.ds(p * PAIR, PAIR)])
            for k in range(3)
        ]))
    gets = [pltpu.make_async_copy(a, b, isem.at[i]) for i, (a, b, _) in enumerate(jobs)]
    for get in gets:
        get.start()
    gets[0].wait()
    heads = bias_q.shape[1]
    for k, out in (
        (8, gain_one), (9, shift_one), (3, bias_p), (1, gain_two), (2, shift_two), (0, bias_c),
    ):
        out[...] = small[k, :]
    half = bias_e.shape[0] // 2
    bias_e[:half] = small[4, :half]
    bias_e[half:] = small[5, :half]
    bias_q[...] = small[10:13, :heads]
    for p in range(pairs):
        tile = small[8:16, p * PAIR : (p + 1) * PAIR]
        both = tile + pltpu.roll(tile, PAIR - HALF // 2, 1)
        rope[2 * p] = both[5:7, : HALF // 2]
        rope[2 * p + 1] = pltpu.roll(both, HALF, 1)[5:7, : HALF // 2]
    last = [pltpu.make_async_copy(a, b, tsem.at[i]) for i, (a, b) in enumerate(zip(tiny, tiny_o))]
    for put in last:
        put.start()
    puts = []
    for get, (_, _, todo) in list(zip(gets, jobs))[1:]:
        get.wait()
        for a, b in todo:
            puts.append(pltpu.make_async_copy(a, b, osem.at[len(puts)]))
            puts[-1].start()
    for put in puts + last:
        put.wait()


def finish(mixed, pgrad, ff, pq, small, hidden):
    rows, width = mixed.shape
    mine = ff.shape[1]
    heads = pq.shape[2]
    shape = lambda *s: jax.ShapeDtypeStruct(s, F32)
    outs = [
        jax.ShapeDtypeStruct((rows, width), BF16), shape(rows, width), shape(3, mine, heads),
        shape(mine, heads), shape(mine, hidden), shape(mine, hidden), shape(width), shape(width),
        shape(3, heads), shape(heads // HALF, 2, HALF // 2), shape(width), shape(width),
        shape(width), shape(hidden), shape(width),
    ]
    any_spec = pl.BlockSpec(memory_space=ANY)
    reads = 1 + 2 * (rows // R) + ff.shape[0] + pq.shape[0]
    writes = 2 * (rows // R) + 2 * ff.shape[0] + 3 * pq.shape[0] - 2
    big = (mixed, pgrad, ff, pq, small)
    return pl.pallas_call(
        finish_kernel,
        name="finish",
        out_shape=outs,
        in_specs=[any_spec] * 5,
        out_specs=[any_spec] * len(outs),
        scratch_shapes=[pltpu.VMEM(v.shape, v.dtype) for v in (*big, *outs[6:])]
        + [pltpu.SemaphoreType.DMA((n,)) for n in (reads, writes, 9)],
        compiler_params=pltpu.CompilerParams(vmem_limit_bytes=67043328),
    )(*big)


def body(
    fuse, parts,
    patches, image_grids, out_grad, first_gain, first_shift, qkv_weight, qkv_bias, rope_freqs,
    proj_weight, proj_bias, second_gain, second_shift, expand_weight, expand_bias,
    contract_weight, contract_bias,
):
    width = patches.shape[1]
    mixed, pgrad, ff, pq, small, _, _ = main_call(
        fuse,
        parts,
        (patches, out_grad, proj_weight, expand_weight, contract_weight, qkv_weight),
        image_grids.T,
        rope_freqs.transpose(1, 0, 2),
        qkv_bias,
        (first_gain, first_shift, proj_bias, second_gain, second_shift, expand_bias, contract_bias),
    )
    if not fuse:
        scatter = partial(lax.psum_scatter, axis_name="dp", scatter_dimension=1, tiled=True)
        ff = scatter(ff.reshape(ff.shape[0], width, ff.shape[-1]))
        pq = scatter(pq.reshape(pq.shape[0], width, pq.shape[-1]))
        small = lax.psum(small, "dp")
    (
        mixed, pgrad, qkv, proj, expand, contract, gain_one, shift_one, bias_q, rope,
        bias_p, gain_two, shift_two, bias_e, bias_c,
    ) = finish(mixed, pgrad, ff, pq, small, expand_bias.shape[0])
    return (
        mixed, pgrad, qkv, proj.T, expand, contract.T, gain_one, shift_one, bias_q,
        rope.transpose(1, 0, 2), bias_p, gain_two, shift_two, bias_e, bias_c,
    )


def solution(mesh):
    in_specs = (
        P("dp", None), P("dp", None), P("dp", None), P(), P(), P(None, None, "head"),
        P(None, "head"), P(None, "head", None), P("head", None), P(), P(), P(),
        P(None, "head"), P("head"), P("head", None), P(),
    )
    out_specs = (
        P("dp", None), P("dp", None), P(None, "dp", "head"), P("head", "dp"), P("dp", "head"),
        P("head", "dp"), P(), P(), P(None, "head"), P(None, "head", None), P(), P(), P(),
        P("head"), P(),
    )
    parts = mesh.shape["dp"]
    run = partial(body, parts == PARTS, parts)
    return jax.shard_map(run, mesh=mesh, in_specs=in_specs, out_specs=out_specs, check_vma=False)
```

```python
from functools import partial

import jax
import jax.numpy as jnp
from jax import lax
from jax.experimental import pallas as pl
from jax.experimental.pallas import tpu as pltpu
from jax.sharding import PartitionSpec as P

F32 = jnp.float32
BF16 = jnp.bfloat16
EPS = 1e-06
FAR = 2.0**100
R = 256
QR = 512
SUB = 64
PAIR = 128
HALF = 64
CHUNK = 256
MESH = pl.DeviceIdType.MESH
ANY = pl.ANY


def dot_nn(a, b):
    return lax.dot_general(a, b, (((1,), (0,)), ((), ())), preferred_element_type=F32)


def dot_nt(a, b):
    return lax.dot_general(a, b, (((1,), (1,)), ((), ())), preferred_element_type=F32)


def aligned(i, size):
    return pl.ds(pl.multiple_of(i * size, size), size)


def loop(count, fn):
    def step(i, carry):
        fn(i)
        return carry

    lax.fori_loop(0, count, step, 0)


def unit_of(rows):
    centred = rows - jnp.mean(rows, axis=-1, keepdims=True)
    inv = lax.rsqrt(jnp.mean(centred * centred, axis=-1, keepdims=True) + EPS)
    return centred * inv, inv


def norm_back(upstream, unit, inv, gain):
    scaled = upstream * gain
    return inv * (
        scaled
        - jnp.mean(scaled, axis=-1, keepdims=True)
        - unit * jnp.mean(scaled * unit, axis=-1, keepdims=True)
    )


def swap_halves(v, lane_first):
    return jnp.where(lane_first, pltpu.roll(v, PAIR - HALF // 2, 1), pltpu.roll(v, HALF // 2, 1))


def lane_ids(rows):
    return lax.broadcasted_iota(jnp.int32, (rows, PAIR), 1)


def head_mask(h):
    lane = lax.broadcasted_iota(jnp.int32, (1, PAIR), 1)
    return (lane // HALF == h).astype(F32)


def pieces(table):
    high = table.astype(BF16)
    rest = table - high.astype(F32)
    mid = rest.astype(BF16)
    low = (rest - mid.astype(F32)).astype(BF16)
    return jnp.concatenate([high, mid, low], axis=0)


def front_place(grids, slots, freqs, ohq, ohk, cossin, pos):
    rows_all, width_all = pos.shape[0], freqs[0].shape[1]
    side = lax.broadcasted_iota(jnp.int32, (32, 1), 0).astype(F32)
    ang_r = side * freqs[0]
    ang_c = side * freqs[1]
    table_r = pieces(jnp.concatenate([jnp.cos(ang_r), jnp.sin(ang_r)], axis=1))
    table_c = pieces(jnp.concatenate([jnp.cos(ang_c), jnp.sin(ang_c)], axis=1))

    def place(r):
        rows = aligned(r, 256)
        t = lax.broadcasted_iota(jnp.int32, (256, 1), 0) + r * 256
        seg = jnp.zeros((256, 1), jnp.int32)
        start = jnp.zeros((256, 1), jnp.int32)
        width = jnp.ones((256, 1), jnp.int32)
        end = jnp.int32(0)
        for s in range(slots):
            begun = t >= end
            start = jnp.where(begun, end, start)
            width = jnp.where(begun, jnp.maximum(grids[1, s], 1), width)
            end = end + grids[0, s] * grids[1, s]
            seg = jnp.where(t >= end, s + 1, seg)
        real = (seg < slots).astype(F32)
        off = (t - start).astype(F32)
        wide = width.astype(F32)
        grow = jnp.floor((off + 0.5) / wide) * real
        gcol = (off - grow * wide) * real
        lane = lane_ids(256)
        pos[rows, :] = jnp.where(lane == 0, real, jnp.where(lane == 1, grow, gcol))
        hot = lane % HALF == seg
        ohq[rows, :] = jnp.where(hot, 1.0, 0.0).astype(BF16)
        ohk[rows, :] = jnp.where(hot, 0.0, -FAR).astype(BF16)
        spot = (lax.broadcasted_iota(jnp.int32, (256, 96), 1) % 32).astype(F32)
        got_r = dot_nn(jnp.where(spot == grow, 1.0, 0.0).astype(BF16), table_r)
        got_c = dot_nn(jnp.where(spot == gcol, 1.0, 0.0).astype(BF16), table_c)
        cr, sr = got_r[:, :width_all], got_r[:, width_all:]
        cc, sc = got_c[:, :width_all], got_c[:, width_all:]
        cossin[rows, :width_all] = cr * cc - sr * sc
        cossin[rows, width_all:] = sr * cc + cr * sc

    loop(rows_all // 256, place)


def front_rows(x, gain, shift, w, b, q8, key, val, nf, cossin):
    rows_all, width_all = q8.shape
    pairs = width_all // PAIR

    def norm(r):
        rows = aligned(r, SUB)
        unit, _ = unit_of(x[rows, :].astype(F32))
        nf[rows, :] = (unit * gain + shift).astype(BF16)

    loop(rows_all // SUB, norm)

    def project(r):
        rows = aligned(r, QR)
        lane_first = lane_ids(QR) % HALF < HALF // 2
        sign = jnp.where(lane_first, -1.0, 1.0)
        for k, out in ((0, q8), (1, key)):
            got = dot_nn(nf[rows, :], w[:, k * width_all : (k + 1) * width_all]) + b[k : k + 1, :]
            for p in range(pairs):
                cols = slice(p * PAIR, (p + 1) * PAIR)
                part = got[:, cols]
                turned = part * cossin[rows, cols] + swap_halves(part, lane_first) * (
                    cossin[rows, width_all + p * PAIR : width_all + (p + 1) * PAIR] * sign
                )
                turned = turned.astype(BF16)
                if k == 0:
                    turned = turned * jnp.asarray(HALF**-0.5, BF16)
                out[rows, cols] = turned
        got = dot_nn(nf[rows, :], w[:, 2 * width_all : 3 * width_all])
        val[rows, :] = (got + b[2:3, :]).astype(BF16)

    loop(rows_all // QR, project)


def front_heads(q8, key, val, ohq, ohk, att, kxs, scs, lcol, after):
    rows_all, width_all = q8.shape
    blocks, pieces_all, wide = rows_all // QR, rows_all // R, scs[0].shape[1] // R
    masks = [head_mask(h).astype(BF16) for h in range(2)]

    def piece(h, k):
        at = (k // wide) * QR
        return scs[h].at[at : at + QR, (k % wide) * R : (k % wide + 1) * R]

    pairs = width_all // PAIR

    def keys(h, p):
        kxs[h][...] = key[:, aligned(p, PAIR)] * masks[h] + ohk[...] * masks[1 - h]

    def scores(h, r, p):
        rows = aligned(r, QR)
        qx = q8[rows, aligned(p, PAIR)] * masks[h] + ohq[rows, :] * masks[1 - h]
        for k in range(pieces_all):
            piece(h, k)[...] = dot_nt(qx, kxs[h][k * R : (k + 1) * R, :])

    def weigh(h, r, p):
        rows, cols = aligned(r, QR), aligned(p, PAIR)
        top = piece(h, 0)[...]
        for k in range(1, pieces_all):
            top = jnp.maximum(top, piece(h, k)[...])
        top = jnp.max(top, axis=-1, keepdims=True)
        total = jnp.zeros((QR, PAIR), F32)
        got = jnp.zeros((QR, PAIR), F32)
        for k in range(pieces_all):
            grown = jnp.exp(piece(h, k)[...] - top)
            for m in range(R // PAIR):
                total = total + grown[:, m * PAIR : (m + 1) * PAIR]
            got = got + dot_nn(grown.astype(BF16), val[k * R : (k + 1) * R, cols])
        total = jnp.sum(total, axis=-1, keepdims=True)
        got = got * (1.0 / total)
        lane = lane_ids(QR)
        if h == 0:
            att[rows, cols] = got
        else:
            att[rows, cols] = jnp.where(lane < HALF, att[rows, cols], got)
        lcol[rows, :] = jnp.where(lane == p * 2 + h, top + jnp.log(total), lcol[rows, :])

    keys(0, 0)
    keys(1, 0)
    scores(0, 0, 0)

    def half(r):
        def step(p):
            n = jnp.minimum(r * pairs + p + 1, blocks * pairs - 1)
            scores(1, r, p)
            weigh(0, r, p)
            keys(0, n % pairs)
            scores(0, n // pairs, n % pairs)
            weigh(1, r, p)
            keys(1, n % pairs)

        loop(pairs, step)
        after(r)

    loop(blocks, half)


PARTS = 16


def main_kernel(
    fuse, pairs, chunks,
    x_h, og_h, wp_h, we_h, wc_h, wq_h,
    grids, freqs, bias_q, *rest,
):
    (
    gain_one, shift_one, bias_p, gain_two, shift_two, bias_e, bias_c,
    mixed_h, pgrad_h, ff_h, pq_h, small_h, nf_h, cossin_h,
    att, q8, key, val, ohq, ohk, lse, pos, x, cot, wp, we, wc,
    acc_a, acc_b, xbuf, mid, cott, ns, nst, act, hgb, dgrad, delta,
    km, vm, kt, kmt, dk, dv, dqt, qkvg, cos, sin, sums,
    gf, gq, r1, r2, r3, small, small_r,
    lsem, xs, xr, credit, s1, e1, s2, e2, s3, e3, c1, c2, c3, ms, mr, osem, zs, s4, e4,
    ) = rest
    gain_one, shift_one, bias_p, gain_two, shift_two, bias_e, bias_c = (
        v[...].reshape(1, -1)
        for v in (gain_one, shift_one, bias_p, gain_two, shift_two, bias_e, bias_c)
    )
    me = lax.axis_index("dp")
    core = lax.axis_index("head")
    blocks = x.shape[0] // R
    subs = x.shape[0] // SUB
    mate = (me, 1 - core)
    if fuse:
        xx, yy, zz = me % 2, (me // 2) % 2, me // 4
        fst = xx * (1 - core) + yy * core
        snd = yy * (1 - core) + xx * core
        peer1 = (me + (1 - 2 * fst) * (1 + core), core)
        peer2 = (me + (1 - 2 * snd) * (2 - core), core)
        peers_z = [(((zz + j) % 4) * 4 + me % 4, core) for j in (1, 2, 3)]
        odd, across = zz % 2, (zz + 2) % 4
        near = ((zz + 1 - 2 * odd) * 4 + me % 4, core)
        far = (across * 4 + me % 4, core)

        def where(z, f, s):
            return z * 4 + s * (2 - core) + f * (1 + core)

    def load(src, dst, i):
        copy = pltpu.make_async_copy(src, dst, lsem.at[i])
        copy.start()
        return copy

    heads = q8.shape[1]
    slots = grids.shape[1]
    get_x = load(x_h, x, 4)
    get_wq = [load(wq_h.at[k], we.at[:, pl.ds(k * heads, heads)], 7 + k) for k in range(3)]
    get_wp = load(wp_h, wp, 1)
    get_og = load(og_h, cot, 2)
    get_wc = load(wc_h, wc, 6)

    barrier = pltpu.get_barrier_semaphore()
    friends = [mate] + ([peer1, peer2] + peers_z if fuse else [])
    for friend in friends:
        pl.semaphore_signal(barrier, inc=1, device_id=friend, device_id_type=MESH)

    def exchange(src, r):
        return pltpu.make_async_remote_copy(
            src.at[aligned(r, R), :], xbuf.at[aligned(r, R), :], xs.at[r], xr.at[r],
            device_id=mate, device_id_type=MESH,
        )

    def send(src, r):
        exchange(src, r).start()

    def give_credit(r):
        pl.semaphore_signal(credit.at[r], inc=1, device_id=mate, device_id_type=MESH)

    def take_credit(r):
        pl.semaphore_wait(credit.at[r], 1)

    def remote(src, dst, ss, rs, peer):
        return pltpu.make_async_remote_copy(
            src, dst, ss, rs, device_id=peer, device_id_type=MESH
        )

    class Line:
        def __init__(self, grads, base, width, out, guard, parts):
            self.g, self.base, self.out, self.guard = grads, base, out, guard
            self.n, self.parts = width // parts, parts

        def cols(self, k):
            return pl.ds(k * self.n, self.n)

        def at(self, j, k):
            return self.base + j * self.parts + k

        def step(self, j, k, first, src, dst, ss, rs, peer):
            i = self.at(j, k)
            return remote(
                self.g.at[j, src, :, self.cols(k)], first.at[j, dst, :, self.cols(k)],
                ss.at[i], rs.at[i], peer,
            )

        def whole(self, j, k, n, ss, rs, buf, peer):
            return self.step(j, k, buf, pl.ds(0, n), pl.ds(0, n), ss, rs, peer)

        def add(self, j, k, b, got):
            c = self.cols(k)
            self.g[j, b, :, c] = self.g[j, b, :, c] + got

        def start1(self, j):
            if self.guard == "take":
                pl.semaphore_wait(c1.at[j], 1)
            for k in range(self.parts):

                def one(i, k=k):
                    b = where(i // 2, 1 - fst, i % 2)
                    self.step(j, k, r1, b, i, s1, e1, peer1).start()

                loop(8, one)

        def give(self, sem, j, peers):
            if self.guard == "give":
                def go():
                    for peer in peers:
                        pl.semaphore_signal(sem.at[j], inc=1, device_id=peer, device_id_type=MESH)
                if isinstance(j, int):
                    if j < 4:
                        go()
                else:
                    pl.when(j < 4)(go)

        def finish1(self, j, k=0):
            self.whole(j, k, 8, s1, e1, r1, peer1).wait_recv()
            c = self.cols(k)

            def one(i):
                self.add(j, k, where(i // 2, fst, i % 2), r1[j, i, :, c])

            loop(8, one)
            self.give(c1, j, [peer1])
            if self.guard == "take" and k == 0:
                pl.semaphore_wait(c2.at[j], 1)

            def two(i):
                self.step(j, k, r2, where(i, fst, 1 - snd), i, s2, e2, peer2).start()

            loop(4, two)

        def finish2(self, j, k=0):
            self.whole(j, k, 4, s2, e2, r2, peer2).wait_recv()
            c = self.cols(k)

            def one(i):
                self.add(j, k, where(i, fst, snd), r2[j, i, :, c])

            loop(4, one)
            self.give(c2, j, [peer2])
            if self.guard == "take" and k == 0:
                pl.semaphore_wait(c3.at[j], 3)
            for m in range(3):
                b = where((zz + m + 1) % 4, fst, snd)
                self.step(j, k, r3, b, m, s3, e3, peers_z[m]).start()

        def result(self, j, k):
            c = self.cols(k)
            return pltpu.make_async_copy(
                self.g.at[j, me, :, c], self.out.at[j, :, c], osem.at[self.at(j, k)]
            )

        def finish3(self, j, k=0):
            self.whole(j, k, 3, s3, e3, r3, peers_z[0]).wait_recv()
            c = self.cols(k)
            self.add(j, k, me, r3[j, 0, :, c] + r3[j, 1, :, c] + r3[j, 2, :, c])
            self.give(c3, j, peers_z)
            self.result(j, k).start()

        def drain(self, j):
            for k in range(self.parts):
                self.whole(j, k, 8, s1, e1, r1, peer1).wait_send()
                self.whole(j, k, 4, s2, e2, r2, peer2).wait_send()
                self.whole(j, k, 3, s3, e3, r3, peers_z[0]).wait_send()
                self.result(j, k).wait()

    class Two(Line):
        def finish2(self, j, k=0):
            self.whole(j, k, 4, s2, e2, r2, peer2).wait_recv()
            c = self.cols(k)

            def one(i):
                self.add(j, k, where(i, fst, snd), r2[j, i, :, c])

            loop(4, one)
            self.give(c2, j, [peer2])
            for m in range(2):
                b = where(1 - odd + 2 * m, fst, snd)
                self.step(j, k, r3, b, m, s3, e3, near).start()

        def finish3(self, j, k=0):
            self.whole(j, k, 2, s3, e3, r3, near).wait_recv()
            c = self.cols(k)
            for m in range(2):
                self.add(j, k, where(odd + 2 * m, fst, snd), r3[j, m, :, c])
            self.step(j, k, r3, where(across, fst, snd), 2, s4, e4, far).start()

        def finish4(self, j, k=0):
            self.step(j, k, r3, 0, 2, s4, e4, far).wait_recv()
            self.add(j, k, me, r3[j, 2, :, self.cols(k)])
            self.give(c3, j, peers_z)
            self.result(j, k).start()

        def drain(self, j):
            for k in range(self.parts):
                self.whole(j, k, 8, s1, e1, r1, peer1).wait_send()
                self.whole(j, k, 4, s2, e2, r2, peer2).wait_send()
                self.whole(j, k, 2, s3, e3, r3, near).wait_send()
                self.step(j, k, r3, 0, 2, s4, e4, far).wait_send()
                self.result(j, k).wait()

    class Deep:
        def __init__(self, grads, j, out, line):
            self.g, self.j, self.out, self.line = grads, j, out, line

        def one(self):
            j = self.j
            return remote(self.g.at[j, pl.ds(0, 8)], r1.at[j], s1.at[j], e1.at[j], near)

        def two(self):
            j = self.j
            return remote(self.g.at[j, pl.ds(across * 4, 4)], r2.at[j], s2.at[j], e2.at[j], far)

        def three(self):
            j = self.j
            return remote(
                self.g.at[j, pl.ds(0, 2)], r3.at[j, pl.ds(0, 2)], s3.at[j], e3.at[j], peer1
            )

        def four(self):
            return remote(
                self.g.at[self.j, where(zz, fst, 1 - snd)], r3.at[self.j, 2],
                zs.at[2 * self.line], zs.at[2 * self.line + 1], peer2,
            )

        def result(self):
            return pltpu.make_async_copy(
                self.g.at[self.j, me], self.out.at[self.j], osem.at[self.j]
            )

        def start(self):
            j = self.j
            for m in range(2):
                remote(
                    self.g.at[j, pl.ds((1 - odd + 2 * m) * 4, 4)], r1.at[j, pl.ds(4 * m, 4)],
                    s1.at[j], e1.at[j], near,
                ).start()

        def finish1(self):
            j = self.j
            self.one().wait_recv()

            def add(i):
                b = (odd + 2 * (i // 4)) * 4 + i % 4
                self.g[j, b] = self.g[j, b] + r1[j, i]

            loop(8, add)
            self.two().start()

        def finish2(self):
            j = self.j
            self.two().wait_recv()

            def add(i):
                self.g[j, zz * 4 + i] = self.g[j, zz * 4 + i] + r2[j, i]

            loop(4, add)
            for s in range(2):
                remote(
                    self.g.at[j, where(zz, 1 - fst, s)], r3.at[j, s], s3.at[j], e3.at[j], peer1
                ).start()

        def finish3(self):
            j = self.j
            self.three().wait_recv()
            for s in range(2):
                b = where(zz, fst, s)
                self.g[j, b] = self.g[j, b] + r3[j, s]
            self.four().start()

        def finish4(self):
            self.four().wait_recv()
            self.g[self.j, me] = self.g[self.j, me] + r3[self.j, 2]
            self.result().start()

        def drain(self):
            for copy in (self.one(), self.two(), self.three(), self.four()):
                copy.wait_send()
            self.result().wait()

    class Plain:
        def __init__(self, grads, base, width, out, guard, parts):
            self.g, self.base, self.out = grads, base, out

        def copy(self, j):
            return pltpu.make_async_copy(self.g.at[j], self.out.at[j], osem.at[self.base + j])

        def start1(self, j):
            self.copy(j).start()

        def finish1(self, j):
            pass

        finish2 = finish3 = finish1

        def drain(self, j):
            self.copy(j).wait()

    kind = Line if fuse else Plain
    ff = (Two if fuse else Plain)(gf, 0, 2 * CHUNK, ff_h, "give", 1)
    pq = kind(gq, chunks, 3 * PAIR, pq_h, "take", 3)
    deep = [Deep(gf, chunks - 1 - n, ff_h, n) for n in range(2)]

    small[...] = jnp.zeros_like(small)
    sums[...] = jnp.zeros_like(sums)
    sums[7:8, :] = bias_e

    turns = []
    for axis in range(2):
        lines = [freqs[n, axis : axis + 1, :] for n in range(heads // HALF) for _ in range(2)]
        turns.append(jnp.concatenate(lines, axis=1))
    front_place(grids, slots, turns, ohq, ohk, acc_b, pos)
    put_cossin = load(acc_b.at[:, pl.ds(0, 2 * heads)], cossin_h, 11)
    get_x.wait()
    for copy in get_wq:
        copy.wait()
    front_rows(x, gain_one, shift_one, we, bias_q, q8, key, val, ns, acc_b)
    get_we = load(we_h, we, 5)
    put_nf = load(ns, nf_h, 10)
    put_cossin.wait()
    get_wp.wait()
    pl.semaphore_wait(barrier, len(friends))

    def project(r):
        for n in range(QR // R):
            rows = aligned(r * (QR // R) + n, R)
            acc_a[rows, :] = dot_nn(att[rows, :].astype(BF16), wp[...])
            send(acc_a, r * (QR // R) + n)

    front_heads(q8, key, val, ohq, ohk, att, (km, vm), (mid, acc_b), dk, project)

    def turn(r):
        rows = aligned(r, PAIR)
        lse[:, rows] = jnp.transpose(dk[rows, :])[: lse.shape[0], :]

    loop(x.shape[0] // PAIR, turn)

    get_og.wait()

    def mask_cot(r):
        rows = aligned(r, R)
        block = (cot[rows, :].astype(F32) * pos[rows, 0:1])
        small[0, 0:1, :] = small[0, 0:1, :] + jnp.sum(block, axis=0, keepdims=True)
        low = block.astype(BF16)
        cot[rows, :] = low
        cott[:, rows] = jnp.transpose(low)

    loop(blocks, mask_cot)
    put_nf.wait()

    def second_norm(r):
        exchange(acc_a, r).wait()

        def sub(i):
            rows = pl.ds(pl.multiple_of(r * R + i * SUB, SUB), SUB)
            middle = x[rows, :].astype(F32) + ((acc_a[rows, :] + xbuf[rows, :]) + bias_p)
            unit, _ = unit_of(middle)
            mid[rows, :] = middle
            ns[rows, :] = (unit * gain_two + shift_two).astype(BF16)
            acc_b[rows, :] = 0.5 * (middle + bias_c)
            acc_a[rows, :] = jnp.zeros_like(middle)

        loop(R // SUB, sub)
        give_credit(r)
        nst[:, aligned(r, R)] = jnp.transpose(ns[aligned(r, R), :])

    loop(blocks, second_norm)
    get_we.wait()
    get_wc.wait()

    def feed(i):
        none, upto = 1 - (i + chunks - 1) // chunks, 1 - (i + chunks - 3) // chunks
        j = (i - 2) * (1 - upto) + (chunks - i) * (upto - none)
        cols = aligned(j, CHUNK)

        def rows_of(r):
            rows = aligned(r, QR)
            hidden = dot_nn(ns[rows, :], we[:, cols]) + sums[7:8, cols]
            upstream = dot_nt(cot[rows, :], wc[cols, :])
            phi = 0.5 * (1.0 + lax.erf(hidden * (0.5**0.5)))
            slope = phi + hidden * (jnp.exp(-0.5 * hidden * hidden) * (0.3989422804014327))
            active = (hidden * phi).astype(BF16)
            hgrad = (upstream * slope).astype(BF16)
            act[rows, :] = active
            hgb[rows, :] = hgrad
            sums[0:1, cols] = sums[0:1, cols] + jnp.sum(hgrad.astype(F32), axis=0, keepdims=True)
            acc_b[rows, :] = acc_b[rows, :] + dot_nn(active, wc[cols, :])
            acc_a[rows, :] = acc_a[rows, :] + dot_nt(hgrad, we[:, cols])

            def leave():
                for n in range(QR // R):
                    take_credit(r * (QR // R) + n)
                    send(acc_a, r * (QR // R) + n)

            pl.when(i == chunks - 1)(leave)

        loop(x.shape[0] // QR, rows_of)
        got = dot_nn(cott[...], act[...])
        gf[j, :, :, pl.ds(0, CHUNK)] = got.reshape(gf.shape[1], gf.shape[2], CHUNK)
        got = dot_nn(nst[...], hgb[...])
        gf[j, :, :, pl.ds(CHUNK, CHUNK)] = got.reshape(gf.shape[1], gf.shape[2], CHUNK)
        if fuse:
            pl.when(i == 1)(deep[0].start)
            pl.when(i == 2)(deep[1].start)
            pl.when((i != 1) & (i != 2))(lambda: ff.start1(j))
            pl.when(i == 4)(lambda: ff.finish1(0))
        else:
            ff.start1(j)

    loop(chunks, feed)
    if fuse:
        deep[0].finish1()
        ff.finish1(1)

    get_nf = load(nf_h, ns, 0)
    get_wq = [
        load(wq_h.at[k], we.at[:, pl.ds(k * pairs * PAIR, pairs * PAIR)], 4 + k) for k in range(3)
    ]
    kt[...] = jnp.transpose(key[...])
    get_nf.wait()

    def turn_first(r):
        nst[:, aligned(r, R)] = jnp.transpose(ns[aligned(r, R), :])

    loop(blocks, turn_first)

    def second_back(r):
        exchange(acc_a, r).wait()

        def sub(i):
            rows = pl.ds(pl.multiple_of(r * R + i * SUB, SUB), SUB)
            up = acc_a[rows, :] + xbuf[rows, :]
            unit, inv = unit_of(mid[rows, :])
            small[0, 1:2, :] = small[0, 1:2, :] + jnp.sum(up * unit, axis=0, keepdims=True)
            small[0, 2:3, :] = small[0, 2:3, :] + jnp.sum(up, axis=0, keepdims=True)
            grad = cot[rows, :].astype(F32) + norm_back(up, unit, inv, gain_two)
            mid[rows, :] = grad
            low = grad.astype(BF16)
            cot[rows, :] = low
            small[0, 3:4, :] = small[0, 3:4, :] + jnp.sum(
                low.astype(F32), axis=0, keepdims=True
            )

        loop(R // SUB, sub)
        give_credit(r)
        rows = aligned(r, R)
        cott[:, rows] = jnp.transpose(cot[rows, :])
        low = dot_nt(cot[rows, :], wp[...]).astype(BF16)
        dgrad[rows, :] = low
        prod = low.astype(F32) * att[rows, :]
        head = lax.broadcasted_iota(jnp.int32, (8, prod.shape[1]), 0)
        lane = lax.broadcasted_iota(jnp.int32, (8, prod.shape[1]), 1)
        pick = (lane // HALF == head).astype(F32)
        delta[:, rows] = lax.dot_general(
            pick, prod, (((1,), (1,)), ((), ())), precision=lax.Precision.HIGHEST,
            preferred_element_type=F32,
        )

    loop(blocks, second_back)
    if fuse:
        ff.finish2(0)

    def small_copy(i, k, peer, late=1):
        rows = pl.ds(8 * late, 8)
        return remote(
            small.at[k, rows], small_r.at[i, rows], ms.at[4 + 6 * late + i], mr.at[6 * late + i],
            peer,
        )

    early, late = slice(0, 8), slice(8, 16)
    n = chunks * CHUNK // 2
    small[0, 4:5, :] = sums[0:1, 0:n]
    small[0, 5:6, :] = sums[0:1, n : 2 * n]
    small[1, early] = small[0, early]

    def early_one():
        small_copy(1, 1, peer1, 0).wait()
        small[2, early] = small[1, early] + small_r[1, early]
        small_copy(2, 2, peer2, 0).start()

    def early_two():
        small_copy(2, 2, peer2, 0).wait()
        small[3, early] = small[2, early] + small_r[2, early]
        for k in range(3):
            small_copy(3 + k, 3, peers_z[k], 0).start()

    def early_three():
        for k in range(3):
            small_copy(3 + k, 3, peers_z[k], 0).wait()
        small[4, early] = small[3, early] + (small_r[3, early] + small_r[4, early] + small_r[5, early])

    if fuse:
        small_copy(1, 1, peer1, 0).start()
    gq[0] = dot_nn(cott[...], att[...].astype(BF16)).reshape(gq.shape[1:])
    pq.start1(0)
    if fuse:
        ff.finish1(2)

    def send_mixed(r):
        take_credit(r)
        send(acc_b, r)

    loop(blocks, send_mixed)

    def mixed_block(r):
        exchange(acc_b, r).wait()
        rows = aligned(r, R)
        ns[rows, :] = (acc_b[rows, :] + xbuf[rows, :]).astype(BF16)
        give_credit(r)
        pltpu.make_async_copy(ns.at[rows, :], mixed_h.at[rows, :], ms.at[r]).start()

    def thrice(step, j):
        for k in range(3):
            step(j, k)

    def gap0():
        ff.finish2(1)

    def gap1():
        deep[1].finish1()
        ff.finish1(3)

    def gap2():
        deep[0].finish2()
        ff.finish3(0)
        ff.finish2(2)

    def gap3():
        thrice(pq.finish1, 0)
        ff.finish3(1)

    def gap4():
        ff.finish2(3)
        ff.finish4(0)
        deep[1].finish2()

    def gap5():
        thrice(pq.finish2, 0)
        thrice(pq.finish1, 1)
        early_one()

    between = (gap0, gap1, gap2, gap3, gap4, gap5)

    def pair_back(p):
        cols = aligned(p, PAIR)
        get_cos = load(cossin_h.at[:, cols], cos, 0)
        get_sin = load(cossin_h.at[:, aligned(pairs + p, PAIR)], sin, 1)
        dk[...] = jnp.zeros_like(dk)
        dv[...] = jnp.zeros_like(dv)
        dqt[...] = jnp.zeros_like(dqt)

        def head_back(h):
            mine = head_mask(h).astype(BF16)
            other = head_mask(1 - h).astype(BF16)
            km[...] = key[:, cols] * mine + ohk[...] * other
            vm[...] = val[:, cols] * mine
            spot = lax.broadcasted_iota(jnp.int32, (PAIR, 1), 0)
            kmt[...] = kt[cols, :] * (spot // HALF == h).astype(F32).astype(BF16)
            n = p * 2 + h

            def query_back(r):
                rows = aligned(r, R)
                qm = q8[rows, cols] * mine
                qx = qm + ohq[rows, :] * other
                do = dgrad[rows, cols]
                score = dot_nt(km[...], qx)
                prob = jnp.exp(score - lse[pl.ds(n, 1), rows])
                pgrad = dot_nt(vm[...], do)
                sgrad = (prob * (pgrad - delta[pl.ds(n, 1), rows])).astype(BF16)
                dv[...] = dv[...] + dot_nn(prob.astype(BF16), do * mine)
                dk[...] = dk[...] + dot_nn(sgrad, qm)
                dqt[:, rows] = dqt[:, rows] + dot_nn(kmt[...], sgrad)

            loop(blocks, query_back)
            if fuse:
                for q in range(3):
                    pl.when(p == q)(lambda q=q: between[2 * q + h]())

        head_back(0)
        head_back(1)
        get_cos.wait()
        get_sin.wait()

        def turn_back(r):
            rows = aligned(r, R)
            lane_first = lane_ids(R) % HALF < HALF // 2
            sign = jnp.where(lane_first, 1.0, -1.0)
            c, s = cos[rows, :], sin[rows, :]
            total = jnp.zeros((R, PAIR), F32)
            grads = []
            scale = HALF**-0.5
            for k, (grad, turned) in enumerate(
                (
                    (jnp.transpose(dqt[:, rows]) * scale, q8[rows, cols].astype(F32) * (1.0 / scale)),
                    (dk[rows, :], key[rows, cols].astype(F32)),
                )
            ):
                swapped = swap_halves(grad, lane_first) * sign
                total = total + swapped * turned
                grads.append((grad * c + swapped * s).astype(BF16))
            grads.append(dv[rows, :].astype(BF16))
            for k, low in enumerate(grads):
                qkvg[p, rows, k * PAIR : (k + 1) * PAIR] = low
                sums[k + 1 : k + 2, cols] = sums[k + 1 : k + 2, cols] + jnp.sum(
                    low.astype(F32), axis=0, keepdims=True
                )
            for k in range(2):
                sums[k + 4 : k + 5, cols] = sums[k + 4 : k + 5, cols] + jnp.sum(
                    total * pos[rows, k + 1 : k + 2], axis=0, keepdims=True
                )

        loop(blocks, turn_back)
        gq[p + 1] = dot_nn(nst[...], qkvg[p]).reshape(gq.shape[1:])
        pq.start1(p + 1)

    loop(pairs, pair_back)

    def first_send(r):
        def sub(i):
            rows = pl.ds(pl.multiple_of(r * R + i * SUB, SUB), SUB)
            unit, _ = unit_of(x[rows, :].astype(F32))
            up = acc_a[rows, :]
            small[0, 8:9, :] = small[0, 8:9, :] + jnp.sum(up * unit, axis=0, keepdims=True)
            small[0, 9:10, :] = small[0, 9:10, :] + jnp.sum(up, axis=0, keepdims=True)

        rows = aligned(r, R)
        total = jnp.zeros((R, acc_a.shape[1]), F32)
        for p in range(pairs):
            weight = jnp.concatenate(
                [we[:, (k * pairs + p) * PAIR : (k * pairs + p + 1) * PAIR] for k in range(3)],
                axis=1,
            )
            total = total + dot_nt(qkvg[p, rows, :], weight)
        acc_a[rows, :] = total
        take_credit(r)
        send(acc_a, r)
        loop(R // SUB, sub)

    if fuse:
        ff.finish3(2)
        ff.finish4(1)
        thrice(pq.finish2, 1)
        deep[0].finish3()
        pq.finish1(2, 0)
    loop(blocks, mixed_block)
    for copy in get_wq:
        copy.wait()
    loop(blocks, first_send)

    m = pairs * PAIR
    for k in range(5):
        small[0, 10 + k : 11 + k, 0:m] = sums[1 + k : 2 + k, 0:m]

    copy = small_copy(0, 0, mate)
    copy.start()
    if fuse:
        pq.finish1(2, 1)
        pq.finish1(2, 2)
        deep[1].finish3()
        ff.finish3(3)
        ff.finish4(2)
    copy.wait()
    line = lax.broadcasted_iota(jnp.int32, (8, small.shape[2]), 0)
    small[1, late] = small[0, late] + jnp.where(line < 2, small_r[0, late], 0.0)
    if fuse:
        small_copy(1, 1, peer1).start()
        thrice(pq.finish2, 2)
    last = 4 if fuse else 1

    def first_back(r):
        exchange(acc_a, r).wait()

        def sub(i):
            rows = pl.ds(pl.multiple_of(r * R + i * SUB, SUB), SUB)
            unit, inv = unit_of(x[rows, :].astype(F32))
            up = acc_a[rows, :] + xbuf[rows, :]
            mid[rows, :] = mid[rows, :] + norm_back(up, unit, inv, gain_one)

        loop(R // SUB, sub)
        rows = aligned(r, R)
        pltpu.make_async_copy(mid.at[rows, :], pgrad_h.at[rows, :], xs.at[r]).start()

    if fuse:
        early_two()
        ff.finish4(3)
        thrice(pq.finish3, 0)
        pq.finish1(3, 0)
        pq.finish1(3, 1)
        pq.finish2(3, 0)
        thrice(pq.finish3, 1)
        pq.finish1(3, 2)
        small_copy(1, 1, peer1).wait()
        small[2, late] = small[1, late] + small_r[1, late]
        small_copy(2, 2, peer2).start()
        pq.finish2(3, 1)
        pq.finish2(3, 2)
        deep[0].finish4()
        deep[1].finish4()
        early_three()
        small_copy(2, 2, peer2).wait()
        small[3, late] = small[2, late] + small_r[2, late]
        copies = [small_copy(3 + k, 3, peers_z[k]) for k in range(3)]
        for copy in copies:
            copy.start()
        loop(blocks, first_back)
        thrice(pq.finish3, 2)
        thrice(pq.finish3, 3)
        for copy in copies:
            copy.wait()
        small[4, late] = small[3, late] + (small_r[3, late] + small_r[4, late] + small_r[5, late])
    if not fuse:
        loop(blocks, first_back)
    out_small = pltpu.make_async_copy(small.at[last], small_h, lsem.at[0])
    out_small.start()
    if fuse:
        deep[0].drain()
        deep[1].drain()
        loop(chunks - 2, ff.drain)
    else:
        loop(chunks, ff.drain)
    loop(pairs + 1, pq.drain)
    out_small.wait()

    def finish_out(r):
        rows = aligned(r, R)
        pltpu.make_async_copy(ns.at[rows, :], mixed_h.at[rows, :], ms.at[r]).wait()
        pltpu.make_async_copy(mid.at[rows, :], pgrad_h.at[rows, :], xs.at[r]).wait()

    loop(blocks, finish_out)


def main_call(fuse, parts, big, grids, freqs, bias_q, vectors):
    x, og, wp, we, wc, wq = big
    rows, width = x.shape
    heads = wq.shape[2]
    hidden = we.shape[1]
    pairs, chunks = heads // PAIR, hidden // CHUNK
    shape = jax.ShapeDtypeStruct
    part_rows = width // parts
    sent = parts if fuse else 0
    if fuse:
        ff_shape, pq_shape = (chunks, part_rows, 2 * CHUNK), (pairs + 1, part_rows, 3 * PAIR)
        grain = (parts, part_rows)
        slots = chunks
    else:
        ff_shape, pq_shape = (chunks, 1, width, 2 * CHUNK), (pairs + 1, 1, width, 3 * PAIR)
        grain = (1, width)
        slots = 1
    outs = [
        shape((rows, width), BF16), shape((rows, width), F32), shape(ff_shape, F32),
        shape(pq_shape, F32), shape((16, width), F32), shape((rows, width), BF16),
        shape((rows, 2 * heads), F32),
    ]
    any_spec = pl.BlockSpec(memory_space=ANY)
    vm_spec = pl.BlockSpec(memory_space=pltpu.VMEM)
    V = pltpu.VMEM
    DMA = pltpu.SemaphoreType.DMA
    REG = pltpu.SemaphoreType.REGULAR
    blocks = rows // R
    lines = chunks + 3 * (pairs + 1)
    recv = (lambda n: V((slots, n, part_rows, 2 * CHUNK), F32)) if fuse else (lambda n: V((1, 1, 8, PAIR), F32))
    scratch = [
        V((rows, heads), F32), V((rows, heads), BF16), V((rows, heads), BF16), V((rows, heads), BF16),
        V((rows, PAIR), BF16), V((rows, PAIR), BF16), V((8, rows), F32), V((rows, PAIR), F32),
        V((rows, width), BF16), V((rows, width), BF16), V((heads, width), BF16),
        V((width, hidden), BF16), V((hidden, width), BF16),
        V((rows, width), F32), V((rows, width), F32), V((rows, width), F32), V((rows, width), F32),
        V((width, rows), BF16), V((rows, width), BF16), V((width, rows), BF16),
        V((rows, CHUNK), BF16), V((rows, CHUNK), BF16), V((rows, heads), BF16), V((8, rows), F32),
        V((rows, PAIR), BF16), V((rows, PAIR), BF16), V((heads, rows), BF16), V((PAIR, rows), BF16),
        V((rows, PAIR), F32), V((rows, PAIR), F32), V((PAIR, rows), F32), V((pairs, rows, 3 * PAIR), BF16),
        V((rows, PAIR), F32), V((rows, PAIR), F32), V((8, hidden), F32),
        V((chunks, *grain, 2 * CHUNK), F32), V((pairs + 1, *grain, 3 * PAIR), F32),
        recv(8), recv(4), recv(3), V((5, 16, width), F32), V((6, 16, width), F32),
        DMA((16,)), DMA((blocks,)), DMA((blocks,)), REG((blocks,)),
        DMA((lines,)), DMA((lines,)), DMA((lines,)), DMA((lines,)), DMA((lines,)), DMA((lines,)),
        REG((4,)), REG((4,)), REG((4,)), DMA((16,)), DMA((12,)), DMA((lines,)), DMA((4,)), DMA((chunks,)), DMA((chunks,)),
    ]
    return pl.pallas_call(
        partial(main_kernel, fuse, pairs, chunks),
        name="main",
        out_shape=outs,
        in_specs=[any_spec] * len(big)
        + [pl.BlockSpec(memory_space=pltpu.SMEM)]
        + [vm_spec] * (2 + len(vectors)),
        out_specs=[any_spec] * len(outs),
        scratch_shapes=scratch,
        compiler_params=pltpu.CompilerParams(
            collective_id=0, has_side_effects=True, vmem_limit_bytes=67043328
        ),
    )(*big, grids, freqs, bias_q, *vectors)


def finish_kernel(
    mixed_h, pgrad_h, ff_h, pq_h, small_h,
    mixed_o, pgrad_o, qkv_o, proj_o, expand_o, contract_o,
    *rest,
):
    tiny_o, (mixed, pgrad, ff, pq, small), tiny, (isem, osem, tsem) = (
        rest[:9], rest[9:14], rest[14:23], rest[23:],
    )
    gain_one, shift_one, bias_q, rope, bias_p, gain_two, shift_two, bias_e, bias_c = tiny
    blocks = mixed.shape[0] // R
    chunks, pairs = ff.shape[0], pq.shape[0] - 1
    jobs = [(small_h, small, [])]
    for src, buf, dst in ((pgrad_h, pgrad, pgrad_o), (mixed_h, mixed, mixed_o)):
        for r in range(blocks):
            part = (pl.ds(r * R, R), slice(None))
            jobs.append((src.at[part], buf.at[part], [(buf.at[part], dst.at[part])]))
    for j in range(chunks):
        cols = pl.ds(j * CHUNK, CHUNK)
        jobs.append((ff_h.at[j], ff.at[j], [
            (ff.at[j, :, pl.ds(0, CHUNK)], contract_o.at[:, cols]),
            (ff.at[j, :, pl.ds(CHUNK, CHUNK)], expand_o.at[:, cols]),
        ]))
    jobs.append((pq_h.at[0], pq.at[0], [(pq.at[0], proj_o)]))
    for p in range(pairs):
        jobs.append((pq_h.at[p + 1], pq.at[p + 1], [
            (pq.at[p + 1, :, pl.ds(k * PAIR, PAIR)], qkv_o.at[k, :, pl.ds(p * PAIR, PAIR)])
            for k in range(3)
        ]))
    gets = [pltpu.make_async_copy(a, b, isem.at[i]) for i, (a, b, _) in enumerate(jobs)]
    for get in gets:
        get.start()
    gets[0].wait()
    heads = bias_q.shape[1]
    for k, out in (
        (8, gain_one), (9, shift_one), (3, bias_p), (1, gain_two), (2, shift_two), (0, bias_c),
    ):
        out[...] = small[k, :]
    half = bias_e.shape[0] // 2
    bias_e[:half] = small[4, :half]
    bias_e[half:] = small[5, :half]
    bias_q[...] = small[10:13, :heads]
    for p in range(pairs):
        tile = small[8:16, p * PAIR : (p + 1) * PAIR]
        both = tile + pltpu.roll(tile, PAIR - HALF // 2, 1)
        rope[2 * p] = both[5:7, : HALF // 2]
        rope[2 * p + 1] = pltpu.roll(both, HALF, 1)[5:7, : HALF // 2]
    last = [pltpu.make_async_copy(a, b, tsem.at[i]) for i, (a, b) in enumerate(zip(tiny, tiny_o))]
    for put in last:
        put.start()
    puts = []
    for get, (_, _, todo) in list(zip(gets, jobs))[1:]:
        get.wait()
        for a, b in todo:
            puts.append(pltpu.make_async_copy(a, b, osem.at[len(puts)]))
            puts[-1].start()
    for put in puts + last:
        put.wait()


def finish(mixed, pgrad, ff, pq, small, hidden):
    rows, width = mixed.shape
    mine = ff.shape[1]
    heads = pq.shape[2]
    shape = lambda *s: jax.ShapeDtypeStruct(s, F32)
    outs = [
        jax.ShapeDtypeStruct((rows, width), BF16), shape(rows, width), shape(3, mine, heads),
        shape(mine, heads), shape(mine, hidden), shape(mine, hidden), shape(width), shape(width),
        shape(3, heads), shape(heads // HALF, 2, HALF // 2), shape(width), shape(width),
        shape(width), shape(hidden), shape(width),
    ]
    any_spec = pl.BlockSpec(memory_space=ANY)
    reads = 1 + 2 * (rows // R) + ff.shape[0] + pq.shape[0]
    writes = 2 * (rows // R) + 2 * ff.shape[0] + 3 * pq.shape[0] - 2
    big = (mixed, pgrad, ff, pq, small)
    return pl.pallas_call(
        finish_kernel,
        name="finish",
        out_shape=outs,
        in_specs=[any_spec] * 5,
        out_specs=[any_spec] * len(outs),
        scratch_shapes=[pltpu.VMEM(v.shape, v.dtype) for v in (*big, *outs[6:])]
        + [pltpu.SemaphoreType.DMA((n,)) for n in (reads, writes, 9)],
        compiler_params=pltpu.CompilerParams(vmem_limit_bytes=67043328),
    )(*big)


def body(
    fuse, parts,
    patches, image_grids, out_grad, first_gain, first_shift, qkv_weight, qkv_bias, rope_freqs,
    proj_weight, proj_bias, second_gain, second_shift, expand_weight, expand_bias,
    contract_weight, contract_bias,
):
    width = patches.shape[1]
    mixed, pgrad, ff, pq, small, _, _ = main_call(
        fuse,
        parts,
        (patches, out_grad, proj_weight, expand_weight, contract_weight, qkv_weight),
        image_grids.T,
        rope_freqs.transpose(1, 0, 2),
        qkv_bias,
        (first_gain, first_shift, proj_bias, second_gain, second_shift, expand_bias, contract_bias),
    )
    if not fuse:
        scatter = partial(lax.psum_scatter, axis_name="dp", scatter_dimension=1, tiled=True)
        ff = scatter(ff.reshape(ff.shape[0], width, ff.shape[-1]))
        pq = scatter(pq.reshape(pq.shape[0], width, pq.shape[-1]))
        small = lax.psum(small, "dp")
    (
        mixed, pgrad, qkv, proj, expand, contract, gain_one, shift_one, bias_q, rope,
        bias_p, gain_two, shift_two, bias_e, bias_c,
    ) = finish(mixed, pgrad, ff, pq, small, expand_bias.shape[0])
    return (
        mixed, pgrad, qkv, proj.T, expand, contract.T, gain_one, shift_one, bias_q,
        rope.transpose(1, 0, 2), bias_p, gain_two, shift_two, bias_e, bias_c,
    )


def solution(mesh):
    in_specs = (
        P("dp", None), P("dp", None), P("dp", None), P(), P(), P(None, None, "head"),
        P(None, "head"), P(None, "head", None), P("head", None), P(), P(), P(),
        P(None, "head"), P("head"), P("head", None), P(),
    )
    out_specs = (
        P("dp", None), P("dp", None), P(None, "dp", "head"), P("head", "dp"), P("dp", "head"),
        P("head", "dp"), P(), P(), P(None, "head"), P(None, "head", None), P(), P(), P(),
        P("head"), P(),
    )
    parts = mesh.shape["dp"]
    run = partial(body, parts == PARTS, parts)
    return jax.shard_map(run, mesh=mesh, in_specs=in_specs, out_specs=out_specs, check_vma=False)
```
